32 devices in a mesh: lon: 32 (over z, y, x, core).
Axes of the slice: x: 2, y: 2, z: 4, core: 2. Of those that a mesh axis runs over, the one named last changes fastest.
Arguments:
- field: float32 [16, 1664, 200], P(None, 'lon'), may hold values from -6 to 6
- south_rows: float32 [8, 1664, 200], P(None, 'lon'), may hold values from -6 to 6
- sign_mask: int32 [200], replicated, may hold values from -1 to 1, as said below
- weights: float32 [4, 9, 200, 200], replicated, may hold values from -0.125 to 0.125
- biases: float32 [4, 200], replicated, may hold values from -3 to 3
Outputs:
- result: float32 [16, 1664, 200], P(None, 'lon')
The draws below stay inside these ranges and needn't reach their ends.
Inputs may be any that keep to these rules, and one draw needn't show every extreme that they name: `sign_mask`: every entry is +1 or -1.
All inputs are finite; a program needn't handle non-finite values.
Results may differ from the reference program's by a relative error of at most 0.0001.
Values sent between devices are 32-bit elements; how exact they have to be, the bound alone decides.
No kernel may reach another device: no remote copies, remote signals or barrier semaphores. Data moves between devices by JAX's collectives and lax.ppermute only.
A program may use at most 64 MiB of HBM per device.

```python
import jax
import jax.numpy as jnp
from jax import lax

C = 200
R = 16
LAYERS = 4
NLON = 1664
SOUTH = 8


def draw_sign_mask(key, part):
    return (2 * jax.random.randint(key, (C,), 0, 2) - 1).astype(jnp.int32)


def block_levels(stream_key, extent, cuts, smallest, top_value):
    def one(dim, blocks):
        draws = jax.random.uniform(jax.random.fold_in(jax.random.fold_in(stream_key, 6), dim), (blocks,), jnp.float32, smallest / len(cuts), top_value / len(cuts))
        return jnp.repeat(jnp.exp(draws), extent[dim] // blocks).reshape((-1,) + (1,) * (len(extent) - dim - 1))

    loudness = one(*cuts[0])
    for cut in cuts[1:]:
        loudness = loudness * one(*cut)
    return loudness


def centred(stream_key, shape, deviation, reach, pieces=(), kind=jnp.bfloat16):
    factor_of = block_levels(stream_key, shape, pieces, -0.22, 0.18) if pieces else 1.0
    result = jax.random.normal(stream_key, shape, jnp.float32) * deviation * factor_of
    return jnp.minimum(jnp.maximum(result, -reach), reach).astype(kind)


def setup_inputs(seed: int = 0) -> dict:
    arg_keys = jax.random.split(jax.random.key(seed), 6)
    return {
        "field": centred(arg_keys[0], (R, NLON, C), 1.0, 6.0, ((1, 32),), jnp.float32),
        "south_rows": centred(arg_keys[1], (SOUTH, NLON, C), 1.0, 6.0, ((1, 32),), jnp.float32),
        "sign_mask": draw_sign_mask(jax.random.fold_in(arg_keys[5], 71), 0),
        "weights": centred(arg_keys[3], (LAYERS, 9, C, C), (9 * C) ** -0.5, 0.125, (), jnp.float32),
        "biases": centred(arg_keys[4], (LAYERS, C), 0.5, 3.0, (), jnp.float32),
    }


def convolve(padded, kernel, offset, dilate, row_count, col_count):
    summed = jnp.zeros((row_count, col_count, kernel.shape[-1]), jnp.float32)
    for tap_row in range(3):
        for tap_col in range(3):
            window = padded[tap_row * dilate:tap_row * dilate + row_count, tap_col * dilate:tap_col * dilate + col_count]
            summed = summed + jnp.einsum("rlc,cd->rld", window, kernel[3 * tap_row + tap_col], precision=lax.Precision.HIGHEST)
    return summed + offset


def reference(field, south_rows, sign_mask, weights, biases):
    row_count, col_count = field.shape[0], field.shape[1]
    channel_signs = sign_mask.astype(jnp.float32)
    for layer_index in range(weights.shape[0]):
        dilate = 2 ** layer_index
        south_part = south_rows[south_rows.shape[0] - dilate:]
        north_rows = (field[row_count - dilate:][::-1] * channel_signs)[:, ::-1]
        stacked = jnp.concatenate([south_part, field, north_rows], 0)
        padded = jnp.concatenate([stacked[:, col_count - dilate:], stacked, stacked[:, :dilate]], 1)
        field = field + jax.nn.gelu(convolve(padded, weights[layer_index], biases[layer_index], dilate, row_count, col_count))
    return field
```

```python
import functools

import jax
import jax.numpy as jnp
from jax import lax
from jax.experimental import pallas as pl
from jax.experimental.pallas import tpu as pltpu
from jax.sharding import PartitionSpec as P

F32 = jnp.float32
BF16 = jnp.bfloat16
LANES = 128
HALF = 64
MW = 64
HALO = 8


def slot_count(rows):
    halves = (rows + 1) // 2
    merged = rows % 2 == 1 and rows <= 8
    return rows + halves + (0 if merged else -(-rows // 16))


def lane_of(width):
    return lax.broadcasted_iota(jnp.int32, (width, LANES), 1)


def roll(x, shift):
    shift = shift % LANES
    return x if shift == 0 else pltpu.roll(x, shift, 1)


def pack(get, put, rows, width, rem):
    lane = lane_of(width)
    halves = (rows + 1) // 2
    merged = rows % 2 == 1 and rows <= 8
    for k in range(rows):
        put(k, get(k, 0))
    second = [get(k, 1) for k in range(rows)]
    for p in range(halves):
        other = roll(second[2 * p + 1], HALF) if 2 * p + 1 < rows else jnp.zeros((width, LANES), F32)
        tile = jnp.where(lane < HALF, second[2 * p], other)
        if merged and p == halves - 1:
            for k in range(rows):
                at = HALF + rem * k
                tile = jnp.where((lane >= at) & (lane < at + rem), roll(second[k], rem * k), tile)
        put(rows + p, tile)
    if not merged:
        for c in range(-(-rows // 16)):
            tile = jnp.zeros((width, LANES), F32)
            for k in range(16 * c, min(rows, 16 * c + 16)):
                at = rem * (k % 16)
                tile = jnp.where((lane >= at) & (lane < at + rem), roll(second[k], at - HALF), tile)
            put(rows + halves + c, tile)


def unpack(slot, k, rows, width, rem):
    lane = lane_of(width)
    halves = (rows + 1) // 2
    merged = rows % 2 == 1 and rows <= 8
    half = roll(slot(rows + k // 2), HALF * (k % 2))
    if merged:
        rest = roll(slot(rows + halves - 1), -rem * k)
    else:
        rest = roll(slot(rows + halves + k // 16), HALF - rem * (k % 16))
    tile = jnp.where(lane < HALF, half, jnp.where(lane < HALF + rem, rest, 0.0))
    return slot(k), tile


def slots_of(ref, width):
    return lambda k: ref[k * width : (k + 1) * width, :]


def putter(ref, width):
    def put(k, tile):
        ref[k * width : (k + 1) * width, :] = tile

    return put


def fill(hi, lo, dst, ref, src, count, offs):
    def body(i, carry):
        for b in range(3):
            for t in range(2):
                x = ref[src + i, t, offs[b] : offs[b] + MW, :]
                h = x.astype(BF16)
                at = b * 2 * LANES + t * LANES
                hi[dst + i, :, at : at + LANES] = h
                lo[dst + i, :, at : at + LANES] = (x - h.astype(F32)).astype(BF16)
        return carry

    lax.fori_loop(0, count, body, 0)


def products(hi, lo, wh, wl, taps, row, chunk, dilate, turn=False):
    total = None
    for a in taps:
        at = pl.ds(row + a * dilate, chunk)
        lh = hi[at].reshape(chunk * MW, hi.shape[-1])
        ll = lo[at].reshape(chunk * MW, hi.shape[-1])
        for left, right in ((lh, wh), (ll, wh), (lh, wl)):
            term = jnp.dot(left, right[2 - a if turn else a], preferred_element_type=F32)
            total = term if total is None else total + term
    return total


def conv(hi, lo, wh, wl, bias, dilate, base, count, chunk, emit, turn=False):
    def body(i, carry):
        row = i * chunk
        total = products(hi, lo, wh, wl, (0, 1, 2), base + row, chunk, dilate, turn)
        emit(row, jax.nn.gelu(total + bias[...]))
        return carry

    if count == chunk:
        body(0, 0)
    else:
        lax.fori_loop(0, count // chunk, body, 0)


def add_rows(out, out_row, res, res_row, off, chunk):
    def emit(row, grown):
        for q in range(chunk):
            for t in range(2):
                out[out_row + row + q, t, 0:MW, :] = (
                    res[res_row + row + q, t, off : off + MW, :]
                    + grown[q * MW : (q + 1) * MW, t * LANES : (t + 1) * LANES]
                )

    return emit


def put_row(dst, row, at, tiles):
    for t in range(2):
        dst[row, t, at : at + tiles[t].shape[0], :] = tiles[t]


def tile_of(ref, row, lo, hi, channels):
    part = ref[row, lo:hi, LANES:channels]
    return jnp.concatenate([part, jnp.zeros((hi - lo, 2 * LANES - channels), F32)], axis=1)


def k_first(par, field, south, main, ewi, ewc, *, top):
    rows, cols, channels = field.shape
    rem = channels - LANES - HALF

    def get(k, t):
        row = rows - 1 - k
        return field[row, :, 0:LANES] if t == 0 else tile_of(field, row, 0, cols, channels)

    pack(get, putter(main, cols), top, cols, rem)
    even = par[0] == 0

    def edge(flip):
        def get(k, t):
            ref, row = (field, k) if k < rows else (south, k - rows)
            if t == 0:
                west, east = ref[row, 0:HALO, 0:LANES], ref[row, cols - HALO : cols, 0:LANES]
            else:
                west = tile_of(ref, row, 0, HALO, channels)
                east = tile_of(ref, row, cols - HALO, cols, channels)
            return jnp.where(even != flip, east, west)

        return get

    count = rows + south.shape[0]
    pack(edge(False), putter(ewi, HALO), count, HALO, rem)
    pack(edge(True), putter(ewc, HALO), count, HALO, rem)


def k_weights(w, wh, wl):
    channels = w.shape[-1]
    wh[...] = jnp.zeros(wh.shape, BF16)
    wl[...] = jnp.zeros(wl.shape, BF16)
    for a in range(3):
        for b in range(3):
            x = w[0, 3 * a + b]
            h = x.astype(BF16)
            at = b * 2 * LANES
            wh[0, a, at : at + channels, 0:channels] = h
            wl[0, a, at : at + channels, 0:channels] = (x - h.astype(F32)).astype(BF16)


def sided(par, ewi, ewc):
    even = par[0] == 0
    west = lambda k: jnp.where(even, slots_of(ewc, HALO)(k), slots_of(ewi, HALO)(k))
    east = lambda k: jnp.where(even, slots_of(ewi, HALO)(k), slots_of(ewc, HALO)(k))
    return west, east


def k_corner(par, ewi, ewc, out, *, count, total, last, rem):
    west, east = sided(par, ewi, ewc)
    tiles = []
    for k in range(count):
        w = unpack(west, last - k, total, HALO, rem)
        e = unpack(east, last - k, total, HALO, rem)
        tiles.append([jnp.concatenate([w[t], e[t]], axis=0) for t in range(2)])
    pack(lambda k, t: tiles[k][t], putter(out, 2 * HALO), count, 2 * HALO, rem)


def k_a(par, field, south, ewi, ewc, wh, wl, bias, st1, se, edge0, x0, hi, lo):
    rows, cols, channels = field.shape
    rem = channels - LANES - HALF
    total = rows + south.shape[0]
    west, east = sided(par, ewi, ewc)
    for k in range(total):
        ref, row, dst = (field, k, x0) if k < rows else (south, k - rows, se)
        put_row(dst, row, 0, unpack(west, k, total, HALO, rem))
        put_row(dst, row, HALO, (ref[row, :, 0:LANES], tile_of(ref, row, 0, cols, channels)))
        put_row(dst, row, HALO + cols, unpack(east, k, total, HALO, rem))
    edge0[...] = x0[rows - 2 :]
    offs = (1, 2, 3)
    fill(hi, lo, 0, se, south.shape[0] - 1, 1, offs)
    fill(hi, lo, 1, x0, 0, rows, offs)
    count = rows - 1
    conv(hi, lo, wh.at[0], wl.at[0], bias, 1, 0, count, 5, add_rows(st1, 0, x0, 0, 2, 5))


def signed(tiles, sign):
    return tiles if sign is None else [tiles[t] * sign[t] for t in range(2)]


def north_rows(dst, dst_row, main, sign, count, cols, width, left, rem):
    n = slot_count(count)
    for k in range(count):
        t = unpack(lambda q: main[(n - 1 - q) * width : (n - q) * width, :], k, count, width, rem)
        put_row(dst, dst_row + k, left, signed(t, sign))


def north_corners(dst, dst_row, corner, sign, ks, total, cols, left, rem):
    n = slot_count(total)
    width = 2 * HALO
    for i, k in enumerate(ks):
        t = unpack(lambda q: corner[(n - 1 - q) * width : (n - q) * width, :], k, total, width, rem)
        t = signed(t, sign)
        put_row(dst, dst_row + i, left - HALO, [x[0:HALO] for x in t])
        put_row(dst, dst_row + i, left + cols, [x[HALO:] for x in t])


def k_b(edge0, main, corner, st1, sign, wh, wl, bias, st2, out, x0, xr, x1, hi, lo, *, cols, rem):
    rows = st1.shape[0] + 1
    north_rows(xr, 1, main, None, 3, cols, cols, HALO, rem)
    north_corners(xr, 1, corner, None, range(3), 3, cols, HALO, rem)
    x0[0:2] = edge0[...]
    for t in range(2):
        x0[2, t] = xr[1, t] * sign[t]
        xr[0, t] = edge0[1, t] * sign[t]
    x1[0:5] = st1[rows - 6 : rows - 1]
    offs = (1, 2, 3)
    fill(hi, lo, 0, x0, 0, 3, offs)
    conv(hi, lo, wh.at[0], wl.at[0], bias.at[0], 1, 0, 1, 1, add_rows(x1, 5, x0, 1, 2, 1))
    fill(hi, lo, 3, xr, 0, 4, offs[::-1])

    def emit(row, grown):
        for q in range(2):
            for t in range(2):
                x1[6 + q, t, 0:MW, :] = sign[t] * (
                    xr[1 + q, t, 2 : 2 + MW, :] + grown[q * MW : (q + 1) * MW, t * LANES : (t + 1) * LANES]
                )

    conv(hi, lo, wh.at[0], wl.at[0], bias.at[0], 1, 3, 2, 2, emit, turn=True)
    fill(hi, lo, 0, x1, 0, 8, (0, 2, 4))
    conv(hi, lo, wh.at[1], wl.at[1], bias.at[1], 2, 0, 4, 4, add_rows(st2, 0, x1, 2, 2, 4))
    wide = cols + 8
    pack(lambda k, t: st2[3 - k, t, 0:wide, :], putter(out, wide), 4, wide, rem)


def k_c(st1, st2b, se, wh, wl, bias, st2, st3, out, hi, lo, *, cols, rem):
    south = se.shape[0]
    rows = st2.shape[0]
    low = rows - 4
    fill(hi, lo, 0, se, south - 2, 2, (2, 4, 6))
    fill(hi, lo, 2, st1, 0, low + 2, (0, 2, 4))
    conv(hi, lo, wh.at[0], wl.at[0], bias.at[0], 2, 0, low, 4, add_rows(st2, 0, st1, 0, 2, 4))
    st2[low:rows] = st2b[...]
    fill(hi, lo, 0, se, south - 4, 4, (4, 8, 12))
    fill(hi, lo, 4, st2, 0, rows, (0, 4, 8))
    conv(hi, lo, wh.at[1], wl.at[1], bias.at[1], 4, 0, low, 4, add_rows(st3, 0, st2, 0, 4, 4))
    pack(lambda k, t: st3[low - 1 - k, t, 0:cols, :], putter(out, cols), 4, cols, rem)


def k_d(par, st2, north, st3a, sign, wh, wl, bias, st3b, out, ewi, ewc, x2, hi, lo, *, cols, rem):
    rows = st2.shape[0]
    wide = cols + 8
    north_rows(x2, 0, north, sign, 4, cols, wide, 0, rem)
    fill(hi, lo, 0, st2, rows - 8, 8, (0, 4, 8))
    fill(hi, lo, 8, x2, 0, 4, (0, 4, 8))
    conv(hi, lo, wh, wl, bias, 4, 0, 4, 4, add_rows(st3b, 0, st2, rows - 4, 4, 4))
    pack(lambda k, t: st3b[3 - k, t, 0:cols, :], putter(out, cols), 4, cols, rem)
    even = par[0] == 0

    def edge(flip):
        def get(k, t):
            ref, row = (st3a, k) if k < rows - 4 else (st3b, k - rows + 4)
            west, east = ref[row, t, 0:HALO, :], ref[row, t, cols - HALO : cols, :]
            return jnp.where(even != flip, east, west)

        return get

    pack(edge(False), putter(ewi, HALO), rows, HALO, rem)
    pack(edge(True), putter(ewc, HALO), rows, HALO, rem)


def k_f(par, st3a, st3b, ewi, ewc, se, wh, wl, bias, outlo, acc, x3, hi, lo, *, cols, channels):
    rem = channels - LANES - HALF
    rows = x3.shape[0]
    south = se.shape[0]
    west, east = sided(par, ewi, ewc)
    for k in range(rows):
        ref, row = (st3a, k) if k < rows - 4 else (st3b, k - rows + 4)
        put_row(x3, k, 0, unpack(west, k, rows, HALO, rem))
        put_row(x3, k, HALO, [ref[row, t, 0:cols, :] for t in range(2)])
        put_row(x3, k, HALO + cols, unpack(east, k, rows, HALO, rem))
    offs = (0, 8, 16)
    fill(hi, lo, 0, se, 0, south, offs)
    fill(hi, lo, south, x3, 0, rows, offs)

    def emit(row, grown):
        for q in range(4):
            g = grown[q * MW : q * MW + cols]
            outlo[row + q, :, 0:LANES] = x3[row + q, 0, HALO : HALO + cols, :] + g[:, 0:LANES]
            outlo[row + q, :, LANES:channels] = (x3[row + q, 1, HALO : HALO + cols, :] + g[:, LANES:])[
                :, 0 : channels - LANES
            ]

    conv(hi, lo, wh, wl, bias, 8, 0, rows - 8, 4, emit)

    def body(i, carry):
        total = products(hi, lo, wh, wl, (0, 1), rows - 8 + 4 * i, 4, 8)
        acc[pl.ds(4 * i, 4)] = (total + bias[...]).reshape(4, MW, 2 * LANES)
        return carry

    lax.fori_loop(0, 2, body, 0)


def k_g(outlo, acc, st3a, st3b, na, nb, nc, sign, wh, wl, out, xn, hi, lo, *, rem):
    rows, cols, channels = out.shape
    north_rows(xn, 0, nb, sign, 4, cols, cols, HALO, rem)
    north_rows(xn, 4, na, sign, 4, cols, cols, HALO, rem)
    north_corners(xn, 0, nc, sign, range(8), 8, cols, HALO, rem)
    fill(hi, lo, 0, xn, 0, 8, (0, 8, 16))
    for r in range(rows - 8):
        out[r] = outlo[r]
    for i in range(2):
        total = None
        at = pl.ds(4 * i, 4)
        lh = hi[at].reshape(4 * MW, hi.shape[-1])
        ll = lo[at].reshape(4 * MW, hi.shape[-1])
        total = acc[at].reshape(4 * MW, 2 * LANES)
        for left, right in ((lh, wh), (ll, wh), (lh, wl)):
            total = total + jnp.dot(left, right[2], preferred_element_type=F32)
        grown = jax.nn.gelu(total)
        for q in range(4):
            r = rows - 8 + 4 * i + q
            ref, row = (st3a, r) if r < rows - 4 else (st3b, r - rows + 4)
            g = grown[q * MW : q * MW + cols]
            out[r, :, 0:LANES] = ref[row, 0, 0:cols, :] + g[:, 0:LANES]
            out[r, :, LANES:channels] = (ref[row, 1, 0:cols, :] + g[:, LANES:])[:, 0 : channels - LANES]


VM = pl.BlockSpec(memory_space=pltpu.VMEM)
SM = pl.BlockSpec(memory_space=pltpu.SMEM)


def lhs(rows):
    return [pltpu.VMEM((rows, MW, 6 * LANES), BF16)] * 2


def call(kernel, outs, scratch, args, smem=0, flops=0, limit=30, name=None, layers=None):
    specs = [SM] * smem + [VM] * (len(args) - smem)
    for at, (first, count) in (layers or {}).items():
        shape = (count,) + args[at].shape[1:]
        assert first % count == 0
        if count == 1:
            shape = (None,) + args[at].shape[1:]
        specs[at] = pl.BlockSpec(
            shape,
            functools.partial(lambda f, nd, i: (f,) + (0,) * (nd - 1), first // count, args[at].ndim),
            pipeline_mode=pl.Buffered(1),
        )
    moved = sum(a.size * a.dtype.itemsize for a in args[smem:])
    return pl.pallas_call(
        kernel,
        grid=(1,),
        out_shape=[jax.ShapeDtypeStruct(s, F32) for s in outs],
        in_specs=specs,
        out_specs=[VM] * len(outs),
        scratch_shapes=scratch,
        compiler_params=pltpu.CompilerParams(vmem_limit_bytes=limit * 2**20),
        cost_estimate=pl.CostEstimate(flops=flops, bytes_accessed=moved, transcendentals=0),
        name=name,
    )(*args)


def local(field, south_rows, sign_mask, weights, biases):
    rows, cols, channels = field.shape
    south = south_rows.shape[0]
    layers = weights.shape[0]
    rem = channels - LANES - HALF
    devices = lax.axis_size("lon")
    mirror = [(i, devices - 1 - i) for i in range(devices)]
    intra = [(i, i ^ 1) for i in range(devices)]
    cross = [(i, (i + 1) % devices if i % 2 else (i - 1) % devices) for i in range(devices)]
    send = lambda x, route: lax.ppermute(x, "lon", route)
    par = (lax.axis_index("lon") % 2).astype(jnp.int32).reshape(1)
    pad = 2 * LANES - channels
    sign = jnp.pad(sign_mask.astype(F32), (0, pad)).reshape(2, 1, LANES)
    bias = jnp.pad(biases, ((0, 0), (0, pad))).reshape(layers, 1, 2 * LANES)
    row_flops = MW * 6 * LANES * 2 * LANES * 2 * 9

    total = rows + south
    ew_rows = slot_count(total) * HALO
    main, ewi, ewc = call(
        functools.partial(k_first, top=3),
        [(slot_count(3) * cols, LANES), (ew_rows, LANES), (ew_rows, LANES)],
        [], [par, field, south_rows], smem=1, name="first",
    )
    ewi, ewc, main = send(ewi, intra), send(ewc, cross), send(main, mirror)

    wshape = jax.ShapeDtypeStruct((layers, 3, 6 * LANES, 2 * LANES), BF16)
    wspec = pl.BlockSpec((1, 3, 6 * LANES, 2 * LANES), lambda i: (i, 0, 0, 0))
    wh, wl = pl.pallas_call(
        k_weights,
        grid=(layers,),
        out_shape=[wshape, wshape],
        in_specs=[pl.BlockSpec((1,) + weights.shape[1:], lambda i: (i, 0, 0, 0))],
        out_specs=[wspec, wspec],
        compiler_params=pltpu.CompilerParams(vmem_limit_bytes=30 * 2**20),
        cost_estimate=pl.CostEstimate(flops=0, bytes_accessed=16 * 2**20, transcendentals=0),
        name="weights",
    )(weights)

    (corner,) = call(
        functools.partial(k_corner, count=3, total=total, last=rows - 1, rem=rem),
        [(slot_count(3) * 2 * HALO, LANES)], [], [par, ewi, ewc], smem=1, name="corner",
    )
    corner = send(corner, mirror)

    def state(n, width):
        return (n, 2, width, LANES)

    st1, se, edge0 = call(
        k_a,
        [state(rows - 1, 72), state(south, 80), state(2, 72)],
        [pltpu.VMEM(state(rows, 72), F32)] + lhs(rows + 1),
        [par, field, south_rows, ewi, ewc, wh[0:1], wl[0:1], bias[0]],
        smem=1, flops=(rows - 1) * row_flops, name="a",
    )
    st2b, north = call(
        functools.partial(k_b, cols=cols, rem=rem),
        [state(4, 72), (slot_count(4) * (cols + 8), LANES)],
        [pltpu.VMEM(state(3, 72), F32), pltpu.VMEM(state(4, 72), F32), pltpu.VMEM(state(8, 72), F32)] + lhs(8),
        [edge0, main[::-1], corner[::-1], st1, sign, wh[0:2], wl[0:2], bias[0:2]],
        flops=7 * row_flops, name="b",
    )
    north = send(north, mirror)
    st2, st3a, na = call(
        functools.partial(k_c, cols=cols, rem=rem),
        [state(rows, 72), state(rows - 4, MW), (slot_count(4) * cols, LANES)],
        lhs(rows + 4),
        [st1, st2b, se, wh[1:3], wl[1:3], bias[1:3]],
        flops=(2 * rows - 8) * row_flops, name="c",
    )
    na = send(na, mirror)
    ew_rows = slot_count(rows) * HALO
    st3b, nb, ewi, ewc = call(
        functools.partial(k_d, cols=cols, rem=rem),
        [state(4, MW), (slot_count(4) * cols, LANES), (ew_rows, LANES), (ew_rows, LANES)],
        [pltpu.VMEM(state(4, 72), F32)] + lhs(12),
        [par, st2, north[::-1], st3a, sign, wh[2], wl[2], bias[2]],
        smem=1, flops=4 * row_flops, name="d",
    )
    nb = send(nb, mirror)
    ewi, ewc = send(ewi, intra), send(ewc, cross)
    (nc,) = call(
        functools.partial(k_corner, count=8, total=rows, last=rows - 1, rem=rem),
        [(slot_count(8) * 2 * HALO, LANES)], [], [par, ewi, ewc], smem=1, name="corner2",
    )
    nc = send(nc, mirror)
    outlo, acc = call(
        functools.partial(k_f, cols=cols, channels=channels),
        [(rows - 8, cols, channels), (8, MW, 2 * LANES)],
        [pltpu.VMEM(state(rows, 80), F32)] + lhs(rows + south),
        [par, st3a, st3b, ewi, ewc, se, wh[3], wl[3], bias[3]],
        smem=1, flops=(rows - 3) * row_flops, name="f",
    )
    (out,) = call(
        functools.partial(k_g, rem=rem),
        [(rows, cols, channels)],
        [pltpu.VMEM(state(8, 80), F32)] + lhs(8),
        [outlo, acc, st3a, st3b, na[::-1], nb[::-1], nc[::-1], sign, wh[3], wl[3]],
        flops=3 * row_flops, name="g",
    )
    return out


def solution(mesh):
    in_specs = (P(None, "lon", None), P(None, "lon", None), P(), P(), P())
    out_specs = P(None, "lon", None)
    return jax.shard_map(local, mesh=mesh, in_specs=in_specs, out_specs=out_specs, check_vma=False)
```

```python
import functools

import jax
import jax.numpy as jnp
from jax import lax
from jax.experimental import pallas as pl
from jax.experimental.pallas import tpu as pltpu
from jax.sharding import PartitionSpec as P

F32 = jnp.float32
BF16 = jnp.bfloat16
LANES = 128
HALF = 64
MW = 64
HALO = 8


def slot_count(rows):
    halves = (rows + 1) // 2
    merged = rows % 2 == 1 and rows <= 8
    return rows + halves + (0 if merged else -(-rows // 16))


def lane_of(width):
    return lax.broadcasted_iota(jnp.int32, (width, LANES), 1)


def roll(x, shift):
    shift = shift % LANES
    return x if shift == 0 else pltpu.roll(x, shift, 1)


def pack(get, put, rows, width, rem):
    lane = lane_of(width)
    halves = (rows + 1) // 2
    merged = rows % 2 == 1 and rows <= 8
    for k in range(rows):
        put(k, get(k, 0))
    second = [get(k, 1) for k in range(rows)]
    for p in range(halves):
        other = roll(second[2 * p + 1], HALF) if 2 * p + 1 < rows else jnp.zeros((width, LANES), F32)
        tile = jnp.where(lane < HALF, second[2 * p], other)
        if merged and p == halves - 1:
            for k in range(rows):
                at = HALF + rem * k
                tile = jnp.where((lane >= at) & (lane < at + rem), roll(second[k], rem * k), tile)
        put(rows + p, tile)
    if not merged:
        for c in range(-(-rows // 16)):
            tile = jnp.zeros((width, LANES), F32)
            for k in range(16 * c, min(rows, 16 * c + 16)):
                at = rem * (k % 16)
                tile = jnp.where((lane >= at) & (lane < at + rem), roll(second[k], at - HALF), tile)
            put(rows + halves + c, tile)


def unpack(slot, k, rows, width, rem):
    lane = lane_of(width)
    halves = (rows + 1) // 2
    merged = rows % 2 == 1 and rows <= 8
    half = roll(slot(rows + k // 2), HALF * (k % 2))
    if merged:
        rest = roll(slot(rows + halves - 1), -rem * k)
    else:
        rest = roll(slot(rows + halves + k // 16), HALF - rem * (k % 16))
    tile = jnp.where(lane < HALF, half, jnp.where(lane < HALF + rem, rest, 0.0))
    return slot(k), tile


def slots_of(ref, width):
    return lambda k: ref[k * width : (k + 1) * width, :]


def putter(ref, width):
    def put(k, tile):
        ref[k * width : (k + 1) * width, :] = tile

    return put


def turned(ref, width, count):
    order = 7 - lax.broadcasted_iota(jnp.int32, (8, LANES), 0)
    flip = lambda x: jnp.take_along_axis(x, order, axis=0)

    def one(k):
        parts, left = [], width
        while left >= 8:
            parts.append(flip(ref[k * width + left - 8 : k * width + left, :]))
            left -= 8
        if left:
            parts.append(flip(ref[k * width : k * width + 8, :])[8 - left :])
        return jnp.concatenate(parts, axis=0)

    tiles = [one(k) for k in range(count)]
    return lambda k: tiles[k]


def fill(hi, lo, dst, ref, src, count, offs):
    def body(i, carry):
        for b in range(3):
            for t in range(2):
                x = ref[src + i, t, offs[b] : offs[b] + MW, :]
                h = x.astype(BF16)
                at = b * 2 * LANES + t * LANES
                hi[dst + i, :, at : at + LANES] = h
                lo[dst + i, :, at : at + LANES] = (x - h.astype(F32)).astype(BF16)
        return carry

    lax.fori_loop(0, count, body, 0)


def products(hi, lo, wh, wl, taps, row, chunk, dilate):
    total = None
    for a in taps:
        at = pl.ds(row + a * dilate, chunk)
        lh = hi[at].reshape(chunk * MW, hi.shape[-1])
        ll = lo[at].reshape(chunk * MW, hi.shape[-1])
        for left, right in ((lh, wh), (ll, wh), (lh, wl)):
            term = jnp.dot(left, right[a], preferred_element_type=F32)
            total = term if total is None else total + term
    return total


def conv(hi, lo, wh, wl, bias, dilate, base, count, chunk, emit):
    def body(i, carry):
        row = i * chunk
        total = products(hi, lo, wh, wl, (0, 1, 2), base + row, chunk, dilate)
        emit(row, jax.nn.gelu(total + bias))
        return carry

    if count == chunk:
        body(0, 0)
    else:
        lax.fori_loop(0, count // chunk, body, 0)


def add_rows(out, out_row, res, res_row, off, chunk):
    def emit(row, grown):
        for q in range(chunk):
            for t in range(2):
                out[out_row + row + q, t, 0:MW, :] = (
                    res[res_row + row + q, t, off : off + MW, :]
                    + grown[q * MW : (q + 1) * MW, t * LANES : (t + 1) * LANES]
                )

    return emit


def put_row(dst, row, at, tiles):
    for t in range(2):
        dst[row, t, at : at + tiles[t].shape[0], :] = tiles[t]


def widen(x):
    return jnp.concatenate([x, jnp.zeros(x.shape[:-1] + (LANES - x.shape[-1],), F32)], axis=-1)


def tile_at(ref, col, lo, hi, t):
    return ref[col, lo:hi, 0:LANES] if t == 0 else widen(ref[col, lo:hi, LANES : ref.shape[-1]])


def strided(dst, first, t, col):
    rows, _, width, _ = dst.shape
    return dst.reshape(rows * 2 * width, LANES), pl.ds((2 * first + t) * width + col, 8, stride=2 * width)


def put_column(dst, first, col, t, tile):
    flat, at = strided(dst, first, t, col)
    flat[at, :] = tile


def get_column(src, first, col, t):
    flat, at = strided(src, first, t, col)
    return flat[at, :]


def lanes_of(ref, row):
    x = ref[row : row + 1, :].astype(F32)
    return [x[:, 0:LANES], widen(x[:, LANES:])]


def bias_of(ref, row):
    return jnp.concatenate(lanes_of(ref, row), axis=1)


def k_first(par, field, south, main, ewi, ewc, top):
    cols, rows, channels = field.shape
    rem = channels - LANES - HALF
    even = par[0] == 0

    def edge(flip):
        def get(k, t):
            pick = []
            for col in (k, cols - HALO + k):
                tiles = [tile_at(field, col, 0, rows, t), tile_at(south, col, 0, south.shape[1], t)]
                pick.append(jnp.concatenate(tiles, axis=0))
            return jnp.where(even != flip, pick[1], pick[0])

        return get

    tall = rows + south.shape[1]
    pack(edge(False), putter(ewi, tall), HALO, tall, rem)
    pack(edge(True), putter(ewc, tall), HALO, tall, rem)
    for col in range(cols):
        for t in range(2):
            put_column(top, 0, col, t, tile_at(field, col, rows - 8, rows, t))
    pack(lambda k, t: top[7 - k, t, 0:cols, :], putter(main, cols), 3, cols, rem)


def k_weights(w, *refs):
    layers, _, channels, _ = w.shape
    outs, (buf, sems) = refs[: 2 * layers], refs[2 * layers :]
    copies = [pltpu.make_async_copy(w.at[i], buf.at[i], sems.at[i]) for i in range(layers)]
    for copy in copies:
        copy.start()
    for i in range(layers):
        wh, wl = outs[2 * i : 2 * i + 2]
        copies[i].wait()
        for k in range(9):
            x = buf[i, k]
            h = x.astype(BF16)
            at = (k % 3) * 2 * LANES
            for ref, value in ((wh, h), (wl, (x - h.astype(F32)).astype(BF16))):
                wide = jnp.concatenate([value, jnp.zeros((channels, 2 * LANES - channels), BF16)], axis=1)
                ref[k // 3, at : at + channels, :] = wide
                ref[k // 3, at + channels : at + 2 * LANES, :] = jnp.zeros((2 * LANES - channels, 2 * LANES), BF16)


def sided(par, ewi, ewc, width, count):
    even = par[0] == 0
    i, c = slots_of(ewi, width), slots_of(ewc, width)
    west = [jnp.where(even, c(k), i(k)) for k in range(count)]
    east = [jnp.where(even, i(k), c(k)) for k in range(count)]
    return (lambda k: west[k]), (lambda k: east[k])


def k_corner(par, ewi, ewc, out, top, *, tall, rows, rem):
    west, east = sided(par, ewi, ewc, tall, slot_count(HALO))
    for side, slot in enumerate((west, east)):
        for k in range(HALO):
            tiles = unpack(slot, k, HALO, tall, rem)
            for t in range(2):
                put_column(top, 0, side * HALO + k, t, tiles[t][rows - 8 : rows])
    pack(lambda k, t: top[7 - k, t], putter(out, 2 * HALO), 3, 2 * HALO, rem)


def k_corner2(par, ewi, ewc, out, *, rows, rem):
    west, east = sided(par, ewi, ewc, HALO, slot_count(rows))
    tiles = []
    for k in range(8):
        w = unpack(west, rows - 1 - k, rows, HALO, rem)
        e = unpack(east, rows - 1 - k, rows, HALO, rem)
        tiles.append([jnp.concatenate([w[t], e[t]], axis=0) for t in range(2)])
    pack(lambda k, t: tiles[k][t], putter(out, 2 * HALO), 8, 2 * HALO, rem)


def k_a(par, field, south, ewi, ewc, wh, wl, bias, st1, se, edge0, x0, hi, lo):
    cols, rows, channels = field.shape
    rem = channels - LANES - HALF
    deep = south.shape[1]
    west, east = sided(par, ewi, ewc, rows + deep, slot_count(HALO))

    def put(col, tiles):
        for t in range(2):
            for h in range(0, rows, 8):
                put_column(x0, h, col, t, tiles[t][h : h + 8])
            put_column(se, 0, col, t, tiles[t][rows : rows + 8])

    for k in range(HALO):
        put(k, unpack(west, k, HALO, rows + deep, rem))
        put(HALO + cols + k, unpack(east, k, HALO, rows + deep, rem))
    for col in range(cols):
        for t in range(2):
            for h in range(0, rows, 8):
                put_column(x0, h, HALO + col, t, tile_at(field, col, h, h + 8, t))
            put_column(se, 0, HALO + col, t, tile_at(south, col, 0, 8, t))
    edge0[...] = x0[rows - 2 :]
    offs = (1, 2, 3)
    fill(hi, lo, 0, se, deep - 1, 1, offs)
    fill(hi, lo, 1, x0, 0, rows, offs)
    conv(hi, lo, wh, wl, bias_of(bias, 0), 1, 0, rows - 1, 5, add_rows(st1, 0, x0, 0, 2, 5))


def signed(tiles, sign):
    return tiles if sign is None else [tiles[t] * sign[t] for t in range(2)]


def north_rows(dst, dst_row, main, sign, count, width, left, rem):
    slot = turned(main, width, slot_count(count))
    for k in range(count):
        put_row(dst, dst_row + k, left, signed(unpack(slot, k, count, width, rem), sign))


def north_corners(dst, dst_row, corner, sign, count, cols, left, rem):
    width = 2 * HALO
    slot = turned(corner, width, slot_count(count))
    for k in range(count):
        t = signed(unpack(slot, k, count, width, rem), sign)
        put_row(dst, dst_row + k, left - HALO, [x[0:HALO] for x in t])
        put_row(dst, dst_row + k, left + cols, [x[HALO:] for x in t])


def k_b(edge0, main, corner, st1, sign, wh0, wl0, wh1, wl1, bias, st2, out, x0, xr, x1, hi, lo, *, cols, rem):
    rows = st1.shape[0] + 1
    sign = lanes_of(sign, 0)
    north_rows(xr, 1, main, None, 3, cols, HALO, rem)
    north_corners(xr, 1, corner, None, 3, cols, HALO, rem)
    x0[0:2] = edge0[...]
    for t in range(2):
        x0[2, t] = xr[1, t] * sign[t]
        xr[0, t] = edge0[1, t] * sign[t]
    x1[0:5] = st1[rows - 6 : rows - 1]
    offs = (1, 2, 3)
    fill(hi, lo, 0, x0, 0, 3, offs)
    fill(hi, lo, 3, xr, 0, 4, offs[::-1])
    total = None
    for a in range(3):
        both = [jnp.concatenate([x[a : a + 1], x[5 - a : 7 - a]]).reshape(3 * MW, x.shape[-1]) for x in (hi, lo)]
        for left, right in ((both[0], wh0), (both[1], wh0), (both[0], wl0)):
            term = jnp.dot(left, right[a], preferred_element_type=F32)
            total = term if total is None else total + term
    grown = jax.nn.gelu(total + bias_of(bias, 0))
    for q in range(3):
        for t in range(2):
            g = grown[q * MW : (q + 1) * MW, t * LANES : (t + 1) * LANES]
            if q == 0:
                x1[5, t, 0:MW, :] = x0[1, t, 2 : 2 + MW, :] + g
            else:
                x1[5 + q, t, 0:MW, :] = sign[t] * (xr[q, t, 2 : 2 + MW, :] + g)
    fill(hi, lo, 0, x1, 0, 8, (0, 2, 4))
    conv(hi, lo, wh1, wl1, bias_of(bias, 1), 2, 0, 4, 4, add_rows(st2, 0, x1, 2, 2, 4))
    wide = cols + 8
    pack(lambda k, t: st2[3 - k, t, 0:wide, :], putter(out, wide), 4, wide, rem)


def k_c(st1, st2b, se, wh1, wl1, wh2, wl2, bias, st2, st3, out, hi, lo, *, cols, rem):
    south = se.shape[0]
    rows = st2.shape[0]
    low = rows - 4
    fill(hi, lo, 0, se, south - 2, 2, (2, 4, 6))
    fill(hi, lo, 2, st1, 0, low + 2, (0, 2, 4))
    conv(hi, lo, wh1, wl1, bias_of(bias, 1), 2, 0, low, 4, add_rows(st2, 0, st1, 0, 2, 4))
    st2[low:rows] = st2b[...]
    fill(hi, lo, 0, se, south - 4, 4, (4, 8, 12))
    fill(hi, lo, 4, st2, 0, rows, (0, 4, 8))
    conv(hi, lo, wh2, wl2, bias_of(bias, 2), 4, 0, low, 4, add_rows(st3, 0, st2, 0, 4, 4))
    pack(lambda k, t: st3[low - 1 - k, t, 0:cols, :], putter(out, cols), 4, cols, rem)


def k_d(par, st2, north, st3a, sign, wh, wl, bias, st3b, out, ewi, ewc, x2, hi, lo, *, cols, rem):
    rows = st2.shape[0]
    wide = cols + 8
    north_rows(x2, 0, north, lanes_of(sign, 0), 4, wide, 0, rem)
    fill(hi, lo, 0, st2, rows - 8, 8, (0, 4, 8))
    fill(hi, lo, 8, x2, 0, 4, (0, 4, 8))
    conv(hi, lo, wh, wl, bias_of(bias, 2), 4, 0, 4, 4, add_rows(st3b, 0, st2, rows - 4, 4, 4))
    pack(lambda k, t: st3b[3 - k, t, 0:cols, :], putter(out, cols), 4, cols, rem)
    even = par[0] == 0

    def edge(flip):
        def get(k, t):
            ref, row = (st3a, k) if k < rows - 4 else (st3b, k - rows + 4)
            west, east = ref[row, t, 0:HALO, :], ref[row, t, cols - HALO : cols, :]
            return jnp.where(even != flip, east, west)

        return get

    pack(edge(False), putter(ewi, HALO), rows, HALO, rem)
    pack(edge(True), putter(ewc, HALO), rows, HALO, rem)


def put_out(out, first, src, cols, channels):
    for col in range(cols):
        out[col, first : first + 8, 0:LANES] = get_column(src, 0, col, 0)
        out[col, first : first + 8, LANES:channels] = get_column(src, 0, col, 1)[:, 0 : channels - LANES]


def k_f(par, st3a, st3b, ewi, ewc, se, wh, wl, bias, outlo, acc, x3, end, hi, lo, *, cols, channels):
    rem = channels - LANES - HALF
    rows = x3.shape[0]
    south = se.shape[0]
    west, east = sided(par, ewi, ewc, HALO, slot_count(rows))
    for k in range(rows):
        ref, row = (st3a, k) if k < rows - 4 else (st3b, k - rows + 4)
        put_row(x3, k, 0, unpack(west, k, rows, HALO, rem))
        put_row(x3, k, HALO, [ref[row, t, 0:cols, :] for t in range(2)])
        put_row(x3, k, HALO + cols, unpack(east, k, rows, HALO, rem))
    offs = (0, 8, 16)
    fill(hi, lo, 0, se, 0, south, offs)
    fill(hi, lo, south, x3, 0, rows, offs)
    bias = bias_of(bias, 3)
    conv(hi, lo, wh, wl, bias, 8, 0, rows - 8, 4, add_rows(end, 0, x3, 0, 8, 4))

    def body(i, carry):
        total = products(hi, lo, wh, wl, (0, 1), rows - 8 + 4 * i, 4, 8)
        acc[pl.ds(4 * i, 4)] = (total + bias).reshape(4, MW, 2 * LANES)
        return carry

    lax.fori_loop(0, 2, body, 0)
    put_out(outlo, 0, end, cols, channels)


def k_g(outlo, acc, st3a, st3b, na, nb, nc, sign, wh, wl, out, xn, end, hi, lo, *, rem):
    cols, rows, channels = out.shape
    sign = lanes_of(sign, 0)
    north_rows(xn, 0, nb, sign, 4, cols, HALO, rem)
    north_rows(xn, 4, na, sign, 4, cols, HALO, rem)
    north_corners(xn, 0, nc, sign, 8, cols, HALO, rem)
    out[:, 0 : rows - 8, :] = outlo[...]
    fill(hi, lo, 0, xn, 0, 8, (0, 8, 16))
    for i in range(2):
        at = pl.ds(4 * i, 4)
        lh = hi[at].reshape(4 * MW, hi.shape[-1])
        ll = lo[at].reshape(4 * MW, hi.shape[-1])
        total = acc[at].reshape(4 * MW, 2 * LANES)
        for left, right in ((lh, wh), (ll, wh), (lh, wl)):
            total = total + jnp.dot(left, right[2], preferred_element_type=F32)
        grown = jax.nn.gelu(total)
        for q in range(4):
            r = rows - 8 + 4 * i + q
            ref, row = (st3a, r) if r < rows - 4 else (st3b, r - rows + 4)
            for t in range(2):
                end[4 * i + q, t] = ref[row, t] + grown[q * MW : (q + 1) * MW, t * LANES : (t + 1) * LANES]
    put_out(out, rows - 8, end, cols, channels)


VM = pl.BlockSpec(memory_space=pltpu.VMEM)
SM = pl.BlockSpec(memory_space=pltpu.SMEM)


def lhs(rows):
    return [pltpu.VMEM((rows, MW, 6 * LANES), BF16)] * 2


def call(kernel, outs, scratch, args, smem=0, flops=0, limit=16, name=None):
    moved = sum(a.size * a.dtype.itemsize for a in args[smem:])
    outs = [o if isinstance(o, jax.ShapeDtypeStruct) else jax.ShapeDtypeStruct(o, F32) for o in outs]
    return pl.pallas_call(
        kernel,
        out_shape=outs,
        in_specs=[SM] * smem + [VM if name != "weights" else pl.BlockSpec(memory_space=pl.ANY)] * (len(args) - smem),
        out_specs=[VM] * len(outs),
        scratch_shapes=scratch,
        compiler_params=pltpu.CompilerParams(vmem_limit_bytes=limit * 2**20),
        cost_estimate=pl.CostEstimate(flops=flops, bytes_accessed=moved, transcendentals=0),
        name=name,
    )(*args)


def local(field, south_rows, sign_mask, weights, biases):
    rows, cols, channels = field.shape
    south = south_rows.shape[0]
    layers = weights.shape[0]
    rem = channels - LANES - HALF
    devices = lax.axis_size("lon")
    mirror = [(i, devices - 1 - i) for i in range(devices)]
    intra = [(i, i ^ 1) for i in range(devices)]
    cross = [(i, (i + 1) % devices if i % 2 else (i - 1) % devices) for i in range(devices)]
    send = lambda x, route: lax.ppermute(x, "lon", route)
    par = (lax.axis_index("lon") % 2).astype(jnp.int32).reshape(1)
    sign = sign_mask.reshape(1, channels)
    field = jnp.swapaxes(field, 0, 1)
    south_rows = jnp.swapaxes(south_rows, 0, 1)
    row_flops = MW * 6 * LANES * 2 * LANES * 2 * 9
    tall = rows + south

    def state(n, width):
        return (n, 2, width, LANES)

    ew_rows = slot_count(HALO) * tall
    main, ewi, ewc = call(
        k_first,
        [(slot_count(3) * cols, LANES), (ew_rows, LANES), (ew_rows, LANES)],
        [pltpu.VMEM(state(8, 56), F32)], [par, field, south_rows], smem=1, name="first",
    )
    ewi, ewc, main = send(ewi, intra), send(ewc, cross), send(main, mirror)
    split = call(
        k_weights,
        [jax.ShapeDtypeStruct((3, 6 * LANES, 2 * LANES), BF16)] * (2 * layers),
        [pltpu.VMEM(weights.shape, F32), pltpu.SemaphoreType.DMA((layers,))],
        [weights], name="weights", limit=24,
    )
    (corner,) = call(
        functools.partial(k_corner, tall=tall, rows=rows, rem=rem),
        [(slot_count(3) * 2 * HALO, LANES)], [pltpu.VMEM(state(8, 2 * HALO), F32)],
        [par, ewi, ewc], smem=1, name="corner",
    )
    corner = send(corner, mirror)
    st1, se, edge0 = call(
        k_a,
        [state(rows - 1, 72), state(south, 80), state(2, 72)],
        [pltpu.VMEM(state(rows, 72), F32)] + lhs(rows + 1),
        [par, field, south_rows, ewi, ewc, *split[0:2], biases],
        smem=1, flops=(rows - 1) * row_flops, name="a",
    )
    st2b, north = call(
        functools.partial(k_b, cols=cols, rem=rem),
        [state(4, 72), (slot_count(4) * (cols + 8), LANES)],
        [pltpu.VMEM(state(3, 72), F32), pltpu.VMEM(state(4, 72), F32), pltpu.VMEM(state(8, 72), F32)] + lhs(8),
        [edge0, main, corner, st1, sign, *split[0:4], biases],
        flops=7 * row_flops, name="b",
    )
    north = send(north, mirror)
    st2, st3a, na = call(
        functools.partial(k_c, cols=cols, rem=rem),
        [state(rows, 72), state(rows - 4, MW), (slot_count(4) * cols, LANES)],
        lhs(rows + 4),
        [st1, st2b, se, *split[2:6], biases],
        flops=(2 * rows - 8) * row_flops, name="c",
    )
    na = send(na, mirror)
    ew_rows = slot_count(rows) * HALO
    st3b, nb, ewi, ewc = call(
        functools.partial(k_d, cols=cols, rem=rem),
        [state(4, MW), (slot_count(4) * cols, LANES), (ew_rows, LANES), (ew_rows, LANES)],
        [pltpu.VMEM(state(4, 72), F32)] + lhs(12),
        [par, st2, north, st3a, sign, *split[4:6], biases],
        smem=1, flops=4 * row_flops, name="d",
    )
    ewi, ewc, nb = send(ewi, intra), send(ewc, cross), send(nb, mirror)
    (nc,) = call(
        functools.partial(k_corner2, rows=rows, rem=rem),
        [(slot_count(8) * 2 * HALO, LANES)], [], [par, ewi, ewc], smem=1, name="corner2",
    )
    nc = send(nc, mirror)
    outlo, acc = call(
        functools.partial(k_f, cols=cols, channels=channels),
        [(cols, rows - 8, channels), (8, MW, 2 * LANES)],
        [pltpu.VMEM(state(rows, 80), F32), pltpu.VMEM(state(8, MW), F32)] + lhs(rows + south),
        [par, st3a, st3b, ewi, ewc, se, *split[6:8], biases],
        smem=1, flops=(rows - 3) * row_flops, name="f",
    )
    (out,) = call(
        functools.partial(k_g, rem=rem),
        [(cols, rows, channels)],
        [pltpu.VMEM(state(8, 80), F32), pltpu.VMEM(state(8, MW), F32)] + lhs(8),
        [outlo, acc, st3a, st3b, na, nb, nc, sign, *split[6:8]],
        flops=3 * row_flops, name="g",
    )
    return jnp.swapaxes(out, 0, 1)


def solution(mesh):
    in_specs = (P(None, "lon", None), P(None, "lon", None), P(), P(), P())
    out_specs = P(None, "lon", None)
    return jax.shard_map(local, mesh=mesh, in_specs=in_specs, out_specs=out_specs, check_vma=False)
```

```python
import functools

import jax
import jax.numpy as jnp
from jax import lax
from jax.experimental import pallas as pl
from jax.experimental.pallas import tpu as pltpu
from jax.sharding import PartitionSpec as P

F32 = jnp.float32
BF16 = jnp.bfloat16
LANES = 128
HALF = 64
MW = 64
HALO = 8


def merged(rows):
    return rows % 2 == 1 and rows <= 8


def rest_groups(rows, width, rem):
    groups = max(1, LANES // (rows * rem))
    return groups, width if groups == 1 else (-(-width // groups) + 7) // 8 * 8


def packed_rows(rows, width, rem):
    full = rows + (rows + 1) // 2
    return full * width + (0 if merged(rows) else rest_groups(rows, width, rem)[1])


def lane_of(width):
    return lax.broadcasted_iota(jnp.int32, (width, LANES), 1)


def roll(x, shift):
    shift = shift % LANES
    return x if shift == 0 else pltpu.roll(x, shift, 1)


def pack(get, put, rows, width, rem):
    lane = lane_of(width)
    halves = (rows + 1) // 2
    for k in range(rows):
        put(k, get(k, 0))
    second = [get(k, 1) for k in range(rows)]
    for p in range(halves):
        other = roll(second[2 * p + 1], HALF) if 2 * p + 1 < rows else jnp.zeros((width, LANES), F32)
        tile = jnp.where(lane < HALF, second[2 * p], other)
        if merged(rows) and p == halves - 1:
            for k in range(rows):
                at = HALF + rem * k
                tile = jnp.where((lane >= at) & (lane < at + rem), roll(second[k], rem * k), tile)
        put(rows + p, tile)
    if not merged(rows):
        tile = jnp.zeros((width, LANES), F32)
        for k in range(rows):
            tile = jnp.where((lane >= rem * k) & (lane < rem * k + rem), roll(second[k], rem * k - HALF), tile)
        groups, high = rest_groups(rows, width, rem)
        total = None
        for g in range(groups):
            part = tile[g * high : min(width, (g + 1) * high)]
            if part.shape[0] < high:
                part = jnp.concatenate([part, jnp.zeros((high - part.shape[0], LANES), F32)], axis=0)
            part = roll(part, g * rows * rem)
            total = part if total is None else total + part
        put(rows + halves, total)


def unpack(slot, k, rows, width, rem):
    lane = lane_of(width)
    halves = (rows + 1) // 2
    half = roll(slot(rows + k // 2), HALF * (k % 2))
    if merged(rows):
        rest = roll(slot(rows + halves - 1), -rem * k)
    else:
        rest = roll(slot(rows + halves), HALF - rem * k)
    tile = jnp.where(lane < HALF, half, jnp.where(lane < HALF + rem, rest, 0.0))
    return slot(k), tile


def slots_of(ref, rows, width, rem):
    full = rows + (rows + 1) // 2
    tiles = [ref[k * width : (k + 1) * width, :] for k in range(full)]
    if not merged(rows):
        groups, high = rest_groups(rows, width, rem)
        block = ref[full * width : full * width + high, :]
        parts = [roll(block, -g * rows * rem)[: min(high, width - g * high)] for g in range(groups)]
        tiles.append(parts[0] if groups == 1 else jnp.concatenate(parts, axis=0))
    return tiles


def putter(ref, width):
    def put(k, tile):
        ref[k * width : (k + 1) * width, :] = tile

    return put


def turned(tiles):
    order = 7 - lax.broadcasted_iota(jnp.int32, (8, LANES), 0)
    flip = lambda x: jnp.take_along_axis(x, order, axis=0)

    def one(x):
        parts, left = [], x.shape[0]
        while left >= 8:
            parts.append(flip(x[left - 8 : left]))
            left -= 8
        if left:
            parts.append(flip(x[0:8])[8 - left :])
        return jnp.concatenate(parts, axis=0)

    return [one(x) for x in tiles]


def fill_row(hi, lo, dst, ref, row, offs):
    for b in range(3):
        for t in range(2):
            x = ref[row, t, offs[b] : offs[b] + MW, :]
            h = x.astype(BF16)
            at = b * 2 * LANES + t * LANES
            hi[dst, :, at : at + LANES] = h
            lo[dst, :, at : at + LANES] = (x - h.astype(F32)).astype(BF16)


def fill(hi, lo, dst, ref, src, count, offs):
    for i in range(count):
        fill_row(hi, lo, dst + i, ref, src + i, offs)


def run(ref, first, count, offs):
    return [(ref, first + i, offs) for i in range(count)]


def products(hi, lo, wh, wl, taps, row, chunk, dilate):
    total = None
    for a in taps:
        at = slice(row + a * dilate, row + a * dilate + chunk)
        lh = hi[at].reshape(chunk * MW, hi.shape[-1])
        ll = lo[at].reshape(chunk * MW, hi.shape[-1])
        for left, right in ((lh, wh), (ll, wh), (lh, wl)):
            term = jnp.dot(left, right[a], preferred_element_type=F32)
            total = term if total is None else total + term
    return total


def conv(buffers, wh, wl, bias, dilate, sources, count, chunk, emit):
    hi, lo = buffers
    filled = 0
    for row in range(0, count, chunk):
        while filled < row + chunk + 2 * dilate:
            fill_row(hi, lo, filled, *sources[filled])
            filled += 1
        total = products(hi, lo, wh, wl, (0, 1, 2), row, chunk, dilate)
        emit(row, jax.nn.gelu(total + bias))


def add_rows(out, out_row, res, res_row, off, chunk):
    def emit(row, grown):
        for q in range(chunk):
            for t in range(2):
                out[out_row + row + q, t, 0:MW, :] = (
                    res[res_row + row + q, t, off : off + MW, :]
                    + grown[q * MW : (q + 1) * MW, t * LANES : (t + 1) * LANES]
                )

    return emit


def put_row(dst, row, at, tiles):
    for t in range(2):
        dst[row, t, at : at + tiles[t].shape[0], :] = tiles[t]


def widen(x):
    return jnp.concatenate([x, jnp.zeros(x.shape[:-1] + (LANES - x.shape[-1],), F32)], axis=-1)


def tile_at(ref, col, lo, hi, t):
    return ref[col, lo:hi, 0:LANES] if t == 0 else widen(ref[col, lo:hi, LANES : ref.shape[-1]])


def strided(dst, first, t, col):
    rows, _, width, _ = dst.shape
    return dst.reshape(rows * 2 * width, LANES), pl.ds((2 * first + t) * width + col, 8, stride=2 * width)


def put_column(dst, first, col, t, tile):
    flat, at = strided(dst, first, t, col)
    flat[at, :] = tile


def get_column(src, first, col, t):
    flat, at = strided(src, first, t, col)
    return flat[at, :]


def lanes_of(ref, row):
    x = ref[row : row + 1, :].astype(F32)
    return [x[:, 0:LANES], widen(x[:, LANES:])]


def bias_of(ref, row):
    return jnp.concatenate(lanes_of(ref, row), axis=1)


def k_first(par, field, south, main, ewi, ewc, top):
    cols, rows, channels = field.shape
    rem = channels - LANES - HALF
    even = par[0] == 0

    def edge(flip):
        def get(k, t):
            pick = []
            for col in (k, cols - HALO + k):
                tiles = [tile_at(field, col, 0, rows, t), tile_at(south, col, 0, south.shape[1], t)]
                pick.append(jnp.concatenate(tiles, axis=0))
            return jnp.where(even != flip, pick[1], pick[0])

        return get

    tall = rows + south.shape[1]
    pack(edge(False), putter(ewi, tall), HALO, tall, rem)
    pack(edge(True), putter(ewc, tall), HALO, tall, rem)
    for col in range(cols):
        for t in range(2):
            put_column(top, 0, col, t, tile_at(field, col, rows - 8, rows, t))
    pack(lambda k, t: top[7 - k, t, 0:cols, :], putter(main, cols), 3, cols, rem)


def k_weights(w, *refs):
    layers, _, channels, _ = w.shape
    outs, (buf, sems) = refs[: 2 * layers], refs[2 * layers :]
    copies = [pltpu.make_async_copy(w.at[i], buf.at[i], sems.at[i]) for i in range(layers)]
    for copy in copies:
        copy.start()
    for i in range(layers):
        wh, wl = outs[2 * i : 2 * i + 2]
        copies[i].wait()
        for k in range(9):
            x = buf[i, k]
            h = x.astype(BF16)
            at = (k % 3) * 2 * LANES
            for ref, value in ((wh, h), (wl, (x - h.astype(F32)).astype(BF16))):
                wide = jnp.concatenate([value, jnp.zeros((channels, 2 * LANES - channels), BF16)], axis=1)
                ref[k // 3, at : at + channels, :] = wide
                ref[k // 3, at + channels : at + 2 * LANES, :] = jnp.zeros((2 * LANES - channels, 2 * LANES), BF16)


def sided(par, ewi, ewc, rows, width, rem):
    even = par[0] == 0
    i, c = slots_of(ewi, rows, width, rem), slots_of(ewc, rows, width, rem)
    west = [jnp.where(even, y, x) for x, y in zip(i, c)]
    east = [jnp.where(even, x, y) for x, y in zip(i, c)]
    return west.__getitem__, east.__getitem__


def k_corner(par, ewi, ewc, out, top, *, tall, rows, rem):
    west, east = sided(par, ewi, ewc, HALO, tall, rem)
    for side, slot in enumerate((west, east)):
        for k in range(HALO):
            tiles = unpack(slot, k, HALO, tall, rem)
            for t in range(2):
                put_column(top, 0, side * HALO + k, t, tiles[t][rows - 8 : rows])
    pack(lambda k, t: top[7 - k, t], putter(out, 2 * HALO), 3, 2 * HALO, rem)


def k_corner2(par, ewi, ewc, out, *, rows, rem):
    west, east = sided(par, ewi, ewc, rows, HALO, rem)
    tiles = []
    for k in range(8):
        w = unpack(west, rows - 1 - k, rows, HALO, rem)
        e = unpack(east, rows - 1 - k, rows, HALO, rem)
        tiles.append([jnp.concatenate([w[t], e[t]], axis=0) for t in range(2)])
    pack(lambda k, t: tiles[k][t], putter(out, 2 * HALO), 8, 2 * HALO, rem)


def k_a(par, field, south, ewi, ewc, wh, wl, bias, st1, se, x0, *buffers):
    cols, rows, channels = field.shape
    rem = channels - LANES - HALF
    deep = south.shape[1]
    west, east = sided(par, ewi, ewc, HALO, rows + deep, rem)

    def put(col, tiles):
        for t in range(2):
            for h in range(0, rows, 8):
                put_column(x0, h, col, t, tiles[t][h : h + 8])
            put_column(se, 0, col, t, tiles[t][rows : rows + 8])

    for k in range(HALO):
        put(k, unpack(west, k, HALO, rows + deep, rem))
        put(HALO + cols + k, unpack(east, k, HALO, rows + deep, rem))
    for col in range(cols):
        for t in range(2):
            for h in range(0, rows, 8):
                put_column(x0, h, HALO + col, t, tile_at(field, col, h, h + 8, t))
            put_column(se, 0, HALO + col, t, tile_at(south, col, 0, 8, t))
    sources = run(se, deep - 1, 1, (1, 2, 3)) + run(x0, 0, rows, (1, 2, 3))
    conv(buffers, wh, wl, bias_of(bias, 0), 1, sources, rows - 1, 5, add_rows(st1, 0, x0, 0, 2, 5))


def signed(tiles, sign):
    return tiles if sign is None else [tiles[t] * sign[t] for t in range(2)]


def north_rows(dst, dst_row, main, sign, count, width, left, rem):
    slot = turned(slots_of(main, count, width, rem)).__getitem__
    for k in range(count):
        put_row(dst, dst_row + k, left, signed(unpack(slot, k, count, width, rem), sign))


def north_corners(dst, dst_row, corner, sign, count, cols, left, rem):
    width = 2 * HALO
    slot = turned(slots_of(corner, count, width, rem)).__getitem__
    for k in range(count):
        t = signed(unpack(slot, k, count, width, rem), sign)
        put_row(dst, dst_row + k, left - HALO, [x[0:HALO] for x in t])
        put_row(dst, dst_row + k, left + cols, [x[HALO:] for x in t])


def k_b(edge, main, corner, st1, sign, wh0, wl0, wh1, wl1, bias, st2, out, x0, xr, x1, hi, lo, *buffers, cols, rem):
    rows = edge.shape[0]
    sign = lanes_of(sign, 0)
    north_rows(xr, 1, main, None, 3, cols, HALO, rem)
    north_corners(xr, 1, corner, None, 3, cols, HALO, rem)
    x0[0:2] = edge[rows - 2 :]
    for t in range(2):
        x0[2, t] = xr[1, t] * sign[t]
        xr[0, t] = edge[rows - 1, t] * sign[t]
    x1[0:5] = st1[rows - 6 : rows - 1]
    offs = (1, 2, 3)
    fill(hi, lo, 0, x0, 0, 3, offs)
    fill(hi, lo, 3, xr, 0, 4, offs[::-1])
    total = None
    for a in range(3):
        both = [jnp.concatenate([x[a : a + 1], x[5 - a : 7 - a]]).reshape(3 * MW, x.shape[-1]) for x in (hi, lo)]
        for left, right in ((both[0], wh0), (both[1], wh0), (both[0], wl0)):
            term = jnp.dot(left, right[a], preferred_element_type=F32)
            total = term if total is None else total + term
    grown = jax.nn.gelu(total + bias_of(bias, 0))
    for q in range(3):
        for t in range(2):
            g = grown[q * MW : (q + 1) * MW, t * LANES : (t + 1) * LANES]
            if q == 0:
                x1[5, t, 0:MW, :] = x0[1, t, 2 : 2 + MW, :] + g
            else:
                x1[5 + q, t, 0:MW, :] = sign[t] * (xr[q, t, 2 : 2 + MW, :] + g)
    conv(buffers, wh1, wl1, bias_of(bias, 1), 2, run(x1, 0, 8, (0, 2, 4)), 4, 4, add_rows(st2, 0, x1, 2, 2, 4))
    wide = cols + 8
    pack(lambda k, t: st2[3 - k, t, 0:wide, :], putter(out, wide), 4, wide, rem)


def k_c1(st1, st2b, wh1, wl1, wh2, wl2, bias, st2, st3, out, h1, l1, h2, l2, *, cols, rem):
    conv((h1, l1), wh1, wl1, bias_of(bias, 1), 2, run(st1, 2, 12, (0, 2, 4)), 8, 4, add_rows(st2, 0, st1, 4, 2, 4))
    st2[8:12] = st2b[...]
    conv((h2, l2), wh2, wl2, bias_of(bias, 2), 4, run(st2, 0, 12, (0, 4, 8)), 4, 4, add_rows(st3, 0, st2, 4, 4, 4))
    pack(lambda k, t: st3[3 - k, t, 0:cols, :], putter(out, cols), 4, cols, rem)


def k_c2(st1, st2m, se, wh1, wl1, wh2, wl2, bias, st3, x2, h1, l1, h2, l2):
    south = se.shape[0]
    sources = run(se, south - 2, 2, (2, 4, 6)) + run(st1, 0, 6, (0, 2, 4))
    conv((h1, l1), wh1, wl1, bias_of(bias, 1), 2, sources, 4, 4, add_rows(x2, 0, st1, 0, 2, 4))
    x2[4:8] = st2m[0:4]
    sources = run(se, south - 4, 4, (4, 8, 12)) + run(x2, 0, 4, (0, 4, 8)) + run(st2m, 0, 8, (0, 4, 8))
    conv((h2, l2), wh2, wl2, bias_of(bias, 2), 4, sources, 8, 4, add_rows(st3, 0, x2, 0, 4, 4))


def row_of(parts, row):
    for part in parts:
        if row < part.shape[0]:
            return part, row
        row -= part.shape[0]


def k_d(par, st2, north, st3l, st3m, sign, wh, wl, bias, st3b, out, ewi, ewc, x2, hi, lo, *, cols, rem):
    wide = cols + 8
    north_rows(x2, 0, north, lanes_of(sign, 0), 4, wide, 0, rem)
    sources = run(st2, 4, 8, (0, 4, 8)) + run(x2, 0, 4, (0, 4, 8))
    conv((hi, lo), wh, wl, bias_of(bias, 2), 4, sources, 4, 4, add_rows(st3b, 0, st2, 8, 4, 4))
    pack(lambda k, t: st3b[3 - k, t, 0:cols, :], putter(out, cols), 4, cols, rem)
    even = par[0] == 0
    parts = (st3l, st3m, st3b)
    rows = sum(x.shape[0] for x in parts)

    def edge(flip):
        def get(k, t):
            ref, row = row_of(parts, k)
            west, east = ref[row, t, 0:HALO, :], ref[row, t, cols - HALO : cols, :]
            return jnp.where(even != flip, east, west)

        return get

    pack(edge(False), putter(ewi, HALO), rows, HALO, rem)
    pack(edge(True), putter(ewc, HALO), rows, HALO, rem)


def put_out(out, first, src, cols, channels):
    for col in range(cols):
        out[col, first : first + 8, 0:LANES] = get_column(src, 0, col, 0)
        out[col, first : first + 8, LANES:channels] = get_column(src, 0, col, 1)[:, 0 : channels - LANES]


def k_f(st3l, st3m, st3b, se, wh, wl, bias, acc, x3, hi, lo, *, cols):
    rows = acc.shape[0]
    south = se.shape[0]
    zero = jnp.zeros((2, HALO, LANES), F32)
    for k in range(rows + south):
        ref, row = (se, k) if k < south else row_of((st3l, st3m, st3b), k - south)
        x3[k, :, 0:HALO, :] = zero
        at = HALO if k < south else 0
        x3[k, :, HALO : HALO + cols, :] = ref[row, :, at : at + cols, :]
        x3[k, :, HALO + cols : 2 * HALO + cols, :] = zero
    bias = bias_of(bias, 3)
    filled = 0
    for row in range(0, rows, 4):
        taps = (0, 1, 2) if row < rows - 8 else (0, 1)
        while filled < row + 4 + 8 * taps[-1]:
            fill_row(hi, lo, filled, x3, filled, (0, 8, 16))
            filled += 1
        total = products(hi, lo, wh, wl, taps, row, 4, 8)
        acc[row : row + 4] = (total + bias).reshape(4, MW, 2 * LANES)


def split_bf16(x):
    h = x.astype(BF16)
    return h, (x - h.astype(F32)).astype(BF16)


def edge_sums(tiles_of, wh, wl, taps):
    total = None
    for a in taps:
        h, l = split_bf16(tiles_of(a))
        for left, right in ((h, wh), (l, wh), (h, wl)):
            term = jnp.dot(left, right(a), preferred_element_type=F32)
            total = term if total is None else total + term
    return total


def side_weights(ref, b):
    at = b * 2 * LANES
    return lambda a: ref[a, at : at + 2 * LANES, :]


def k_g(par, acc, st3l, st3m, st3b, se, ewi, ewc, na, nb, sign, wh, wl, out, accn, xn, halo, end, hi, lo, *, cols, rem):
    rows = acc.shape[0]
    channels = out.shape[-1]
    south = se.shape[0]
    sign = lanes_of(sign, 0)
    zero = jnp.zeros((8, 2, HALO, LANES), F32)
    xn[:, :, 0:HALO, :] = zero
    xn[:, :, HALO + cols : 2 * HALO + cols, :] = zero
    north_rows(xn, 0, nb, sign, 4, cols, HALO, rem)
    north_rows(xn, 4, na, sign, 4, cols, HALO, rem)
    fill(hi, lo, 0, xn, 0, 8, (0, 8, 16))
    accn[0 : rows - 8] = acc[0 : rows - 8]
    for i in range(2):
        at = slice(4 * i, 4 * i + 4)
        lh = hi[at].reshape(4 * MW, hi.shape[-1])
        ll = lo[at].reshape(4 * MW, hi.shape[-1])
        total = acc[rows - 8 + 4 * i : rows - 4 + 4 * i].reshape(4 * MW, 2 * LANES)
        for left, right in ((lh, wh), (ll, wh), (lh, wl)):
            total = total + jnp.dot(left, right[2], preferred_element_type=F32)
        accn[rows - 8 + 4 * i : rows - 4 + 4 * i] = total.reshape(4, MW, 2 * LANES)
    for side, slot in enumerate(sided(par, ewi, ewc, rows, HALO, rem)):
        b, to = ((0, 0), (2, cols - HALO))[side]
        at = side * (HALO + cols)
        for k in range(south):
            for t in range(2):
                halo[side, k * HALO : (k + 1) * HALO, t * LANES : (t + 1) * LANES] = se[k, t, at : at + HALO, :]
        for k in range(rows):
            tiles = unpack(slot, k, rows, HALO, rem)
            for t in range(2):
                halo[side, (south + k) * HALO : (south + k + 1) * HALO, t * LANES : (t + 1) * LANES] = tiles[t]
        halo[side, (south + rows) * HALO :, :] = jnp.zeros((8 * HALO, 2 * LANES), F32)
        total = edge_sums(
            lambda a: halo[side, 8 * a * HALO : (8 * a + rows) * HALO, :],
            side_weights(wh, b), side_weights(wl, b), (0, 1, 2),
        )
        for k in range(rows):
            accn[k, to : to + HALO, :] += total[k * HALO : (k + 1) * HALO]
    for half in range(0, rows, 8):
        for k in range(8):
            grown = jax.nn.gelu(accn[half + k])
            ref, row = row_of((st3l, st3m, st3b), half + k)
            for t in range(2):
                end[half // 8, k, t] = ref[row, t] + grown[:, t * LANES : (t + 1) * LANES]
        put_out(out, half, end.at[half // 8], cols, channels)


def k_h(before, accn, st3m, st3b, nc, sign, wh, wl, out, xc, end, done, sems, *, cols, rem):
    rows = accn.shape[0]
    channels = out.shape[-1]
    slot = turned(slots_of(nc, 8, 2 * HALO, rem)).__getitem__
    for k in range(8):
        tiles = signed(unpack(slot, k, 8, 2 * HALO, rem), lanes_of(sign, 0))
        for t in range(2):
            for side in range(2):
                xc[side, k * HALO : (k + 1) * HALO, t * LANES : (t + 1) * LANES] = tiles[t][side * HALO : (side + 1) * HALO]
    copies = []
    for side in range(2):
        b, at = ((0, 0), (2, cols - HALO))[side]
        total = edge_sums(lambda a: xc[side], side_weights(wh, b), side_weights(wl, b), (2,))
        for k in range(8):
            ref, row = row_of((st3m, st3b), k)
            grown = jax.nn.gelu(accn[rows - 8 + k, at : at + HALO, :] + total[k * HALO : (k + 1) * HALO])
            for t in range(2):
                end[k, t] = ref[row, t, at : at + HALO, :] + grown[:, t * LANES : (t + 1) * LANES]
        put_out(done.at[side], 0, end, HALO, channels)
        copies.append(
            pltpu.make_async_copy(done.at[side], out.at[pl.ds(at, HALO), pl.ds(rows - 8, 8), :], sems.at[side])
        )
        copies[-1].start()
    for copy in copies:
        copy.wait()


VM = pl.BlockSpec(memory_space=pltpu.VMEM)
SM = pl.BlockSpec(memory_space=pltpu.SMEM)
HB = pl.BlockSpec(memory_space=pl.ANY)


def lhs(rows):
    return [pltpu.VMEM((rows, MW, 6 * LANES), BF16)] * 2


def call(kernel, outs, scratch, args, smem=0, flops=0, limit=16, hbm=(), alias=None):
    moved = sum(a.size * a.dtype.itemsize for a in args[smem:])
    outs = [o if isinstance(o, jax.ShapeDtypeStruct) else jax.ShapeDtypeStruct(o, F32) for o in outs]
    return pl.pallas_call(
        kernel,
        out_shape=outs,
        in_specs=[SM if i < smem else HB if i in hbm else VM for i in range(len(args))],
        out_specs=[HB if alias else VM] * len(outs),
        input_output_aliases=alias or {},
        scratch_shapes=scratch,
        compiler_params=pltpu.CompilerParams(vmem_limit_bytes=limit * 2**20),
        cost_estimate=pl.CostEstimate(flops=flops, bytes_accessed=moved, transcendentals=0),
    )(*args)


def layers_of(field, south_rows, sign_mask, weights, biases):
    rows, cols, channels = field.shape
    south = south_rows.shape[0]
    layers = weights.shape[0]
    rem = channels - LANES - HALF
    devices = lax.axis_size("lon")
    mirror = [(i, devices - 1 - i) for i in range(devices)]
    intra = [(i, i ^ 1) for i in range(devices)]
    cross = [(i, (i + 1) % devices if i % 2 else (i - 1) % devices) for i in range(devices)]
    send = lambda x, route: lax.ppermute(x, "lon", route)
    par = (lax.axis_index("lon") % 2).astype(jnp.int32).reshape(1)
    sign = sign_mask.reshape(1, channels)
    field = jnp.swapaxes(field, 0, 1)
    south_rows = jnp.swapaxes(south_rows, 0, 1)
    row_flops = MW * 6 * LANES * 2 * LANES * 2 * 9
    tall = rows + south

    def state(n, width):
        return (n, 2, width, LANES)

    ew_rows = packed_rows(HALO, tall, rem)
    main, ewi, ewc = call(
        k_first,
        [(packed_rows(3, cols, rem), LANES), (ew_rows, LANES), (ew_rows, LANES)],
        [pltpu.VMEM(state(8, 56), F32)], [par, field, south_rows], smem=1,
    )
    ewi, ewc, main = send(ewi, intra), send(ewc, cross), send(main, mirror)
    split = call(
        k_weights,
        [jax.ShapeDtypeStruct((3, 6 * LANES, 2 * LANES), BF16)] * (2 * layers),
        [pltpu.VMEM(weights.shape, F32), pltpu.SemaphoreType.DMA((layers,))],
        [weights], limit=24, hbm=(0,),
    )
    (corner,) = call(
        functools.partial(k_corner, tall=tall, rows=rows, rem=rem),
        [(packed_rows(3, 2 * HALO, rem), LANES)], [pltpu.VMEM(state(8, 2 * HALO), F32)],
        [par, ewi, ewc], smem=1,
    )
    corner = send(corner, mirror)
    st1, se, x0 = call(
        k_a,
        [state(rows - 1, 72), state(south, 80), state(rows, 72)],
        lhs(rows + 1),
        [par, field, south_rows, ewi, ewc, *split[0:2], biases],
        smem=1, flops=15 * row_flops,
    )
    st2b, north = call(
        functools.partial(k_b, cols=cols, rem=rem),
        [state(4, 72), (packed_rows(4, cols + 8, rem), LANES)],
        [pltpu.VMEM(state(3, 72), F32), pltpu.VMEM(state(4, 72), F32), pltpu.VMEM(state(8, 72), F32)] + lhs(7) + lhs(8),
        [x0, main, corner, st1, sign, *split[0:4], biases],
        flops=7 * row_flops,
    )
    north = send(north, mirror)
    st2m, st3m, na = call(
        functools.partial(k_c1, cols=cols, rem=rem),
        [state(12, 72), state(4, MW), (packed_rows(4, cols, rem), LANES)],
        lhs(12) + lhs(12),
        [st1, st2b, *split[2:6], biases],
        flops=12 * row_flops,
    )
    na = send(na, mirror)
    (st3l,) = call(
        k_c2,
        [state(8, MW)],
        [pltpu.VMEM(state(8, 72), F32)] + lhs(8) + lhs(16),
        [st1, st2m, se, *split[2:6], biases],
        flops=12 * row_flops,
    )
    ew_rows = packed_rows(rows, HALO, rem)
    st3b, nb, ewi, ewc = call(
        functools.partial(k_d, cols=cols, rem=rem),
        [state(4, MW), (packed_rows(4, cols, rem), LANES), (ew_rows, LANES), (ew_rows, LANES)],
        [pltpu.VMEM(state(4, 72), F32)] + lhs(12),
        [par, st2m, north, st3l, st3m, sign, *split[4:6], biases],
        smem=1, flops=4 * row_flops,
    )
    ewi, ewc = send(ewi, intra), send(ewc, cross)
    nb = send(nb, mirror)
    (nc,) = call(
        functools.partial(k_corner2, rows=rows, rem=rem),
        [(packed_rows(8, 2 * HALO, rem), LANES)], [], [par, ewi, ewc], smem=1,
    )
    nc = send(nc, mirror)
    (acc,) = call(
        functools.partial(k_f, cols=cols),
        [(rows, MW, 2 * LANES)],
        [pltpu.VMEM(state(rows + south, 80), F32)] + lhs(rows + south),
        [st3l, st3m, st3b, se, *split[6:8], biases],
        flops=(rows - 3) * row_flops,
    )
    out, acc = call(
        functools.partial(k_g, cols=cols, rem=rem),
        [(cols, rows, channels), (rows, MW, 2 * LANES)],
        [pltpu.VMEM(state(8, 80), F32), pltpu.VMEM((2, (rows + south + 8) * HALO, 2 * LANES), F32),
         pltpu.VMEM((2,) + state(8, MW), F32)] + lhs(8),
        [par, acc, st3l, st3m, st3b, se, ewi, ewc, na, nb, sign, *split[6:8]],
        smem=1, flops=4 * row_flops,
    )
    (out,) = call(
        functools.partial(k_h, cols=cols, rem=rem),
        [(cols, rows, channels)],
        [pltpu.VMEM((2, 8 * HALO, 2 * LANES), F32), pltpu.VMEM(state(8, HALO), F32),
         pltpu.VMEM((2, HALO, 8, channels), F32), pltpu.SemaphoreType.DMA((2,))],
        [out, acc, st3m, st3b, nc, sign, *split[6:8]],
        hbm=(0,), alias={0: 0}, flops=row_flops,
    )
    return jnp.swapaxes(out, 0, 1)


def solution(mesh):
    in_specs = (P(None, "lon", None), P(None, "lon", None), P(), P(), P())
    out_specs = P(None, "lon", None)
    return jax.shard_map(layers_of, mesh=mesh, in_specs=in_specs, out_specs=out_specs, check_vma=False)
```

```python
import functools

import jax
import jax.numpy as jnp
from jax import lax
from jax.experimental import pallas as pl
from jax.experimental.pallas import tpu as pltpu
from jax.sharding import PartitionSpec as P

F32 = jnp.float32
BF16 = jnp.bfloat16
LANES = 128
HALF = 64
MW = 64
HALO = 8


def merged(rows):
    return rows % 2 == 1 and rows <= 8


def rest_groups(rows, width, rem):
    groups = max(1, LANES // (rows * rem))
    return groups, width if groups == 1 else (-(-width // groups) + 7) // 8 * 8


def packed_rows(rows, width, rem):
    full = rows + (rows + 1) // 2
    return full * width + (0 if merged(rows) else rest_groups(rows, width, rem)[1])


def lane_of(width):
    return lax.broadcasted_iota(jnp.int32, (width, LANES), 1)


def roll(x, shift):
    shift = shift % LANES
    return x if shift == 0 else pltpu.roll(x, shift, 1)


def pack(get, put, rows, width, rem):
    lane = lane_of(width)
    halves = (rows + 1) // 2
    for k in range(rows):
        put(k, get(k, 0))
    second = [get(k, 1) for k in range(rows)]
    for p in range(halves):
        other = roll(second[2 * p + 1], HALF) if 2 * p + 1 < rows else jnp.zeros((width, LANES), F32)
        tile = jnp.where(lane < HALF, second[2 * p], other)
        if merged(rows) and p == halves - 1:
            for k in range(rows):
                at = HALF + rem * k
                tile = jnp.where((lane >= at) & (lane < at + rem), roll(second[k], rem * k), tile)
        put(rows + p, tile)
    if not merged(rows):
        tile = jnp.zeros((width, LANES), F32)
        for k in range(rows):
            tile = jnp.where((lane >= rem * k) & (lane < rem * k + rem), roll(second[k], rem * k - HALF), tile)
        groups, high = rest_groups(rows, width, rem)
        total = None
        for g in range(groups):
            part = tile[g * high : min(width, (g + 1) * high)]
            if part.shape[0] < high:
                part = jnp.concatenate([part, jnp.zeros((high - part.shape[0], LANES), F32)], axis=0)
            part = roll(part, g * rows * rem)
            total = part if total is None else total + part
        put(rows + halves, total)


def unpack(slot, k, rows, width, rem):
    lane = lane_of(width)
    halves = (rows + 1) // 2
    half = roll(slot(rows + k // 2), HALF * (k % 2))
    if merged(rows):
        rest = roll(slot(rows + halves - 1), -rem * k)
    else:
        rest = roll(slot(rows + halves), HALF - rem * k)
    tile = jnp.where(lane < HALF, half, jnp.where(lane < HALF + rem, rest, 0.0))
    return slot(k), tile


def slots_of(ref, rows, width, rem):
    full = rows + (rows + 1) // 2
    tiles = [ref[k * width : (k + 1) * width, :] for k in range(full)]
    if not merged(rows):
        groups, high = rest_groups(rows, width, rem)
        block = ref[full * width : full * width + high, :]
        parts = [roll(block, -g * rows * rem)[: min(high, width - g * high)] for g in range(groups)]
        tiles.append(parts[0] if groups == 1 else jnp.concatenate(parts, axis=0))
    return tiles


def putter(ref, width):
    def put(k, tile):
        ref[k * width : (k + 1) * width, :] = tile

    return put


def turned(tiles):
    order = 7 - lax.broadcasted_iota(jnp.int32, (8, LANES), 0)
    flip = lambda x: jnp.take_along_axis(x, order, axis=0)

    def one(x):
        parts, left = [], x.shape[0]
        while left >= 8:
            parts.append(flip(x[left - 8 : left]))
            left -= 8
        if left:
            parts.append(flip(x[0:8])[8 - left :])
        return jnp.concatenate(parts, axis=0)

    return [one(x) for x in tiles]


def fill_row(hi, lo, dst, ref, row, offs):
    for b in range(3):
        for t in range(2):
            x = ref[row, t, offs[b] : offs[b] + MW, :]
            h = x.astype(BF16)
            at = b * 2 * LANES + t * LANES
            hi[dst, :, at : at + LANES] = h
            lo[dst, :, at : at + LANES] = (x - h.astype(F32)).astype(BF16)


def fill(hi, lo, dst, ref, src, count, offs):
    for i in range(count):
        fill_row(hi, lo, dst + i, ref, src + i, offs)


def run(ref, first, count, offs):
    return [(ref, first + i, offs) for i in range(count)]


def products(hi, lo, wh, wl, taps, row, chunk, dilate):
    total = None
    for a in taps:
        at = slice(row + a * dilate, row + a * dilate + chunk)
        lh = hi[at].reshape(chunk * MW, hi.shape[-1])
        ll = lo[at].reshape(chunk * MW, hi.shape[-1])
        for left, right in ((lh, wh), (ll, wh), (lh, wl)):
            term = jnp.dot(left, right[a], preferred_element_type=F32)
            total = term if total is None else total + term
    return total


def conv(buffers, wh, wl, bias, dilate, sources, count, chunk, emit):
    hi, lo = buffers
    filled = 0
    for row in range(0, count, chunk):
        while filled < row + chunk + 2 * dilate:
            fill_row(hi, lo, filled, *sources[filled])
            filled += 1
        total = products(hi, lo, wh, wl, (0, 1, 2), row, chunk, dilate)
        emit(row, jax.nn.gelu(total + bias))


def add_rows(out, out_row, res, res_row, off, chunk):
    def emit(row, grown):
        for q in range(chunk):
            for t in range(2):
                out[out_row + row + q, t, 0:MW, :] = (
                    res[res_row + row + q, t, off : off + MW, :]
                    + grown[q * MW : (q + 1) * MW, t * LANES : (t + 1) * LANES]
                )

    return emit


def put_row(dst, row, at, tiles):
    for t in range(2):
        dst[row, t, at : at + tiles[t].shape[0], :] = tiles[t]


def widen(x):
    return jnp.concatenate([x, jnp.zeros(x.shape[:-1] + (LANES - x.shape[-1],), F32)], axis=-1)


def tile_at(ref, col, lo, hi, t):
    return ref[col, lo:hi, 0:LANES] if t == 0 else widen(ref[col, lo:hi, LANES : ref.shape[-1]])


def strided(dst, first, t, col):
    rows, _, width, _ = dst.shape
    return dst.reshape(rows * 2 * width, LANES), pl.ds((2 * first + t) * width + col, 8, stride=2 * width)


def put_column(dst, first, col, t, tile):
    flat, at = strided(dst, first, t, col)
    flat[at, :] = tile


def get_column(src, first, col, t):
    flat, at = strided(src, first, t, col)
    return flat[at, :]


def lanes_of(ref, row):
    x = ref[row : row + 1, :].astype(F32)
    return [x[:, 0:LANES], widen(x[:, LANES:])]


def bias_of(ref, row):
    return jnp.concatenate(lanes_of(ref, row), axis=1)


def k_first(par, field, south, main, ewi, ewc, top, fedge, sedge, last, sems):
    cols, rows, channels = field.shape
    rem = channels - LANES - HALF
    even = par[0] == 0
    sides = (pl.ds(0, HALO), pl.ds(cols - HALO, HALO))
    copies = [pltpu.make_async_copy(field.at[at], fedge.at[i], sems.at[i]) for i, at in enumerate(sides)]
    copies += [pltpu.make_async_copy(south.at[at], sedge.at[i], sems.at[2 + i]) for i, at in enumerate(sides)]
    copies += [pltpu.make_async_copy(field.at[:, pl.ds(rows - 8, 8), :], last, sems.at[4])]
    for copy in copies:
        copy.start()
    for copy in copies[:4]:
        copy.wait()

    def edge(flip):
        def get(k, t):
            pick = []
            for i in range(2):
                tiles = [tile_at(fedge.at[i], k, 0, rows, t), tile_at(sedge.at[i], k, 0, south.shape[1], t)]
                pick.append(jnp.concatenate(tiles, axis=0))
            return jnp.where(even != flip, pick[1], pick[0])

        return get

    tall = rows + south.shape[1]
    pack(edge(False), putter(ewi, tall), HALO, tall, rem)
    pack(edge(True), putter(ewc, tall), HALO, tall, rem)
    copies[4].wait()
    for col in range(cols):
        for t in range(2):
            put_column(top, 0, col, t, tile_at(last, col, 0, 8, t))
    pack(lambda k, t: top[7 - k, t, 0:cols, :], putter(main, cols), 3, cols, rem)


def k_weights(w, *refs):
    layers, _, channels, _ = w.shape
    outs, (buf, sems) = refs[: 2 * layers], refs[2 * layers :]
    copies = [pltpu.make_async_copy(w.at[i], buf.at[i], sems.at[i]) for i in range(layers)]
    for copy in copies:
        copy.start()
    for i in range(layers):
        wh, wl = outs[2 * i : 2 * i + 2]
        copies[i].wait()
        for k in range(9):
            x = buf[i, k]
            h = x.astype(BF16)
            at = (k % 3) * 2 * LANES
            for ref, value in ((wh, h), (wl, (x - h.astype(F32)).astype(BF16))):
                wide = jnp.concatenate([value, jnp.zeros((channels, 2 * LANES - channels), BF16)], axis=1)
                ref[k // 3, at : at + channels, :] = wide
                ref[k // 3, at + channels : at + 2 * LANES, :] = jnp.zeros((2 * LANES - channels, 2 * LANES), BF16)


def sided(par, ewi, ewc, rows, width, rem):
    even = par[0] == 0
    i, c = slots_of(ewi, rows, width, rem), slots_of(ewc, rows, width, rem)
    west = [jnp.where(even, y, x) for x, y in zip(i, c)]
    east = [jnp.where(even, x, y) for x, y in zip(i, c)]
    return west.__getitem__, east.__getitem__


def k_corner(par, ewi, ewc, out, top, *, tall, rows, rem):
    west, east = sided(par, ewi, ewc, HALO, tall, rem)
    for side, slot in enumerate((west, east)):
        for k in range(HALO):
            tiles = unpack(slot, k, HALO, tall, rem)
            for t in range(2):
                put_column(top, 0, side * HALO + k, t, tiles[t][rows - 8 : rows])
    pack(lambda k, t: top[7 - k, t], putter(out, 2 * HALO), 3, 2 * HALO, rem)


def k_corner2(par, ewi, ewc, out, *, rows, rem):
    west, east = sided(par, ewi, ewc, rows, HALO, rem)
    tiles = []
    for k in range(8):
        w = unpack(west, rows - 1 - k, rows, HALO, rem)
        e = unpack(east, rows - 1 - k, rows, HALO, rem)
        tiles.append([jnp.concatenate([w[t], e[t]], axis=0) for t in range(2)])
    pack(lambda k, t: tiles[k][t], putter(out, 2 * HALO), 8, 2 * HALO, rem)


def k_a(par, field, south, ewi, ewc, wh, wl, bias, st1, se, x0, *buffers):
    cols, rows, channels = field.shape
    rem = channels - LANES - HALF
    deep = south.shape[1]
    west, east = sided(par, ewi, ewc, HALO, rows + deep, rem)

    def put(col, tiles):
        for t in range(2):
            for h in range(0, rows, 8):
                put_column(x0, h, col, t, tiles[t][h : h + 8])
            put_column(se, 0, col, t, tiles[t][rows : rows + 8])

    for k in range(HALO):
        put(k, unpack(west, k, HALO, rows + deep, rem))
        put(HALO + cols + k, unpack(east, k, HALO, rows + deep, rem))
    for col in range(cols):
        for t in range(2):
            for h in range(0, rows, 8):
                put_column(x0, h, HALO + col, t, tile_at(field, col, h, h + 8, t))
            put_column(se, 0, HALO + col, t, tile_at(south, col, 0, 8, t))
    sources = run(se, deep - 1, 1, (1, 2, 3)) + run(x0, 0, rows, (1, 2, 3))
    conv(buffers, wh, wl, bias_of(bias, 0), 1, sources, rows - 1, 5, add_rows(st1, 0, x0, 0, 2, 5))


def signed(tiles, sign):
    return tiles if sign is None else [tiles[t] * sign[t] for t in range(2)]


def north_rows(dst, dst_row, main, sign, count, width, left, rem):
    slot = turned(slots_of(main, count, width, rem)).__getitem__
    for k in range(count):
        put_row(dst, dst_row + k, left, signed(unpack(slot, k, count, width, rem), sign))


def north_corners(dst, dst_row, corner, sign, count, cols, left, rem):
    width = 2 * HALO
    slot = turned(slots_of(corner, count, width, rem)).__getitem__
    for k in range(count):
        t = signed(unpack(slot, k, count, width, rem), sign)
        put_row(dst, dst_row + k, left - HALO, [x[0:HALO] for x in t])
        put_row(dst, dst_row + k, left + cols, [x[HALO:] for x in t])


def k_b(edge, main, corner, st1, sign, wh0, wl0, wh1, wl1, bias, st2, out, x0, xr, x1, hi, lo, *buffers, cols, rem):
    rows = edge.shape[0]
    sign = lanes_of(sign, 0)
    north_rows(xr, 1, main, None, 3, cols, HALO, rem)
    north_corners(xr, 1, corner, None, 3, cols, HALO, rem)
    x0[0:2] = edge[rows - 2 :]
    for t in range(2):
        x0[2, t] = xr[1, t] * sign[t]
        xr[0, t] = edge[rows - 1, t] * sign[t]
    x1[0:5] = st1[rows - 6 : rows - 1]
    offs = (1, 2, 3)
    fill(hi, lo, 0, x0, 0, 3, offs)
    fill(hi, lo, 3, xr, 0, 4, offs[::-1])
    total = None
    for a in range(3):
        both = [jnp.concatenate([x[a : a + 1], x[5 - a : 7 - a]]).reshape(3 * MW, x.shape[-1]) for x in (hi, lo)]
        for left, right in ((both[0], wh0), (both[1], wh0), (both[0], wl0)):
            term = jnp.dot(left, right[a], preferred_element_type=F32)
            total = term if total is None else total + term
    grown = jax.nn.gelu(total + bias_of(bias, 0))
    for q in range(3):
        for t in range(2):
            g = grown[q * MW : (q + 1) * MW, t * LANES : (t + 1) * LANES]
            if q == 0:
                x1[5, t, 0:MW, :] = x0[1, t, 2 : 2 + MW, :] + g
            else:
                x1[5 + q, t, 0:MW, :] = sign[t] * (xr[q, t, 2 : 2 + MW, :] + g)
    conv(buffers, wh1, wl1, bias_of(bias, 1), 2, run(x1, 0, 8, (0, 2, 4)), 4, 4, add_rows(st2, 0, x1, 2, 2, 4))
    wide = cols + 8
    pack(lambda k, t: st2[3 - k, t, 0:wide, :], putter(out, wide), 4, wide, rem)


def k_c1(st1, st2b, wh1, wl1, wh2, wl2, bias, st2, st3, out, h1, l1, h2, l2, *, cols, rem):
    conv((h1, l1), wh1, wl1, bias_of(bias, 1), 2, run(st1, 2, 12, (0, 2, 4)), 8, 4, add_rows(st2, 0, st1, 4, 2, 4))
    st2[8:12] = st2b[...]
    conv((h2, l2), wh2, wl2, bias_of(bias, 2), 4, run(st2, 0, 12, (0, 4, 8)), 4, 4, add_rows(st3, 0, st2, 4, 4, 4))
    pack(lambda k, t: st3[3 - k, t, 0:cols, :], putter(out, cols), 4, cols, rem)


def k_c2(st1, st2m, se, wh1, wl1, wh2, wl2, bias, st3, x2, h1, l1, h2, l2):
    south = se.shape[0]
    sources = run(se, south - 2, 2, (2, 4, 6)) + run(st1, 0, 6, (0, 2, 4))
    conv((h1, l1), wh1, wl1, bias_of(bias, 1), 2, sources, 4, 4, add_rows(x2, 0, st1, 0, 2, 4))
    x2[4:8] = st2m[0:4]
    sources = run(se, south - 4, 4, (4, 8, 12)) + run(x2, 0, 4, (0, 4, 8)) + run(st2m, 0, 8, (0, 4, 8))
    conv((h2, l2), wh2, wl2, bias_of(bias, 2), 4, sources, 8, 4, add_rows(st3, 0, x2, 0, 4, 4))


def row_of(parts, row):
    for part in parts:
        if row < part.shape[0]:
            return part, row
        row -= part.shape[0]


def k_d(par, st2, north, st3l, st3m, sign, wh, wl, bias, st3b, out, ewi, ewc, x2, hi, lo, *, cols, rem):
    wide = cols + 8
    north_rows(x2, 0, north, lanes_of(sign, 0), 4, wide, 0, rem)
    sources = run(st2, 4, 8, (0, 4, 8)) + run(x2, 0, 4, (0, 4, 8))
    conv((hi, lo), wh, wl, bias_of(bias, 2), 4, sources, 4, 4, add_rows(st3b, 0, st2, 8, 4, 4))
    pack(lambda k, t: st3b[3 - k, t, 0:cols, :], putter(out, cols), 4, cols, rem)
    even = par[0] == 0
    parts = (st3l, st3m, st3b)
    rows = sum(x.shape[0] for x in parts)

    def edge(flip):
        def get(k, t):
            ref, row = row_of(parts, k)
            west, east = ref[row, t, 0:HALO, :], ref[row, t, cols - HALO : cols, :]
            return jnp.where(even != flip, east, west)

        return get

    pack(edge(False), putter(ewi, HALO), rows, HALO, rem)
    pack(edge(True), putter(ewc, HALO), rows, HALO, rem)


def put_out(out, first, src, cols, channels):
    for col in range(cols):
        out[col, first : first + 8, 0:LANES] = get_column(src, 0, col, 0)
        out[col, first : first + 8, LANES:channels] = get_column(src, 0, col, 1)[:, 0 : channels - LANES]


def k_f(st3l, st3m, st3b, se, wh, wl, bias, acc, x3, hi, lo, *, cols):
    rows = acc.shape[0]
    south = se.shape[0]
    zero = jnp.zeros((2, HALO, LANES), F32)
    for k in range(rows + south):
        ref, row = (se, k) if k < south else row_of((st3l, st3m, st3b), k - south)
        x3[k, :, 0:HALO, :] = zero
        at = HALO if k < south else 0
        x3[k, :, HALO : HALO + cols, :] = ref[row, :, at : at + cols, :]
        x3[k, :, HALO + cols : 2 * HALO + cols, :] = zero
    bias = bias_of(bias, 3)
    filled = 0
    for row in range(0, rows, 4):
        taps = (0, 1, 2) if row < rows - 8 else (0, 1)
        while filled < row + 4 + 8 * taps[-1]:
            fill_row(hi, lo, filled, x3, filled, (0, 8, 16))
            filled += 1
        total = products(hi, lo, wh, wl, taps, row, 4, 8)
        acc[row : row + 4] = (total + bias).reshape(4, MW, 2 * LANES)


def split_bf16(x):
    h = x.astype(BF16)
    return h, (x - h.astype(F32)).astype(BF16)


def edge_sums(tiles_of, wh, wl, taps):
    total = None
    for a in taps:
        h, l = split_bf16(tiles_of(a))
        for left, right in ((h, wh), (l, wh), (h, wl)):
            term = jnp.dot(left, right(a), preferred_element_type=F32)
            total = term if total is None else total + term
    return total


def side_weights(ref, b):
    at = b * 2 * LANES
    return lambda a: ref[a, at : at + 2 * LANES, :]


def k_g(par, acc, st3l, st3m, st3b, se, ewi, ewc, na, nb, sign, wh, wl, out, accn, xn, halo, end, hi, lo, *, cols, rem):
    rows = acc.shape[0]
    channels = out.shape[-1]
    south = se.shape[0]
    sign = lanes_of(sign, 0)
    zero = jnp.zeros((8, 2, HALO, LANES), F32)
    xn[:, :, 0:HALO, :] = zero
    xn[:, :, HALO + cols : 2 * HALO + cols, :] = zero
    north_rows(xn, 0, nb, sign, 4, cols, HALO, rem)
    north_rows(xn, 4, na, sign, 4, cols, HALO, rem)
    fill(hi, lo, 0, xn, 0, 8, (0, 8, 16))
    accn[0 : rows - 8] = acc[0 : rows - 8]
    for i in range(2):
        at = slice(4 * i, 4 * i + 4)
        lh = hi[at].reshape(4 * MW, hi.shape[-1])
        ll = lo[at].reshape(4 * MW, hi.shape[-1])
        total = acc[rows - 8 + 4 * i : rows - 4 + 4 * i].reshape(4 * MW, 2 * LANES)
        for left, right in ((lh, wh), (ll, wh), (lh, wl)):
            total = total + jnp.dot(left, right[2], preferred_element_type=F32)
        accn[rows - 8 + 4 * i : rows - 4 + 4 * i] = total.reshape(4, MW, 2 * LANES)
    for side, slot in enumerate(sided(par, ewi, ewc, rows, HALO, rem)):
        b, to = ((0, 0), (2, cols - HALO))[side]
        at = side * (HALO + cols)
        for k in range(south):
            for t in range(2):
                halo[side, k * HALO : (k + 1) * HALO, t * LANES : (t + 1) * LANES] = se[k, t, at : at + HALO, :]
        for k in range(rows):
            tiles = unpack(slot, k, rows, HALO, rem)
            for t in range(2):
                halo[side, (south + k) * HALO : (south + k + 1) * HALO, t * LANES : (t + 1) * LANES] = tiles[t]
        halo[side, (south + rows) * HALO :, :] = jnp.zeros((8 * HALO, 2 * LANES), F32)
        total = edge_sums(
            lambda a: halo[side, 8 * a * HALO : (8 * a + rows) * HALO, :],
            side_weights(wh, b), side_weights(wl, b), (0, 1, 2),
        )
        for k in range(rows):
            accn[k, to : to + HALO, :] += total[k * HALO : (k + 1) * HALO]
    for half in range(0, rows, 8):
        for k in range(8):
            grown = jax.nn.gelu(accn[half + k])
            ref, row = row_of((st3l, st3m, st3b), half + k)
            for t in range(2):
                end[half // 8, k, t] = ref[row, t] + grown[:, t * LANES : (t + 1) * LANES]
        put_out(out, half, end.at[half // 8], cols, channels)


def k_h(before, accn, st3m, st3b, nc, sign, wh, wl, out, xc, end, done, sems, *, cols, rem):
    rows = accn.shape[0]
    channels = out.shape[-1]
    slot = turned(slots_of(nc, 8, 2 * HALO, rem)).__getitem__
    for k in range(8):
        tiles = signed(unpack(slot, k, 8, 2 * HALO, rem), lanes_of(sign, 0))
        for t in range(2):
            for side in range(2):
                xc[side, k * HALO : (k + 1) * HALO, t * LANES : (t + 1) * LANES] = tiles[t][side * HALO : (side + 1) * HALO]
    copies = []
    for side in range(2):
        b, at = ((0, 0), (2, cols - HALO))[side]
        total = edge_sums(lambda a: xc[side], side_weights(wh, b), side_weights(wl, b), (2,))
        for k in range(8):
            ref, row = row_of((st3m, st3b), k)
            grown = jax.nn.gelu(accn[rows - 8 + k, at : at + HALO, :] + total[k * HALO : (k + 1) * HALO])
            for t in range(2):
                end[k, t] = ref[row, t, at : at + HALO, :] + grown[:, t * LANES : (t + 1) * LANES]
        put_out(done.at[side], 0, end, HALO, channels)
        copies.append(
            pltpu.make_async_copy(done.at[side], out.at[pl.ds(at, HALO), pl.ds(rows - 8, 8), :], sems.at[side])
        )
        copies[-1].start()
    for copy in copies:
        copy.wait()


VM = pl.BlockSpec(memory_space=pltpu.VMEM)
SM = pl.BlockSpec(memory_space=pltpu.SMEM)
HB = pl.BlockSpec(memory_space=pltpu.HBM)


def lhs(rows):
    return [pltpu.VMEM((rows, MW, 6 * LANES), BF16)] * 2


def call(kernel, outs, scratch, args, smem=0, flops=0, limit=16, hbm=(), alias=None):
    args = [pltpu.with_memory_space_constraint(a, pltpu.HBM) if i in hbm else a for i, a in enumerate(args)]
    moved = sum(a.size * a.dtype.itemsize for a in args[smem:])
    outs = [o if isinstance(o, jax.ShapeDtypeStruct) else jax.ShapeDtypeStruct(o, F32) for o in outs]
    return pl.pallas_call(
        kernel,
        out_shape=outs,
        in_specs=[SM if i < smem else HB if i in hbm else VM for i in range(len(args))],
        out_specs=[HB if alias else VM] * len(outs),
        input_output_aliases=alias or {},
        scratch_shapes=scratch,
        compiler_params=pltpu.CompilerParams(vmem_limit_bytes=limit * 2**20),
        cost_estimate=pl.CostEstimate(flops=flops, bytes_accessed=moved, transcendentals=0),
    )(*args)


def layers_of(field, south_rows, sign_mask, weights, biases):
    rows, cols, channels = field.shape
    south = south_rows.shape[0]
    layers = weights.shape[0]
    rem = channels - LANES - HALF
    devices = lax.axis_size("lon")
    mirror = [(i, devices - 1 - i) for i in range(devices)]
    intra = [(i, i ^ 1) for i in range(devices)]
    cross = [(i, (i + 1) % devices if i % 2 else (i - 1) % devices) for i in range(devices)]
    send = lambda x, route: lax.ppermute(x, "lon", route)
    par = (lax.axis_index("lon") % 2).astype(jnp.int32).reshape(1)
    sign = sign_mask.reshape(1, channels)
    field = jnp.swapaxes(field, 0, 1)
    south_rows = jnp.swapaxes(south_rows, 0, 1)
    row_flops = MW * 6 * LANES * 2 * LANES * 2 * 9
    tall = rows + south

    def state(n, width):
        return (n, 2, width, LANES)

    ew_rows = packed_rows(HALO, tall, rem)
    main, ewi, ewc = call(
        k_first,
        [(packed_rows(3, cols, rem), LANES), (ew_rows, LANES), (ew_rows, LANES)],
        [pltpu.VMEM(state(8, 56), F32), pltpu.VMEM((2, HALO, rows, channels), F32),
         pltpu.VMEM((2, HALO, south, channels), F32), pltpu.VMEM((cols, 8, channels), F32),
         pltpu.SemaphoreType.DMA((5,))],
        [par, field, south_rows], smem=1, hbm=(1, 2), limit=16,
    )
    ewi, ewc, main = send(ewi, intra), send(ewc, cross), send(main, mirror)
    split = call(
        k_weights,
        [jax.ShapeDtypeStruct((3, 6 * LANES, 2 * LANES), BF16)] * (2 * layers),
        [pltpu.VMEM(weights.shape, F32), pltpu.SemaphoreType.DMA((layers,))],
        [weights], limit=24, hbm=(0,),
    )
    (corner,) = call(
        functools.partial(k_corner, tall=tall, rows=rows, rem=rem),
        [(packed_rows(3, 2 * HALO, rem), LANES)], [pltpu.VMEM(state(8, 2 * HALO), F32)],
        [par, ewi, ewc], smem=1,
    )
    corner = send(corner, mirror)
    st1, se, x0 = call(
        k_a,
        [state(rows - 1, 72), state(south, 80), state(rows, 72)],
        lhs(rows + 1),
        [par, field, south_rows, ewi, ewc, *split[0:2], biases],
        smem=1, flops=15 * row_flops,
    )
    st2b, north = call(
        functools.partial(k_b, cols=cols, rem=rem),
        [state(4, 72), (packed_rows(4, cols + 8, rem), LANES)],
        [pltpu.VMEM(state(3, 72), F32), pltpu.VMEM(state(4, 72), F32), pltpu.VMEM(state(8, 72), F32)] + lhs(7) + lhs(8),
        [x0, main, corner, st1, sign, *split[0:4], biases],
        flops=7 * row_flops,
    )
    north = send(north, mirror)
    st2m, st3m, na = call(
        functools.partial(k_c1, cols=cols, rem=rem),
        [state(12, 72), state(4, MW), (packed_rows(4, cols, rem), LANES)],
        lhs(12) + lhs(12),
        [st1, st2b, *split[2:6], biases],
        flops=12 * row_flops,
    )
    na = send(na, mirror)
    (st3l,) = call(
        k_c2,
        [state(8, MW)],
        [pltpu.VMEM(state(8, 72), F32)] + lhs(8) + lhs(16),
        [st1, st2m, se, *split[2:6], biases],
        flops=12 * row_flops,
    )
    ew_rows = packed_rows(rows, HALO, rem)
    st3b, nb, ewi, ewc = call(
        functools.partial(k_d, cols=cols, rem=rem),
        [state(4, MW), (packed_rows(4, cols, rem), LANES), (ew_rows, LANES), (ew_rows, LANES)],
        [pltpu.VMEM(state(4, 72), F32)] + lhs(12),
        [par, st2m, north, st3l, st3m, sign, *split[4:6], biases],
        smem=1, flops=4 * row_flops,
    )
    ewi, ewc = send(ewi, intra), send(ewc, cross)
    nb = send(nb, mirror)
    (acc,) = call(
        functools.partial(k_f, cols=cols),
        [(rows, MW, 2 * LANES)],
        [pltpu.VMEM(state(rows + south, 80), F32)] + lhs(rows + south),
        [st3l, st3m, st3b, se, *split[6:8], biases],
        flops=(rows - 3) * row_flops,
    )
    ewi, ewc, acc = lax.optimization_barrier((ewi, ewc, acc))
    (nc,) = call(
        functools.partial(k_corner2, rows=rows, rem=rem),
        [(packed_rows(8, 2 * HALO, rem), LANES)], [], [par, ewi, ewc], smem=1,
    )
    nc = send(nc, mirror)
    out, acc = call(
        functools.partial(k_g, cols=cols, rem=rem),
        [(cols, rows, channels), (rows, MW, 2 * LANES)],
        [pltpu.VMEM(state(8, 80), F32), pltpu.VMEM((2, (rows + south + 8) * HALO, 2 * LANES), F32),
         pltpu.VMEM((2,) + state(8, MW), F32)] + lhs(8),
        [par, acc, st3l, st3m, st3b, se, ewi, ewc, na, nb, sign, *split[6:8]],
        smem=1, flops=4 * row_flops,
    )
    (out,) = call(
        functools.partial(k_h, cols=cols, rem=rem),
        [(cols, rows, channels)],
        [pltpu.VMEM((2, 8 * HALO, 2 * LANES), F32), pltpu.VMEM(state(8, HALO), F32),
         pltpu.VMEM((2, HALO, 8, channels), F32), pltpu.SemaphoreType.DMA((2,))],
        [out, acc, st3m, st3b, nc, sign, *split[6:8]],
        hbm=(0,), alias={0: 0}, flops=row_flops,
    )
    return jnp.swapaxes(out, 0, 1)


def solution(mesh):
    in_specs = (P(None, "lon", None), P(None, "lon", None), P(), P(), P())
    out_specs = P(None, "lon", None)
    return jax.shard_map(layers_of, mesh=mesh, in_specs=in_specs, out_specs=out_specs, check_vma=False)
```

```python
import functools

import jax
import jax.numpy as jnp
from jax import lax
from jax.experimental import pallas as pl
from jax.experimental.pallas import tpu as pltpu
from jax.sharding import PartitionSpec as P

F32 = jnp.float32
BF16 = jnp.bfloat16
LANES = 128
HALF = 64
MW = 64
HALO = 8


def merged(rows):
    return rows % 2 == 1 and rows <= 8


def rest_groups(rows, width, rem):
    groups = max(1, LANES // (rows * rem))
    return groups, width if groups == 1 else (-(-width // groups) + 7) // 8 * 8


def packed_rows(rows, width, rem):
    full = rows + (rows + 1) // 2
    return full * width + (0 if merged(rows) else rest_groups(rows, width, rem)[1])


def lane_of(width):
    return lax.broadcasted_iota(jnp.int32, (width, LANES), 1)


def roll(x, shift):
    shift = shift % LANES
    return x if shift == 0 else pltpu.roll(x, shift, 1)


def pack(get, put, rows, width, rem):
    lane = lane_of(width)
    halves = (rows + 1) // 2
    for k in range(rows):
        put(k, get(k, 0))
    second = [get(k, 1) for k in range(rows)]
    for p in range(halves):
        other = roll(second[2 * p + 1], HALF) if 2 * p + 1 < rows else jnp.zeros((width, LANES), F32)
        tile = jnp.where(lane < HALF, second[2 * p], other)
        if merged(rows) and p == halves - 1:
            for k in range(rows):
                at = HALF + rem * k
                tile = jnp.where((lane >= at) & (lane < at + rem), roll(second[k], rem * k), tile)
        put(rows + p, tile)
    if not merged(rows):
        tile = jnp.zeros((width, LANES), F32)
        for k in range(rows):
            tile = jnp.where((lane >= rem * k) & (lane < rem * k + rem), roll(second[k], rem * k - HALF), tile)
        groups, high = rest_groups(rows, width, rem)
        total = None
        for g in range(groups):
            part = tile[g * high : min(width, (g + 1) * high)]
            if part.shape[0] < high:
                part = jnp.concatenate([part, jnp.zeros((high - part.shape[0], LANES), F32)], axis=0)
            part = roll(part, g * rows * rem)
            total = part if total is None else total + part
        put(rows + halves, total)


def unpack(slot, k, rows, width, rem):
    lane = lane_of(width)
    halves = (rows + 1) // 2
    half = roll(slot(rows + k // 2), HALF * (k % 2))
    if merged(rows):
        rest = roll(slot(rows + halves - 1), -rem * k)
    else:
        rest = roll(slot(rows + halves), HALF - rem * k)
    tile = jnp.where(lane < HALF, half, jnp.where(lane < HALF + rem, rest, 0.0))
    return slot(k), tile


def slots_of(ref, rows, width, rem):
    full = rows + (rows + 1) // 2
    tiles = [ref[k * width : (k + 1) * width, :] for k in range(full)]
    if not merged(rows):
        groups, high = rest_groups(rows, width, rem)
        block = ref[full * width : full * width + high, :]
        parts = [roll(block, -g * rows * rem)[: min(high, width - g * high)] for g in range(groups)]
        tiles.append(parts[0] if groups == 1 else jnp.concatenate(parts, axis=0))
    return tiles


def putter(ref, width):
    def put(k, tile):
        ref[k * width : (k + 1) * width, :] = tile

    return put


def turned(tiles):
    order = 7 - lax.broadcasted_iota(jnp.int32, (8, LANES), 0)
    flip = lambda x: jnp.take_along_axis(x, order, axis=0)

    def one(x):
        parts, left = [], x.shape[0]
        while left >= 8:
            parts.append(flip(x[left - 8 : left]))
            left -= 8
        if left:
            parts.append(flip(x[0:8])[8 - left :])
        return jnp.concatenate(parts, axis=0)

    return [one(x) for x in tiles]


def fill_row(hi, lo, dst, ref, row, offs):
    for b in range(3):
        for t in range(2):
            x = ref[row, t, offs[b] : offs[b] + MW, :]
            h = x.astype(BF16)
            at = b * 2 * LANES + t * LANES
            hi[dst, :, at : at + LANES] = h
            lo[dst, :, at : at + LANES] = (x - h.astype(F32)).astype(BF16)


def fill(hi, lo, dst, ref, src, count, offs):
    for i in range(count):
        fill_row(hi, lo, dst + i, ref, src + i, offs)


def run(ref, first, count, offs):
    return [(ref, first + i, offs) for i in range(count)]


def products(hi, lo, wh, wl, taps, row, chunk, dilate):
    total = None
    for a in taps:
        at = slice(row + a * dilate, row + a * dilate + chunk)
        lh = hi[at].reshape(chunk * MW, hi.shape[-1])
        ll = lo[at].reshape(chunk * MW, hi.shape[-1])
        for left, right in ((lh, wh), (ll, wh), (lh, wl)):
            term = jnp.dot(left, right[a], preferred_element_type=F32)
            total = term if total is None else total + term
    return total


def conv(buffers, wh, wl, bias, dilate, sources, count, chunk, emit):
    hi, lo = buffers
    filled = 0
    for row in range(0, count, chunk):
        while filled < row + chunk + 2 * dilate:
            fill_row(hi, lo, filled, *sources[filled])
            filled += 1
        total = products(hi, lo, wh, wl, (0, 1, 2), row, chunk, dilate)
        emit(row, jax.nn.gelu(total + bias))


def add_rows(out, out_row, res, res_row, off, chunk):
    def emit(row, grown):
        for q in range(chunk):
            for t in range(2):
                out[out_row + row + q, t, 0:MW, :] = (
                    res[res_row + row + q, t, off : off + MW, :]
                    + grown[q * MW : (q + 1) * MW, t * LANES : (t + 1) * LANES]
                )

    return emit


def put_row(dst, row, at, tiles):
    for t in range(2):
        dst[row, t, at : at + tiles[t].shape[0], :] = tiles[t]


def widen(x):
    return jnp.concatenate([x, jnp.zeros(x.shape[:-1] + (LANES - x.shape[-1],), F32)], axis=-1)


def tile_at(ref, col, lo, hi, t):
    return ref[col, lo:hi, 0:LANES] if t == 0 else widen(ref[col, lo:hi, LANES : ref.shape[-1]])


def strided(dst, first, t, col):
    rows, _, width, _ = dst.shape
    return dst.reshape(rows * 2 * width, LANES), pl.ds((2 * first + t) * width + col, 8, stride=2 * width)


def put_column(dst, first, col, t, tile):
    flat, at = strided(dst, first, t, col)
    flat[at, :] = tile


def get_column(src, first, col, t):
    flat, at = strided(src, first, t, col)
    return flat[at, :]


def lanes_of(ref, row):
    x = ref[row : row + 1, :].astype(F32)
    return [x[:, 0:LANES], widen(x[:, LANES:])]


def bias_of(ref, row):
    return jnp.concatenate(lanes_of(ref, row), axis=1)


def k_first(par, field, south, main, ewi, ewc, top, fedge, sedge, last, sems):
    cols, rows, channels = field.shape
    rem = channels - LANES - HALF
    even = par[0] == 0
    sides = (pl.ds(0, HALO), pl.ds(cols - HALO, HALO))
    copies = [pltpu.make_async_copy(field.at[at], fedge.at[i], sems.at[i]) for i, at in enumerate(sides)]
    copies += [pltpu.make_async_copy(south.at[at], sedge.at[i], sems.at[2 + i]) for i, at in enumerate(sides)]
    copies += [pltpu.make_async_copy(field.at[:, pl.ds(rows - 8, 8), :], last, sems.at[4])]
    for copy in copies:
        copy.start()
    for copy in copies[:4]:
        copy.wait()

    def edge(flip):
        def get(k, t):
            pick = []
            for i in range(2):
                tiles = [tile_at(fedge.at[i], k, 0, rows, t), tile_at(sedge.at[i], k, 0, south.shape[1], t)]
                pick.append(jnp.concatenate(tiles, axis=0))
            return jnp.where(even != flip, pick[1], pick[0])

        return get

    tall = rows + south.shape[1]
    pack(edge(False), putter(ewi, tall), HALO, tall, rem)
    pack(edge(True), putter(ewc, tall), HALO, tall, rem)
    copies[4].wait()
    for col in range(cols):
        for t in range(2):
            put_column(top, 0, col, t, tile_at(last, col, 0, 8, t))
    pack(lambda k, t: top[7 - k, t, 0:cols, :], putter(main, cols), 3, cols, rem)


def k_weights(w, *refs):
    layers, _, channels, _ = w.shape
    outs, (buf, sems) = refs[: 2 * layers], refs[2 * layers :]
    copies = [pltpu.make_async_copy(w.at[i], buf.at[i], sems.at[i]) for i in range(layers)]
    for copy in copies:
        copy.start()
    for i in range(layers):
        wh, wl = outs[2 * i : 2 * i + 2]
        copies[i].wait()
        for k in range(9):
            x = buf[i, k]
            h = x.astype(BF16)
            at = (k % 3) * 2 * LANES
            for ref, value in ((wh, h), (wl, (x - h.astype(F32)).astype(BF16))):
                wide = jnp.concatenate([value, jnp.zeros((channels, 2 * LANES - channels), BF16)], axis=1)
                ref[k // 3, at : at + channels, :] = wide
                ref[k // 3, at + channels : at + 2 * LANES, :] = jnp.zeros((2 * LANES - channels, 2 * LANES), BF16)


def sided(par, ewi, ewc, rows, width, rem):
    even = par[0] == 0
    i, c = slots_of(ewi, rows, width, rem), slots_of(ewc, rows, width, rem)
    west = [jnp.where(even, y, x) for x, y in zip(i, c)]
    east = [jnp.where(even, x, y) for x, y in zip(i, c)]
    return west.__getitem__, east.__getitem__


def k_corner(par, ewi, ewc, out, top, *, tall, rows, rem):
    west, east = sided(par, ewi, ewc, HALO, tall, rem)
    for side, slot in enumerate((west, east)):
        for k in range(HALO):
            tiles = unpack(slot, k, HALO, tall, rem)
            for t in range(2):
                put_column(top, 0, side * HALO + k, t, tiles[t][rows - 8 : rows])
    pack(lambda k, t: top[7 - k, t], putter(out, 2 * HALO), 3, 2 * HALO, rem)


def k_corner2(par, ewi, ewc, out, *, rows, rem):
    west, east = sided(par, ewi, ewc, rows, HALO, rem)
    tiles = []
    for k in range(8):
        w = unpack(west, rows - 1 - k, rows, HALO, rem)
        e = unpack(east, rows - 1 - k, rows, HALO, rem)
        tiles.append([jnp.concatenate([w[t], e[t]], axis=0) for t in range(2)])
    pack(lambda k, t: tiles[k][t], putter(out, 2 * HALO), 8, 2 * HALO, rem)


def k_a(par, field, south, ewi, ewc, wh, wl, bias, st1, se, x0, *buffers):
    cols, rows, channels = field.shape
    rem = channels - LANES - HALF
    deep = south.shape[1]
    west, east = sided(par, ewi, ewc, HALO, rows + deep, rem)

    def put(col, tiles):
        for t in range(2):
            for h in range(0, rows, 8):
                put_column(x0, h, col, t, tiles[t][h : h + 8])
            put_column(se, 0, col, t, tiles[t][rows : rows + 8])

    for k in range(HALO):
        put(k, unpack(west, k, HALO, rows + deep, rem))
        put(HALO + cols + k, unpack(east, k, HALO, rows + deep, rem))
    for col in range(cols):
        for t in range(2):
            for h in range(0, rows, 8):
                put_column(x0, h, HALO + col, t, tile_at(field, col, h, h + 8, t))
            put_column(se, 0, HALO + col, t, tile_at(south, col, 0, 8, t))
    count = st1.shape[0]
    first = rows - 1 - count
    sources = run(x0, first - 1, count + 2, (1, 2, 3))
    conv(buffers, wh, wl, bias_of(bias, 0), 1, sources, count, 5, add_rows(st1, 0, x0, first, 2, 5))


def signed(tiles, sign):
    return tiles if sign is None else [tiles[t] * sign[t] for t in range(2)]


def north_rows(dst, dst_row, main, sign, count, width, left, rem):
    slot = turned(slots_of(main, count, width, rem)).__getitem__
    for k in range(count):
        put_row(dst, dst_row + k, left, signed(unpack(slot, k, count, width, rem), sign))


def north_corners(dst, dst_row, corner, sign, count, cols, left, rem):
    width = 2 * HALO
    slot = turned(slots_of(corner, count, width, rem)).__getitem__
    for k in range(count):
        t = signed(unpack(slot, k, count, width, rem), sign)
        put_row(dst, dst_row + k, left - HALO, [x[0:HALO] for x in t])
        put_row(dst, dst_row + k, left + cols, [x[HALO:] for x in t])


def k_b(edge, se, main, corner, st1, sign, wh0, wl0, wh1, wl1, bias, st2, out, low, x0, xr, x1, hi, lo, h1, l1, *buffers, cols, rem):
    rows = edge.shape[0]
    sign = lanes_of(sign, 0)
    north_rows(xr, 1, main, None, 3, cols, HALO, rem)
    north_corners(xr, 1, corner, None, 3, cols, HALO, rem)
    x0[0:2] = edge[rows - 2 :]
    for t in range(2):
        x0[2, t] = xr[1, t] * sign[t]
        xr[0, t] = edge[rows - 1, t] * sign[t]
    x1[0:5] = st1[st1.shape[0] - 5 :]
    offs = (1, 2, 3)
    fill(hi, lo, 0, x0, 0, 3, offs)
    fill(hi, lo, 3, xr, 0, 4, offs[::-1])
    total = None
    for a in range(3):
        both = [jnp.concatenate([x[a : a + 1], x[5 - a : 7 - a]]).reshape(3 * MW, x.shape[-1]) for x in (hi, lo)]
        for left, right in ((both[0], wh0), (both[1], wh0), (both[0], wl0)):
            term = jnp.dot(left, right[a], preferred_element_type=F32)
            total = term if total is None else total + term
    grown = jax.nn.gelu(total + bias_of(bias, 0))
    for q in range(3):
        for t in range(2):
            g = grown[q * MW : (q + 1) * MW, t * LANES : (t + 1) * LANES]
            if q == 0:
                x1[5, t, 0:MW, :] = x0[1, t, 2 : 2 + MW, :] + g
            else:
                x1[5 + q, t, 0:MW, :] = sign[t] * (xr[q, t, 2 : 2 + MW, :] + g)
    count = low.shape[0]
    sources = run(se, se.shape[0] - 1, 1, offs) + run(edge, 0, count + 1, offs)
    conv((h1, l1), wh0, wl0, bias_of(bias, 0), 1, sources, count, count, add_rows(low, 0, edge, 0, 2, count))
    conv(buffers, wh1, wl1, bias_of(bias, 1), 2, run(x1, 0, 8, (0, 2, 4)), 4, 4, add_rows(st2, 0, x1, 2, 2, 4))
    wide = cols + 8
    pack(lambda k, t: st2[3 - k, t, 0:wide, :], putter(out, wide), 4, wide, rem)


def k_c1(low, st1a, st2b, se, wh1, wl1, wh2, wl2, bias, st2, st3, st3l, out, st1, h0, l0, h1, l1, h2, l2, *, cols, rem):
    south = se.shape[0]
    done = low.shape[0]
    st1[0:done] = low[...]
    st1[done:] = st1a[...]
    bias1 = bias_of(bias, 1)
    conv((h1, l1), wh1, wl1, bias1, 2, run(st1, 2, 12, (0, 2, 4)), 8, 4, add_rows(st2, 4, st1, 4, 2, 4))
    sources = run(se, south - 2, 2, (2, 4, 6)) + run(st1, 0, 6, (0, 2, 4))
    conv((h0, l0), wh1, wl1, bias1, 2, sources, 4, 4, add_rows(st2, 0, st1, 0, 2, 4))
    st2[12:16] = st2b[...]
    bias2 = bias_of(bias, 2)
    sources = run(se, south - 4, 4, (4, 8, 12)) + run(st2, 0, 16, (0, 4, 8))
    for i in range(8, 20):
        fill_row(h2, l2, i, *sources[i])
    for row in (8, 0, 4):
        for i in range(8 if row == 0 else 0):
            fill_row(h2, l2, i, *sources[i])
        total = products(h2, l2, wh2, wl2, (0, 1, 2), row, 4, 4)
        emit = add_rows(st3, -8, st2, 0, 4, 4) if row == 8 else add_rows(st3l, 0, st2, 0, 4, 4)
        emit(row, jax.nn.gelu(total + bias2))
        if row == 8:
            pack(lambda k, t: st3[3 - k, t, 0:cols, :], putter(out, cols), 4, cols, rem)


def row_of(parts, row):
    for part in parts:
        if row < part.shape[0]:
            return part, row
        row -= part.shape[0]


def k_d(par, st2, north, st3l, st3m, sign, wh, wl, bias, st3b, out, ewi, ewc, x2, hi, lo, *, cols, rem):
    wide = cols + 8
    north_rows(x2, 0, north, lanes_of(sign, 0), 4, wide, 0, rem)
    sources = run(st2, 8, 8, (0, 4, 8)) + run(x2, 0, 4, (0, 4, 8))
    conv((hi, lo), wh, wl, bias_of(bias, 2), 4, sources, 4, 4, add_rows(st3b, 0, st2, 12, 4, 4))
    pack(lambda k, t: st3b[3 - k, t, 0:cols, :], putter(out, cols), 4, cols, rem)
    even = par[0] == 0
    parts = (st3l, st3m, st3b)
    rows = sum(x.shape[0] for x in parts)

    def edge(flip):
        def get(k, t):
            ref, row = row_of(parts, k)
            west, east = ref[row, t, 0:HALO, :], ref[row, t, cols - HALO : cols, :]
            return jnp.where(even != flip, east, west)

        return get

    pack(edge(False), putter(ewi, HALO), rows, HALO, rem)
    pack(edge(True), putter(ewc, HALO), rows, HALO, rem)


def put_out(out, first, src, cols, channels):
    for col in range(cols):
        out[col, first : first + 8, 0:LANES] = get_column(src, 0, col, 0)
        out[col, first : first + 8, LANES:channels] = get_column(src, 0, col, 1)[:, 0 : channels - LANES]


def k_f(st3l, st3m, st3b, se, wh, wl, bias, acc, top, x3, hi, lo, *, cols):
    low, south = acc.shape[0], se.shape[0]
    rows = low + top.shape[0]
    zero = jnp.zeros((2, HALO, LANES), F32)
    for k in range(rows + south):
        ref, row = (se, k) if k < south else row_of((st3l, st3m, st3b), k - south)
        x3[k, :, 0:HALO, :] = zero
        at = HALO if k < south else 0
        x3[k, :, HALO : HALO + cols, :] = ref[row, :, at : at + cols, :]
        x3[k, :, HALO + cols : 2 * HALO + cols, :] = zero
    bias = bias_of(bias, 3)
    filled = 0
    for row in range(0, rows, 4):
        taps = (0, 1, 2) if row < low else (0, 1)
        while filled < row + 4 + 8 * taps[-1]:
            fill_row(hi, lo, filled, x3, filled, (0, 8, 16))
            filled += 1
        total = products(hi, lo, wh, wl, taps, row, 4, 8)
        ref, at = (acc, row) if row < low else (top, row - low)
        ref[at : at + 4] = (total + bias).reshape(4, MW, 2 * LANES)


def split_bf16(x):
    h = x.astype(BF16)
    return h, (x - h.astype(F32)).astype(BF16)


def edge_sums(tiles_of, wh, wl, taps):
    total = None
    for a in taps:
        h, l = split_bf16(tiles_of(a))
        for left, right in ((h, wh), (l, wh), (h, wl)):
            term = jnp.dot(left, right(a), preferred_element_type=F32)
            total = term if total is None else total + term
    return total


def side_weights(ref, b):
    at = b * 2 * LANES
    return lambda a: ref[a, at : at + 2 * LANES, :]


def k_g(par, acc1, acc, st3l, st3m, st3b, se, ewi, ewc, na, nb, sign, wh, wl, out, accn, xn, halo, end, hi, lo, *, cols, rem):
    rows = accn.shape[0]
    channels = out.shape[-1]
    south = se.shape[0]
    sign = lanes_of(sign, 0)
    zero = jnp.zeros((8, 2, HALO, LANES), F32)
    xn[:, :, 0:HALO, :] = zero
    xn[:, :, HALO + cols : 2 * HALO + cols, :] = zero
    north_rows(xn, 0, nb, sign, 4, cols, HALO, rem)
    north_rows(xn, 4, na, sign, 4, cols, HALO, rem)
    fill(hi, lo, 0, xn, 0, 8, (0, 8, 16))
    accn[0 : rows - 8] = acc1[...]
    for i in range(2):
        at = slice(4 * i, 4 * i + 4)
        lh = hi[at].reshape(4 * MW, hi.shape[-1])
        ll = lo[at].reshape(4 * MW, hi.shape[-1])
        total = acc[4 * i : 4 * i + 4].reshape(4 * MW, 2 * LANES)
        for left, right in ((lh, wh), (ll, wh), (lh, wl)):
            total = total + jnp.dot(left, right[2], preferred_element_type=F32)
        accn[rows - 8 + 4 * i : rows - 4 + 4 * i] = total.reshape(4, MW, 2 * LANES)
    for side, slot in enumerate(sided(par, ewi, ewc, rows, HALO, rem)):
        b, to = ((0, 0), (2, cols - HALO))[side]
        at = side * (HALO + cols)
        for k in range(south):
            for t in range(2):
                halo[side, k * HALO : (k + 1) * HALO, t * LANES : (t + 1) * LANES] = se[k, t, at : at + HALO, :]
        for k in range(rows):
            tiles = unpack(slot, k, rows, HALO, rem)
            for t in range(2):
                halo[side, (south + k) * HALO : (south + k + 1) * HALO, t * LANES : (t + 1) * LANES] = tiles[t]
        halo[side, (south + rows) * HALO :, :] = jnp.zeros((8 * HALO, 2 * LANES), F32)
        total = edge_sums(
            lambda a: halo[side, 8 * a * HALO : (8 * a + rows) * HALO, :],
            side_weights(wh, b), side_weights(wl, b), (0, 1, 2),
        )
        for k in range(rows):
            accn[k, to : to + HALO, :] += total[k * HALO : (k + 1) * HALO]
    for half in range(0, rows, 8):
        for k in range(8):
            grown = jax.nn.gelu(accn[half + k])
            ref, row = row_of((st3l, st3m, st3b), half + k)
            for t in range(2):
                end[half // 8, k, t] = ref[row, t] + grown[:, t * LANES : (t + 1) * LANES]
        put_out(out, half, end.at[half // 8], cols, channels)


def k_h(before, accn, st3m, st3b, nc, sign, wh, wl, out, xc, end, done, sems, *, cols, rem):
    rows = accn.shape[0]
    channels = out.shape[-1]
    slot = turned(slots_of(nc, 8, 2 * HALO, rem)).__getitem__
    for k in range(8):
        tiles = signed(unpack(slot, k, 8, 2 * HALO, rem), lanes_of(sign, 0))
        for t in range(2):
            for side in range(2):
                xc[side, k * HALO : (k + 1) * HALO, t * LANES : (t + 1) * LANES] = tiles[t][side * HALO : (side + 1) * HALO]
    copies = []
    for side in range(2):
        b, at = ((0, 0), (2, cols - HALO))[side]
        total = edge_sums(lambda a: xc[side], side_weights(wh, b), side_weights(wl, b), (2,))
        for k in range(8):
            ref, row = row_of((st3m, st3b), k)
            grown = jax.nn.gelu(accn[rows - 8 + k, at : at + HALO, :] + total[k * HALO : (k + 1) * HALO])
            for t in range(2):
                end[k, t] = ref[row, t, at : at + HALO, :] + grown[:, t * LANES : (t + 1) * LANES]
        put_out(done.at[side], 0, end, HALO, channels)
        copies.append(
            pltpu.make_async_copy(done.at[side], out.at[pl.ds(at, HALO), pl.ds(rows - 8, 8), :], sems.at[side])
        )
        copies[-1].start()
    for copy in copies:
        copy.wait()


VM = pl.BlockSpec(memory_space=pltpu.VMEM)
SM = pl.BlockSpec(memory_space=pltpu.SMEM)
HB = pl.BlockSpec(memory_space=pltpu.HBM)


def lhs(rows):
    return [pltpu.VMEM((rows, MW, 6 * LANES), BF16)] * 2


def call(kernel, outs, scratch, args, smem=0, flops=0, limit=16, hbm=(), alias=None):
    args = [pltpu.with_memory_space_constraint(a, pltpu.HBM) if i in hbm else a for i, a in enumerate(args)]
    moved = sum(a.size * a.dtype.itemsize for a in args[smem:])
    outs = [o if isinstance(o, jax.ShapeDtypeStruct) else jax.ShapeDtypeStruct(o, F32) for o in outs]
    return pl.pallas_call(
        kernel,
        out_shape=outs,
        in_specs=[SM if i < smem else HB if i in hbm else VM for i in range(len(args))],
        out_specs=[HB if alias else VM] * len(outs),
        input_output_aliases=alias or {},
        scratch_shapes=scratch,
        compiler_params=pltpu.CompilerParams(vmem_limit_bytes=limit * 2**20),
        cost_estimate=pl.CostEstimate(flops=flops, bytes_accessed=moved, transcendentals=0),
    )(*args)


def layers_of(field, south_rows, sign_mask, weights, biases):
    rows, cols, channels = field.shape
    south = south_rows.shape[0]
    layers = weights.shape[0]
    rem = channels - LANES - HALF
    devices = lax.axis_size("lon")
    mirror = [(i, devices - 1 - i) for i in range(devices)]
    intra = [(i, i ^ 1) for i in range(devices)]
    cross = [(i, (i + 1) % devices if i % 2 else (i - 1) % devices) for i in range(devices)]
    send = lambda x, route: lax.ppermute(x, "lon", route)
    par = (lax.axis_index("lon") % 2).astype(jnp.int32).reshape(1)
    sign = sign_mask.reshape(1, channels)
    field = jnp.swapaxes(field, 0, 1)
    south_rows = jnp.swapaxes(south_rows, 0, 1)
    row_flops = MW * 6 * LANES * 2 * LANES * 2 * 9
    tall = rows + south

    def state(n, width):
        return (n, 2, width, LANES)

    ew_rows = packed_rows(HALO, tall, rem)
    main, ewi, ewc = call(
        k_first,
        [(packed_rows(3, cols, rem), LANES), (ew_rows, LANES), (ew_rows, LANES)],
        [pltpu.VMEM(state(8, 56), F32), pltpu.VMEM((2, HALO, rows, channels), F32),
         pltpu.VMEM((2, HALO, south, channels), F32), pltpu.VMEM((cols, 8, channels), F32),
         pltpu.SemaphoreType.DMA((5,))],
        [par, field, south_rows], smem=1, hbm=(1, 2), limit=16,
    )
    ewi, ewc, main = send(ewi, intra), send(ewc, cross), send(main, mirror)
    split = call(
        k_weights,
        [jax.ShapeDtypeStruct((3, 6 * LANES, 2 * LANES), BF16)] * (2 * layers),
        [pltpu.VMEM(weights.shape, F32), pltpu.SemaphoreType.DMA((layers,))],
        [weights], limit=24, hbm=(0,),
    )
    (corner,) = call(
        functools.partial(k_corner, tall=tall, rows=rows, rem=rem),
        [(packed_rows(3, 2 * HALO, rem), LANES)], [pltpu.VMEM(state(8, 2 * HALO), F32)],
        [par, ewi, ewc], smem=1,
    )
    corner = send(corner, mirror)
    st1, se, x0 = call(
        k_a,
        [state(rows - 6, 72), state(south, 80), state(rows, 72)],
        lhs(rows - 4),
        [par, field, south_rows, ewi, ewc, *split[0:2], biases],
        smem=1, flops=10 * row_flops,
    )
    st2b, north, low = call(
        functools.partial(k_b, cols=cols, rem=rem),
        [state(4, 72), (packed_rows(4, cols + 8, rem), LANES), state(5, 72)],
        [pltpu.VMEM(state(3, 72), F32), pltpu.VMEM(state(4, 72), F32), pltpu.VMEM(state(8, 72), F32)] + lhs(7) + lhs(7) + lhs(8),
        [x0, se, main, corner, st1, sign, *split[0:4], biases],
        flops=12 * row_flops,
    )
    north = send(north, mirror)
    st2m, st3m, st3l, na = call(
        functools.partial(k_c1, cols=cols, rem=rem),
        [state(rows, 72), state(4, MW), state(8, MW), (packed_rows(4, cols, rem), LANES)],
        [pltpu.VMEM(state(rows - 1, 72), F32)] + lhs(8) + lhs(12) + lhs(rows + 4),
        [low, st1, st2b, se, *split[2:6], biases],
        flops=24 * row_flops,
    )
    na = send(na, mirror)
    ew_rows = packed_rows(rows, HALO, rem)
    st3b, nb, ewi, ewc = call(
        functools.partial(k_d, cols=cols, rem=rem),
        [state(4, MW), (packed_rows(4, cols, rem), LANES), (ew_rows, LANES), (ew_rows, LANES)],
        [pltpu.VMEM(state(4, 72), F32)] + lhs(12),
        [par, st2m, north, st3l, st3m, sign, *split[4:6], biases],
        smem=1, flops=4 * row_flops,
    )
    ewi, ewc = send(ewi, intra), send(ewc, cross)
    nb = send(nb, mirror)
    acc, acc2 = call(
        functools.partial(k_f, cols=cols),
        [(rows - 8, MW, 2 * LANES), (8, MW, 2 * LANES)],
        [pltpu.VMEM(state(rows + south, 80), F32)] + lhs(rows + south),
        [st3l, st3m, st3b, se, *split[6:8], biases],
        flops=(rows - 3) * row_flops,
    )
    ewi, ewc, acc, acc2 = lax.optimization_barrier((ewi, ewc, acc, acc2))
    (nc,) = call(
        functools.partial(k_corner2, rows=rows, rem=rem),
        [(packed_rows(8, 2 * HALO, rem), LANES)], [], [par, ewi, ewc], smem=1,
    )
    nc = send(nc, mirror)
    out, acc = call(
        functools.partial(k_g, cols=cols, rem=rem),
        [(cols, rows, channels), (rows, MW, 2 * LANES)],
        [pltpu.VMEM(state(8, 80), F32), pltpu.VMEM((2, (rows + south + 8) * HALO, 2 * LANES), F32),
         pltpu.VMEM((2,) + state(8, MW), F32)] + lhs(8),
        [par, acc, acc2, st3l, st3m, st3b, se, ewi, ewc, na, nb, sign, *split[6:8]],
        smem=1, flops=4 * row_flops,
    )
    (out,) = call(
        functools.partial(k_h, cols=cols, rem=rem),
        [(cols, rows, channels)],
        [pltpu.VMEM((2, 8 * HALO, 2 * LANES), F32), pltpu.VMEM(state(8, HALO), F32),
         pltpu.VMEM((2, HALO, 8, channels), F32), pltpu.SemaphoreType.DMA((2,))],
        [out, acc, st3m, st3b, nc, sign, *split[6:8]],
        hbm=(0,), alias={0: 0}, flops=row_flops,
    )
    return jnp.swapaxes(out, 0, 1)


def solution(mesh):
    in_specs = (P(None, "lon", None), P(None, "lon", None), P(), P(), P())
    out_specs = P(None, "lon", None)
    return jax.shard_map(layers_of, mesh=mesh, in_specs=in_specs, out_specs=out_specs, check_vma=False)
```

```python
import functools

import jax
import jax.numpy as jnp
from jax import lax
from jax.experimental import pallas as pl
from jax.experimental.pallas import tpu as pltpu
from jax.sharding import PartitionSpec as P

F32 = jnp.float32
BF16 = jnp.bfloat16
LANES = 128
HALF = 64
MW = 64
NW = 56
HALO = 8


def merged(rows):
    return rows % 2 == 1 and rows <= 8


def rest_groups(rows, width, rem):
    groups = max(1, LANES // (rows * rem))
    return groups, width if groups == 1 else (-(-width // groups) + 7) // 8 * 8


def packed_rows(rows, width, rem):
    full = rows + (rows + 1) // 2
    return full * width + (0 if merged(rows) else rest_groups(rows, width, rem)[1])


def lane_of(width):
    return lax.broadcasted_iota(jnp.int32, (width, LANES), 1)


def roll(x, shift):
    shift = shift % LANES
    return x if shift == 0 else pltpu.roll(x, shift, 1)


def pack(get, put, rows, width, rem):
    lane = lane_of(width)
    halves = (rows + 1) // 2
    for k in range(rows):
        put(k, get(k, 0))
    second = [get(k, 1) for k in range(rows)]
    for p in range(halves):
        other = roll(second[2 * p + 1], HALF) if 2 * p + 1 < rows else jnp.zeros((width, LANES), F32)
        tile = jnp.where(lane < HALF, second[2 * p], other)
        if merged(rows) and p == halves - 1:
            for k in range(rows):
                at = HALF + rem * k
                tile = jnp.where((lane >= at) & (lane < at + rem), roll(second[k], rem * k), tile)
        put(rows + p, tile)
    if not merged(rows):
        tile = jnp.zeros((width, LANES), F32)
        for k in range(rows):
            tile = jnp.where((lane >= rem * k) & (lane < rem * k + rem), roll(second[k], rem * k - HALF), tile)
        groups, high = rest_groups(rows, width, rem)
        total = None
        for g in range(groups):
            part = tile[g * high : min(width, (g + 1) * high)]
            if part.shape[0] < high:
                part = jnp.concatenate([part, jnp.zeros((high - part.shape[0], LANES), F32)], axis=0)
            part = roll(part, g * rows * rem)
            total = part if total is None else total + part
        put(rows + halves, total)


def unpack(slot, k, rows, width, rem):
    lane = lane_of(width)
    halves = (rows + 1) // 2
    half = roll(slot(rows + k // 2), HALF * (k % 2))
    if merged(rows):
        rest = roll(slot(rows + halves - 1), -rem * k)
    else:
        rest = roll(slot(rows + halves), HALF - rem * k)
    tile = jnp.where(lane < HALF, half, jnp.where(lane < HALF + rem, rest, 0.0))
    return slot(k), tile


def slots_of(ref, rows, width, rem):
    full = rows + (rows + 1) // 2
    tiles = [ref[k * width : (k + 1) * width, :] for k in range(full)]
    if not merged(rows):
        groups, high = rest_groups(rows, width, rem)
        block = ref[full * width : full * width + high, :]
        parts = [roll(block, -g * rows * rem)[: min(high, width - g * high)] for g in range(groups)]
        tiles.append(parts[0] if groups == 1 else jnp.concatenate(parts, axis=0))
    return tiles


def putter(ref, width):
    def put(k, tile):
        ref[k * width : (k + 1) * width, :] = tile

    return put


def turned(tiles):
    order = 7 - lax.broadcasted_iota(jnp.int32, (8, LANES), 0)
    flip = lambda x: jnp.take_along_axis(x, order, axis=0)

    def one(x):
        parts, left = [], x.shape[0]
        while left >= 8:
            parts.append(flip(x[left - 8 : left]))
            left -= 8
        if left:
            parts.append(flip(x[0:8])[8 - left :])
        return jnp.concatenate(parts, axis=0)

    return [one(x) for x in tiles]


def fill_row(hi, lo, dst, ref, row, offs):
    for b in range(3):
        for t in range(2):
            x = ref[row, t, offs[b] : offs[b] + MW, :]
            h = x.astype(BF16)
            at = b * 2 * LANES + t * LANES
            hi[dst, :, at : at + LANES] = h
            lo[dst, :, at : at + LANES] = (x - h.astype(F32)).astype(BF16)


def fill_pair(hi, lo, dst, sources, at):
    place = slice(dst * NW, (dst + 2) * NW)
    for b in range(3):
        for t in range(2):
            x = jnp.concatenate(
                [ref[row, t, offs[b] : offs[b] + NW, :] for ref, row, offs in sources[at : at + 2]], axis=0
            )
            h = x.astype(BF16)
            to = b * 2 * LANES + t * LANES
            hi[place, to : to + LANES] = h
            lo[place, to : to + LANES] = (x - h.astype(F32)).astype(BF16)


def narrow(hi, lo, wh, wl, taps, row, chunk, dilate):
    total = None
    for a in taps:
        at = slice((row + a * dilate) * NW, (row + a * dilate + chunk) * NW)
        lh, ll = hi[at], lo[at]
        for left, right in ((lh, wh), (ll, wh), (lh, wl)):
            term = jnp.dot(left, right[a], preferred_element_type=F32)
            total = term if total is None else total + term
    return total


def fill(hi, lo, dst, ref, src, count, offs):
    for i in range(count):
        fill_row(hi, lo, dst + i, ref, src + i, offs)


def run(ref, first, count, offs):
    return [(ref, first + i, offs) for i in range(count)]


def products(hi, lo, wh, wl, taps, row, chunk, dilate):
    total = None
    for a in taps:
        at = slice(row + a * dilate, row + a * dilate + chunk)
        lh = hi[at].reshape(chunk * MW, hi.shape[-1])
        ll = lo[at].reshape(chunk * MW, hi.shape[-1])
        for left, right in ((lh, wh), (ll, wh), (lh, wl)):
            term = jnp.dot(left, right[a], preferred_element_type=F32)
            total = term if total is None else total + term
    return total


def conv(buffers, wh, wl, bias, dilate, sources, count, chunk, emit):
    hi, lo = buffers
    filled = 0
    for row in range(0, count, chunk):
        while filled < row + chunk + 2 * dilate:
            fill_row(hi, lo, filled, *sources[filled])
            filled += 1
        total = products(hi, lo, wh, wl, (0, 1, 2), row, chunk, dilate)
        emit(row, jax.nn.gelu(total + bias))


def add_rows(out, out_row, res, res_row, off, chunk, width=MW):
    def emit(row, grown):
        for q in range(chunk):
            for t in range(2):
                out[out_row + row + q, t, 0:width, :] = (
                    res[res_row + row + q, t, off : off + width, :]
                    + grown[q * width : (q + 1) * width, t * LANES : (t + 1) * LANES]
                )

    return emit


def put_row(dst, row, at, tiles):
    for t in range(2):
        dst[row, t, at : at + tiles[t].shape[0], :] = tiles[t]


def widen(x):
    return jnp.concatenate([x, jnp.zeros(x.shape[:-1] + (LANES - x.shape[-1],), F32)], axis=-1)


def tile_at(ref, col, lo, hi, t):
    return ref[col, lo:hi, 0:LANES] if t == 0 else widen(ref[col, lo:hi, LANES : ref.shape[-1]])


def strided(dst, first, t, col):
    rows, _, width, _ = dst.shape
    return dst.reshape(rows * 2 * width, LANES), pl.ds((2 * first + t) * width + col, 8, stride=2 * width)


def put_column(dst, first, col, t, tile):
    flat, at = strided(dst, first, t, col)
    flat[at, :] = tile


def get_column(src, first, col, t):
    flat, at = strided(src, first, t, col)
    return flat[at, :]


def lanes_of(ref, row):
    x = ref[row : row + 1, :].astype(F32)
    return [x[:, 0:LANES], widen(x[:, LANES:])]


def bias_of(ref, row):
    return jnp.concatenate(lanes_of(ref, row), axis=1)


def k_first(par, field, south, main, ewi, ewc, top, fedge, sedge, last, sems):
    cols, rows, channels = field.shape
    rem = channels - LANES - HALF
    even = par[0] == 0
    sides = (pl.ds(0, HALO), pl.ds(cols - HALO, HALO))
    copies = [pltpu.make_async_copy(field.at[at], fedge.at[i], sems.at[i]) for i, at in enumerate(sides)]
    copies += [pltpu.make_async_copy(south.at[at], sedge.at[i], sems.at[2 + i]) for i, at in enumerate(sides)]
    copies += [pltpu.make_async_copy(field.at[:, pl.ds(rows - 8, 8), :], last, sems.at[4])]
    for copy in copies:
        copy.start()
    for copy in copies[:4]:
        copy.wait()

    def edge(flip):
        def get(k, t):
            pick = []
            for i in range(2):
                tiles = [tile_at(fedge.at[i], k, 0, rows, t), tile_at(sedge.at[i], k, 0, south.shape[1], t)]
                pick.append(jnp.concatenate(tiles, axis=0))
            return jnp.where(even != flip, pick[1], pick[0])

        return get

    tall = rows + south.shape[1]
    pack(edge(False), putter(ewi, tall), HALO, tall, rem)
    pack(edge(True), putter(ewc, tall), HALO, tall, rem)
    copies[4].wait()
    for col in range(cols):
        for t in range(2):
            put_column(top, 0, col, t, tile_at(last, col, 0, 8, t))
    pack(lambda k, t: top[7 - k, t, 0:cols, :], putter(main, cols), 3, cols, rem)


def k_weights(w, *refs):
    layers, _, channels, _ = w.shape
    outs, (buf, sems) = refs[: 2 * layers], refs[2 * layers :]
    copies = [pltpu.make_async_copy(w.at[i], buf.at[i], sems.at[i]) for i in range(layers)]
    for copy in copies:
        copy.start()
    for i in range(layers):
        wh, wl = outs[2 * i : 2 * i + 2]
        copies[i].wait()
        for k in range(9):
            x = buf[i, k]
            h = x.astype(BF16)
            at = (k % 3) * 2 * LANES
            for ref, value in ((wh, h), (wl, (x - h.astype(F32)).astype(BF16))):
                wide = jnp.concatenate([value, jnp.zeros((channels, 2 * LANES - channels), BF16)], axis=1)
                ref[k // 3, at : at + channels, :] = wide
                ref[k // 3, at + channels : at + 2 * LANES, :] = jnp.zeros((2 * LANES - channels, 2 * LANES), BF16)


def sided(par, ewi, ewc, rows, width, rem):
    even = par[0] == 0
    i, c = slots_of(ewi, rows, width, rem), slots_of(ewc, rows, width, rem)
    west = [jnp.where(even, y, x) for x, y in zip(i, c)]
    east = [jnp.where(even, x, y) for x, y in zip(i, c)]
    return west.__getitem__, east.__getitem__


def k_corner(par, ewi, ewc, out, top, *, tall, rows, rem):
    west, east = sided(par, ewi, ewc, HALO, tall, rem)
    for side, slot in enumerate((west, east)):
        for k in range(HALO):
            tiles = unpack(slot, k, HALO, tall, rem)
            for t in range(2):
                put_column(top, 0, side * HALO + k, t, tiles[t][rows - 8 : rows])
    pack(lambda k, t: top[7 - k, t], putter(out, 2 * HALO), 3, 2 * HALO, rem)


def k_corner2(par, ewi, ewc, out, *, rows, rem):
    west, east = sided(par, ewi, ewc, rows, HALO, rem)
    tiles = []
    for k in range(8):
        w = unpack(west, rows - 1 - k, rows, HALO, rem)
        e = unpack(east, rows - 1 - k, rows, HALO, rem)
        tiles.append([jnp.concatenate([w[t], e[t]], axis=0) for t in range(2)])
    pack(lambda k, t: tiles[k][t], putter(out, 2 * HALO), 8, 2 * HALO, rem)


def k_a(par, field, south, ewi, ewc, wh, wl, bias, st1, se, x0, *buffers):
    cols, rows, channels = field.shape
    rem = channels - LANES - HALF
    deep = south.shape[1]
    west, east = sided(par, ewi, ewc, HALO, rows + deep, rem)

    def put(col, tiles):
        for t in range(2):
            for h in range(0, rows, 8):
                put_column(x0, h, col, t, tiles[t][h : h + 8])
            put_column(se, 0, col, t, tiles[t][rows : rows + 8])

    for k in range(HALO):
        put(k, unpack(west, k, HALO, rows + deep, rem))
        put(HALO + cols + k, unpack(east, k, HALO, rows + deep, rem))
    for col in range(cols):
        for t in range(2):
            for h in range(0, rows, 8):
                put_column(x0, h, HALO + col, t, tile_at(field, col, h, h + 8, t))
            put_column(se, 0, HALO + col, t, tile_at(south, col, 0, 8, t))
    count = st1.shape[0]
    first = rows - 1 - count
    sources = run(x0, first - 1, count + 2, (1, 2, 3))
    conv(buffers, wh, wl, bias_of(bias, 0), 1, sources, count, 5, add_rows(st1, 0, x0, first, 2, 5))


def signed(tiles, sign):
    return tiles if sign is None else [tiles[t] * sign[t] for t in range(2)]


def north_rows(dst, dst_row, main, sign, count, width, left, rem):
    slot = turned(slots_of(main, count, width, rem)).__getitem__
    for k in range(count):
        put_row(dst, dst_row + k, left, signed(unpack(slot, k, count, width, rem), sign))


def north_corners(dst, dst_row, corner, sign, count, cols, left, rem):
    width = 2 * HALO
    slot = turned(slots_of(corner, count, width, rem)).__getitem__
    for k in range(count):
        t = signed(unpack(slot, k, count, width, rem), sign)
        put_row(dst, dst_row + k, left - HALO, [x[0:HALO] for x in t])
        put_row(dst, dst_row + k, left + cols, [x[HALO:] for x in t])


def k_b(edge, se, main, corner, st1, sign, wh0, wl0, wh1, wl1, bias, st2, out, low, x0, xr, x1, hi, lo, h1, l1, *buffers, cols, rem):
    rows = edge.shape[0]
    sign = lanes_of(sign, 0)
    north_rows(xr, 1, main, None, 3, cols, HALO, rem)
    north_corners(xr, 1, corner, None, 3, cols, HALO, rem)
    x0[0:2] = edge[rows - 2 :]
    for t in range(2):
        x0[2, t] = xr[1, t] * sign[t]
        xr[0, t] = edge[rows - 1, t] * sign[t]
    x1[0:5] = st1[st1.shape[0] - 5 :]
    offs = (1, 2, 3)
    fill(hi, lo, 0, x0, 0, 3, offs)
    fill(hi, lo, 3, xr, 0, 4, offs[::-1])
    total = None
    for a in range(3):
        both = [jnp.concatenate([x[a : a + 1], x[5 - a : 7 - a]]).reshape(3 * MW, x.shape[-1]) for x in (hi, lo)]
        for left, right in ((both[0], wh0), (both[1], wh0), (both[0], wl0)):
            term = jnp.dot(left, right[a], preferred_element_type=F32)
            total = term if total is None else total + term
    grown = jax.nn.gelu(total + bias_of(bias, 0))
    for q in range(3):
        for t in range(2):
            g = grown[q * MW : (q + 1) * MW, t * LANES : (t + 1) * LANES]
            if q == 0:
                x1[5, t, 0:MW, :] = x0[1, t, 2 : 2 + MW, :] + g
            else:
                x1[5 + q, t, 0:MW, :] = sign[t] * (xr[q, t, 2 : 2 + MW, :] + g)
    count = low.shape[0]
    sources = run(se, se.shape[0] - 1, 1, offs) + run(edge, 0, count + 1, offs)
    conv((h1, l1), wh0, wl0, bias_of(bias, 0), 1, sources, count, count, add_rows(low, 0, edge, 0, 2, count))
    conv(buffers, wh1, wl1, bias_of(bias, 1), 2, run(x1, 0, 8, (0, 2, 4)), 4, 4, add_rows(st2, 0, x1, 2, 2, 4))
    wide = cols + 8
    pack(lambda k, t: st2[3 - k, t, 0:wide, :], putter(out, wide), 4, wide, rem)


def k_c1(low, st1a, st2b, se, wh1, wl1, wh2, wl2, bias, st2, st3, st3l, out, st1, h0, l0, h1, l1, h2, l2, *, cols, rem):
    south = se.shape[0]
    done = low.shape[0]
    st1[0:done] = low[...]
    st1[done:] = st1a[...]
    bias1 = bias_of(bias, 1)
    conv((h1, l1), wh1, wl1, bias1, 2, run(st1, 2, 12, (0, 2, 4)), 8, 4, add_rows(st2, 4, st1, 4, 2, 4))
    sources = run(se, south - 2, 2, (2, 4, 6)) + run(st1, 0, 6, (0, 2, 4))
    conv((h0, l0), wh1, wl1, bias1, 2, sources, 4, 4, add_rows(st2, 0, st1, 0, 2, 4))
    st2[12:16] = st2b[...]
    bias2 = bias_of(bias, 2)
    sources = run(se, south - 4, 4, (4, 8, 12)) + run(st2, 0, 16, (0, 4, 8))
    for i in range(8, 20, 2):
        fill_pair(h2, l2, i, sources, i)
    for row in (8, 0, 4):
        for i in range(0, 8 if row == 0 else 0, 2):
            fill_pair(h2, l2, i, sources, i)
        total = narrow(h2, l2, wh2, wl2, (0, 1, 2), row, 4, 4)
        emit = add_rows(st3, -8, st2, 0, 4, 4, NW) if row == 8 else add_rows(st3l, 0, st2, 0, 4, 4, NW)
        emit(row, jax.nn.gelu(total + bias2))
        if row == 8:
            pack(lambda k, t: st3[3 - k, t, 0:cols, :], putter(out, cols), 4, cols, rem)


def row_of(parts, row):
    for part in parts:
        if row < part.shape[0]:
            return part, row
        row -= part.shape[0]


def k_d(par, st2, north, st3l, st3m, sign, wh, wl, bias, st3b, out, ewi, ewc, x2, hi, lo, *, cols, rem):
    wide = cols + 8
    north_rows(x2, 0, north, lanes_of(sign, 0), 4, wide, 0, rem)
    sources = run(st2, 8, 8, (0, 4, 8)) + run(x2, 0, 4, (0, 4, 8))
    for i in range(0, 12, 2):
        fill_pair(hi, lo, i, sources, i)
    total = narrow(hi, lo, wh, wl, (0, 1, 2), 0, 4, 4)
    add_rows(st3b, 0, st2, 12, 4, 4, NW)(0, jax.nn.gelu(total + bias_of(bias, 2)))
    pack(lambda k, t: st3b[3 - k, t, 0:cols, :], putter(out, cols), 4, cols, rem)
    even = par[0] == 0
    parts = (st3l, st3m, st3b)
    rows = sum(x.shape[0] for x in parts)

    def edge(flip):
        def get(k, t):
            ref, row = row_of(parts, k)
            west, east = ref[row, t, 0:HALO, :], ref[row, t, cols - HALO : cols, :]
            return jnp.where(even != flip, east, west)

        return get

    pack(edge(False), putter(ewi, HALO), rows, HALO, rem)
    pack(edge(True), putter(ewc, HALO), rows, HALO, rem)


def put_out(out, first, src, cols, channels):
    for col in range(cols):
        out[col, first : first + 8, 0:LANES] = get_column(src, 0, col, 0)
        out[col, first : first + 8, LANES:channels] = get_column(src, 0, col, 1)[:, 0 : channels - LANES]


def k_f(st3l, st3m, st3b, se, wh, wl, bias, acc, top, x3, hi, lo, *, cols):
    low, south = acc.shape[0], se.shape[0]
    rows = low + top.shape[0]
    zero = jnp.zeros((2, HALO, LANES), F32)
    for k in range(rows + south):
        ref, row = (se, k) if k < south else row_of((st3l, st3m, st3b), k - south)
        x3[k, :, 0:HALO, :] = zero
        at = HALO if k < south else 0
        x3[k, :, HALO : HALO + cols, :] = ref[row, :, at : at + cols, :]
        x3[k, :, HALO + cols : 2 * HALO + cols, :] = zero
    bias = bias_of(bias, 3)
    filled = 0
    for row in range(0, rows, 4):
        taps = (0, 1, 2) if row < low else (0, 1)
        while filled < row + 4 + 8 * taps[-1]:
            fill_pair(hi, lo, filled, run(x3, filled, 2, (0, 8, 16)), 0)
            filled += 2
        total = narrow(hi, lo, wh, wl, taps, row, 4, 8)
        ref, at = (acc, row) if row < low else (top, row - low)
        ref[at : at + 4] = (total + bias).reshape(4, NW, 2 * LANES)


def split_bf16(x):
    h = x.astype(BF16)
    return h, (x - h.astype(F32)).astype(BF16)


def edge_sums(tiles_of, wh, wl, taps):
    total = None
    for a in taps:
        h, l = split_bf16(tiles_of(a))
        for left, right in ((h, wh), (l, wh), (h, wl)):
            term = jnp.dot(left, right(a), preferred_element_type=F32)
            total = term if total is None else total + term
    return total


def side_weights(ref, b):
    at = b * 2 * LANES
    return lambda a: ref[a, at : at + 2 * LANES, :]


def k_g(par, acc1, acc, st3l, st3m, st3b, se, ewi, ewc, na, nb, sign, wh, wl, out, accn, xn, halo, end, hi, lo, *, cols, rem):
    rows = accn.shape[0]
    channels = out.shape[-1]
    south = se.shape[0]
    sign = lanes_of(sign, 0)
    zero = jnp.zeros((8, 2, HALO, LANES), F32)
    xn[:, :, 0:HALO, :] = zero
    xn[:, :, HALO + cols : 2 * HALO + cols, :] = zero
    north_rows(xn, 0, nb, sign, 4, cols, HALO, rem)
    north_rows(xn, 4, na, sign, 4, cols, HALO, rem)
    for i in range(0, 8, 2):
        fill_pair(hi, lo, i, run(xn, i, 2, (0, 8, 16)), 0)
    accn[0 : rows - 8] = acc1[...]
    for i in range(0, 8, 4):
        at = slice(i * NW, (i + 4) * NW)
        total = acc[i : i + 4].reshape(4 * NW, 2 * LANES)
        for left, right in ((hi[at], wh), (lo[at], wh), (hi[at], wl)):
            total = total + jnp.dot(left, right[2], preferred_element_type=F32)
        accn[rows - 8 + i : rows - 4 + i] = total.reshape(4, NW, 2 * LANES)
    for side, slot in enumerate(sided(par, ewi, ewc, rows, HALO, rem)):
        b, to = ((0, 0), (2, cols - HALO))[side]
        at = side * (HALO + cols)
        for k in range(south):
            for t in range(2):
                halo[side, k * HALO : (k + 1) * HALO, t * LANES : (t + 1) * LANES] = se[k, t, at : at + HALO, :]
        for k in range(rows):
            tiles = unpack(slot, k, rows, HALO, rem)
            for t in range(2):
                halo[side, (south + k) * HALO : (south + k + 1) * HALO, t * LANES : (t + 1) * LANES] = tiles[t]
        halo[side, (south + rows) * HALO :, :] = jnp.zeros((8 * HALO, 2 * LANES), F32)
        total = edge_sums(
            lambda a: halo[side, 8 * a * HALO : (8 * a + rows) * HALO, :],
            side_weights(wh, b), side_weights(wl, b), (0, 1, 2),
        )
        for k in range(rows):
            accn[k, to : to + HALO, :] += total[k * HALO : (k + 1) * HALO]
    for half in range(0, rows, 8):
        for k in range(8):
            grown = jax.nn.gelu(accn[half + k])
            ref, row = row_of((st3l, st3m, st3b), half + k)
            for t in range(2):
                end[half // 8, k, t] = ref[row, t] + grown[:, t * LANES : (t + 1) * LANES]
        put_out(out, half, end.at[half // 8], cols, channels)


def k_h(before, accn, st3m, st3b, nc, sign, wh, wl, out, xc, end, done, sems, *, cols, rem):
    rows = accn.shape[0]
    channels = out.shape[-1]
    slot = turned(slots_of(nc, 8, 2 * HALO, rem)).__getitem__
    for k in range(8):
        tiles = signed(unpack(slot, k, 8, 2 * HALO, rem), lanes_of(sign, 0))
        for t in range(2):
            for side in range(2):
                xc[side, k * HALO : (k + 1) * HALO, t * LANES : (t + 1) * LANES] = tiles[t][side * HALO : (side + 1) * HALO]
    copies = []
    for side in range(2):
        b, at = ((0, 0), (2, cols - HALO))[side]
        total = edge_sums(lambda a: xc[side], side_weights(wh, b), side_weights(wl, b), (2,))
        for k in range(8):
            ref, row = row_of((st3m, st3b), k)
            grown = jax.nn.gelu(accn[rows - 8 + k, at : at + HALO, :] + total[k * HALO : (k + 1) * HALO])
            for t in range(2):
                end[k, t] = ref[row, t, at : at + HALO, :] + grown[:, t * LANES : (t + 1) * LANES]
        put_out(done.at[side], 0, end, HALO, channels)
        copies.append(
            pltpu.make_async_copy(done.at[side], out.at[pl.ds(at, HALO), pl.ds(rows - 8, 8), :], sems.at[side])
        )
        copies[-1].start()
    for copy in copies:
        copy.wait()


VM = pl.BlockSpec(memory_space=pltpu.VMEM)
SM = pl.BlockSpec(memory_space=pltpu.SMEM)
HB = pl.BlockSpec(memory_space=pltpu.HBM)


def lhs(rows):
    return [pltpu.VMEM((rows, MW, 6 * LANES), BF16)] * 2


def flat(rows):
    return [pltpu.VMEM((rows * NW, 6 * LANES), BF16)] * 2


def call(kernel, outs, scratch, args, smem=0, flops=0, limit=16, hbm=(), alias=None):
    args = [pltpu.with_memory_space_constraint(a, pltpu.HBM) if i in hbm else a for i, a in enumerate(args)]
    moved = sum(a.size * a.dtype.itemsize for a in args[smem:])
    outs = [o if isinstance(o, jax.ShapeDtypeStruct) else jax.ShapeDtypeStruct(o, F32) for o in outs]
    return pl.pallas_call(
        kernel,
        out_shape=outs,
        in_specs=[SM if i < smem else HB if i in hbm else VM for i in range(len(args))],
        out_specs=[HB if alias else VM] * len(outs),
        input_output_aliases=alias or {},
        scratch_shapes=scratch,
        compiler_params=pltpu.CompilerParams(vmem_limit_bytes=limit * 2**20),
        cost_estimate=pl.CostEstimate(flops=flops, bytes_accessed=moved, transcendentals=0),
    )(*args)


def layers_of(field, south_rows, sign_mask, weights, biases):
    rows, cols, channels = field.shape
    south = south_rows.shape[0]
    layers = weights.shape[0]
    rem = channels - LANES - HALF
    devices = lax.axis_size("lon")
    mirror = [(i, devices - 1 - i) for i in range(devices)]
    intra = [(i, i ^ 1) for i in range(devices)]
    cross = [(i, (i + 1) % devices if i % 2 else (i - 1) % devices) for i in range(devices)]
    send = lambda x, route: lax.ppermute(x, "lon", route)
    par = (lax.axis_index("lon") % 2).astype(jnp.int32).reshape(1)
    sign = sign_mask.reshape(1, channels)
    field = jnp.swapaxes(field, 0, 1)
    south_rows = jnp.swapaxes(south_rows, 0, 1)
    row_flops = MW * 6 * LANES * 2 * LANES * 2 * 9
    tall = rows + south

    def state(n, width):
        return (n, 2, width, LANES)

    ew_rows = packed_rows(HALO, tall, rem)
    main, ewi, ewc = call(
        k_first,
        [(packed_rows(3, cols, rem), LANES), (ew_rows, LANES), (ew_rows, LANES)],
        [pltpu.VMEM(state(8, 56), F32), pltpu.VMEM((2, HALO, rows, channels), F32),
         pltpu.VMEM((2, HALO, south, channels), F32), pltpu.VMEM((cols, 8, channels), F32),
         pltpu.SemaphoreType.DMA((5,))],
        [par, field, south_rows], smem=1, hbm=(1, 2), limit=16,
    )
    ewi, ewc, main = send(ewi, intra), send(ewc, cross), send(main, mirror)
    split = call(
        k_weights,
        [jax.ShapeDtypeStruct((3, 6 * LANES, 2 * LANES), BF16)] * (2 * layers),
        [pltpu.VMEM(weights.shape, F32), pltpu.SemaphoreType.DMA((layers,))],
        [weights], limit=24, hbm=(0,),
    )
    (corner,) = call(
        functools.partial(k_corner, tall=tall, rows=rows, rem=rem),
        [(packed_rows(3, 2 * HALO, rem), LANES)], [pltpu.VMEM(state(8, 2 * HALO), F32)],
        [par, ewi, ewc], smem=1,
    )
    corner = send(corner, mirror)
    st1, se, x0 = call(
        k_a,
        [state(rows - 6, 72), state(south, 80), state(rows, 72)],
        lhs(rows - 4),
        [par, field, south_rows, ewi, ewc, *split[0:2], biases],
        smem=1, flops=10 * row_flops,
    )
    st2b, north, low = call(
        functools.partial(k_b, cols=cols, rem=rem),
        [state(4, 72), (packed_rows(4, cols + 8, rem), LANES), state(5, 72)],
        [pltpu.VMEM(state(3, 72), F32), pltpu.VMEM(state(4, 72), F32), pltpu.VMEM(state(8, 72), F32)] + lhs(7) + lhs(7) + lhs(8),
        [x0, se, main, corner, st1, sign, *split[0:4], biases],
        flops=12 * row_flops,
    )
    north = send(north, mirror)
    st2m, st3m, st3l, na = call(
        functools.partial(k_c1, cols=cols, rem=rem),
        [state(rows, 72), state(4, NW), state(8, NW), (packed_rows(4, cols, rem), LANES)],
        [pltpu.VMEM(state(rows - 1, 72), F32)] + lhs(8) + lhs(12) + flat(rows + 4),
        [low, st1, st2b, se, *split[2:6], biases],
        flops=24 * row_flops,
    )
    na = send(na, mirror)
    ew_rows = packed_rows(rows, HALO, rem)
    st3b, nb, ewi, ewc = call(
        functools.partial(k_d, cols=cols, rem=rem),
        [state(4, NW), (packed_rows(4, cols, rem), LANES), (ew_rows, LANES), (ew_rows, LANES)],
        [pltpu.VMEM(state(4, 72), F32)] + flat(12),
        [par, st2m, north, st3l, st3m, sign, *split[4:6], biases],
        smem=1, flops=4 * row_flops,
    )
    ewi, ewc = send(ewi, intra), send(ewc, cross)
    nb = send(nb, mirror)
    acc, acc2 = call(
        functools.partial(k_f, cols=cols),
        [(rows - 8, NW, 2 * LANES), (8, NW, 2 * LANES)],
        [pltpu.VMEM(state(rows + south, 80), F32)] + flat(rows + south),
        [st3l, st3m, st3b, se, *split[6:8], biases],
        flops=(rows - 3) * row_flops,
    )
    ewi, ewc, acc, acc2 = lax.optimization_barrier((ewi, ewc, acc, acc2))
    (nc,) = call(
        functools.partial(k_corner2, rows=rows, rem=rem),
        [(packed_rows(8, 2 * HALO, rem), LANES)], [], [par, ewi, ewc], smem=1,
    )
    nc = send(nc, mirror)
    out, acc = call(
        functools.partial(k_g, cols=cols, rem=rem),
        [(cols, rows, channels), (rows, NW, 2 * LANES)],
        [pltpu.VMEM(state(8, 80), F32), pltpu.VMEM((2, (rows + south + 8) * HALO, 2 * LANES), F32),
         pltpu.VMEM((2,) + state(8, NW), F32)] + flat(8),
        [par, acc, acc2, st3l, st3m, st3b, se, ewi, ewc, na, nb, sign, *split[6:8]],
        smem=1, flops=4 * row_flops,
    )
    (out,) = call(
        functools.partial(k_h, cols=cols, rem=rem),
        [(cols, rows, channels)],
        [pltpu.VMEM((2, 8 * HALO, 2 * LANES), F32), pltpu.VMEM(state(8, HALO), F32),
         pltpu.VMEM((2, HALO, 8, channels), F32), pltpu.SemaphoreType.DMA((2,))],
        [out, acc, st3m, st3b, nc, sign, *split[6:8]],
        hbm=(0,), alias={0: 0}, flops=row_flops,
    )
    return jnp.swapaxes(out, 0, 1)


def solution(mesh):
    in_specs = (P(None, "lon", None), P(None, "lon", None), P(), P(), P())
    out_specs = P(None, "lon", None)
    return jax.shard_map(layers_of, mesh=mesh, in_specs=in_specs, out_specs=out_specs, check_vma=False)
```

```python
import functools

import jax
import jax.numpy as jnp
from jax import lax
from jax.experimental import pallas as pl
from jax.experimental.pallas import tpu as pltpu
from jax.sharding import PartitionSpec as P

F32 = jnp.float32
BF16 = jnp.bfloat16
LANES = 128
HALF = 64
MW = 64
NW = 56
HALO = 8


def merged(rows):
    return rows % 2 == 1 and rows <= 8


def rest_groups(rows, width, rem):
    groups = max(1, LANES // (rows * rem))
    return groups, width if groups == 1 else (-(-width // groups) + 7) // 8 * 8


def packed_rows(rows, width, rem):
    full = rows + (rows + 1) // 2
    return full * width + (0 if merged(rows) else rest_groups(rows, width, rem)[1])


def lane_of(width):
    return lax.broadcasted_iota(jnp.int32, (width, LANES), 1)


def roll(x, shift):
    shift = shift % LANES
    return x if shift == 0 else pltpu.roll(x, shift, 1)


def pack(get, put, rows, width, rem):
    lane = lane_of(width)
    halves = (rows + 1) // 2
    for k in range(rows):
        put(k, get(k, 0))
    second = [get(k, 1) for k in range(rows)]
    for p in range(halves):
        other = roll(second[2 * p + 1], HALF) if 2 * p + 1 < rows else jnp.zeros((width, LANES), F32)
        tile = jnp.where(lane < HALF, second[2 * p], other)
        if merged(rows) and p == halves - 1:
            for k in range(rows):
                at = HALF + rem * k
                tile = jnp.where((lane >= at) & (lane < at + rem), roll(second[k], rem * k), tile)
        put(rows + p, tile)
    if not merged(rows):
        tile = jnp.zeros((width, LANES), F32)
        for k in range(rows):
            tile = jnp.where((lane >= rem * k) & (lane < rem * k + rem), roll(second[k], rem * k - HALF), tile)
        groups, high = rest_groups(rows, width, rem)
        total = None
        for g in range(groups):
            part = tile[g * high : min(width, (g + 1) * high)]
            if part.shape[0] < high:
                part = jnp.concatenate([part, jnp.zeros((high - part.shape[0], LANES), F32)], axis=0)
            part = roll(part, g * rows * rem)
            total = part if total is None else total + part
        put(rows + halves, total)


def unpack(slot, k, rows, width, rem):
    lane = lane_of(width)
    halves = (rows + 1) // 2
    half = roll(slot(rows + k // 2), HALF * (k % 2))
    if merged(rows):
        rest = roll(slot(rows + halves - 1), -rem * k)
    else:
        rest = roll(slot(rows + halves), HALF - rem * k)
    tile = jnp.where(lane < HALF, half, jnp.where(lane < HALF + rem, rest, 0.0))
    return slot(k), tile


def slots_of(ref, rows, width, rem):
    full = rows + (rows + 1) // 2
    tiles = [ref[k * width : (k + 1) * width, :] for k in range(full)]
    if not merged(rows):
        groups, high = rest_groups(rows, width, rem)
        block = ref[full * width : full * width + high, :]
        parts = [roll(block, -g * rows * rem)[: min(high, width - g * high)] for g in range(groups)]
        tiles.append(parts[0] if groups == 1 else jnp.concatenate(parts, axis=0))
    return tiles


def putter(ref, width):
    def put(k, tile):
        ref[k * width : (k + 1) * width, :] = tile

    return put


def turned(tiles):
    order = 7 - lax.broadcasted_iota(jnp.int32, (8, LANES), 0)
    flip = lambda x: jnp.take_along_axis(x, order, axis=0)

    def one(x):
        parts, left = [], x.shape[0]
        while left >= 8:
            parts.append(flip(x[left - 8 : left]))
            left -= 8
        if left:
            parts.append(flip(x[0:8])[8 - left :])
        return jnp.concatenate(parts, axis=0)

    return [one(x) for x in tiles]


def fill_row(hi, lo, dst, ref, row, offs):
    for b in range(3):
        for t in range(2):
            x = ref[row, t, offs[b] : offs[b] + MW, :]
            h = x.astype(BF16)
            at = b * 2 * LANES + t * LANES
            hi[dst, :, at : at + LANES] = h
            lo[dst, :, at : at + LANES] = (x - h.astype(F32)).astype(BF16)


def fill_pair(hi, lo, dst, sources, at):
    place = slice(dst * NW, (dst + 2) * NW)
    for b in range(3):
        for t in range(2):
            x = jnp.concatenate(
                [ref[row, t, offs[b] : offs[b] + NW, :] for ref, row, offs in sources[at : at + 2]], axis=0
            )
            h = x.astype(BF16)
            to = b * 2 * LANES + t * LANES
            hi[place, to : to + LANES] = h
            lo[place, to : to + LANES] = (x - h.astype(F32)).astype(BF16)


def narrow(hi, lo, wh, wl, taps, row, chunk, dilate):
    total = None
    for a in taps:
        at = slice((row + a * dilate) * NW, (row + a * dilate + chunk) * NW)
        lh, ll = hi[at], lo[at]
        for left, right in ((lh, wh), (ll, wh), (lh, wl)):
            term = jnp.dot(left, right[a], preferred_element_type=F32)
            total = term if total is None else total + term
    return total


def fill(hi, lo, dst, ref, src, count, offs):
    for i in range(count):
        fill_row(hi, lo, dst + i, ref, src + i, offs)


def run(ref, first, count, offs):
    return [(ref, first + i, offs) for i in range(count)]


def products(hi, lo, wh, wl, taps, row, chunk, dilate):
    total = None
    for a in taps:
        at = slice(row + a * dilate, row + a * dilate + chunk)
        lh = hi[at].reshape(chunk * MW, hi.shape[-1])
        ll = lo[at].reshape(chunk * MW, hi.shape[-1])
        for left, right in ((lh, wh), (ll, wh), (lh, wl)):
            term = jnp.dot(left, right[a], preferred_element_type=F32)
            total = term if total is None else total + term
    return total


def conv(buffers, wh, wl, bias, dilate, sources, count, chunk, emit):
    hi, lo = buffers
    filled = 0
    for row in range(0, count, chunk):
        while filled < row + chunk + 2 * dilate:
            fill_row(hi, lo, filled, *sources[filled])
            filled += 1
        total = products(hi, lo, wh, wl, (0, 1, 2), row, chunk, dilate)
        emit(row, jax.nn.gelu(total + bias))


def add_rows(out, out_row, res, res_row, off, chunk, width=MW):
    def emit(row, grown):
        for q in range(chunk):
            for t in range(2):
                out[out_row + row + q, t, 0:width, :] = (
                    res[res_row + row + q, t, off : off + width, :]
                    + grown[q * width : (q + 1) * width, t * LANES : (t + 1) * LANES]
                )

    return emit


def put_row(dst, row, at, tiles):
    for t in range(2):
        dst[row, t, at : at + tiles[t].shape[0], :] = tiles[t]


def widen(x):
    return jnp.concatenate([x, jnp.zeros(x.shape[:-1] + (LANES - x.shape[-1],), F32)], axis=-1)


def tile_at(ref, col, lo, hi, t):
    return ref[col, lo:hi, 0:LANES] if t == 0 else widen(ref[col, lo:hi, LANES : ref.shape[-1]])


def strided(dst, first, t, col):
    rows, _, width, _ = dst.shape
    return dst.reshape(rows * 2 * width, LANES), pl.ds((2 * first + t) * width + col, 8, stride=2 * width)


def put_column(dst, first, col, t, tile):
    flat, at = strided(dst, first, t, col)
    flat[at, :] = tile


def get_column(src, first, col, t):
    flat, at = strided(src, first, t, col)
    return flat[at, :]


def lanes_of(ref, row):
    x = ref[row : row + 1, :].astype(F32)
    return [x[:, 0:LANES], widen(x[:, LANES:])]


def bias_of(ref, row):
    return jnp.concatenate(lanes_of(ref, row), axis=1)


def k_first(par, field, south, main, ewi, ewc, top, fedge, sedge, last, sems):
    cols, rows, channels = field.shape
    rem = channels - LANES - HALF
    even = par[0] == 0
    sides = (pl.ds(0, HALO), pl.ds(cols - HALO, HALO))
    copies = [pltpu.make_async_copy(field.at[at], fedge.at[i], sems.at[i]) for i, at in enumerate(sides)]
    copies += [pltpu.make_async_copy(south.at[at], sedge.at[i], sems.at[2 + i]) for i, at in enumerate(sides)]
    copies += [pltpu.make_async_copy(field.at[:, pl.ds(rows - 8, 8), :], last, sems.at[4])]
    for copy in copies:
        copy.start()
    for copy in copies[:4]:
        copy.wait()

    def edge(flip):
        def get(k, t):
            pick = []
            for i in range(2):
                tiles = [tile_at(fedge.at[i], k, 0, rows, t), tile_at(sedge.at[i], k, 0, south.shape[1], t)]
                pick.append(jnp.concatenate(tiles, axis=0))
            return jnp.where(even != flip, pick[1], pick[0])

        return get

    tall = rows + south.shape[1]
    pack(edge(False), putter(ewi, tall), HALO, tall, rem)
    pack(edge(True), putter(ewc, tall), HALO, tall, rem)
    copies[4].wait()
    for col in range(cols):
        for t in range(2):
            put_column(top, 0, col, t, tile_at(last, col, 0, 8, t))
    pack(lambda k, t: top[7 - k, t, 0:cols, :], putter(main, cols), 3, cols, rem)


def k_weights(w, *refs):
    layers, _, channels, _ = w.shape
    outs, (buf, sems) = refs[: 2 * layers], refs[2 * layers :]
    copies = [pltpu.make_async_copy(w.at[i], buf.at[i], sems.at[i]) for i in range(layers)]
    for copy in copies:
        copy.start()
    for i in range(layers):
        wh, wl = outs[2 * i : 2 * i + 2]
        copies[i].wait()
        for k in range(9):
            x = buf[i, k]
            h = x.astype(BF16)
            at = (k % 3) * 2 * LANES
            for ref, value in ((wh, h), (wl, (x - h.astype(F32)).astype(BF16))):
                wide = jnp.concatenate([value, jnp.zeros((channels, 2 * LANES - channels), BF16)], axis=1)
                ref[k // 3, at : at + channels, :] = wide
                ref[k // 3, at + channels : at + 2 * LANES, :] = jnp.zeros((2 * LANES - channels, 2 * LANES), BF16)


def sided(par, ewi, ewc, rows, width, rem):
    even = par[0] == 0
    i, c = slots_of(ewi, rows, width, rem), slots_of(ewc, rows, width, rem)
    west = [jnp.where(even, y, x) for x, y in zip(i, c)]
    east = [jnp.where(even, x, y) for x, y in zip(i, c)]
    return west.__getitem__, east.__getitem__


def k_corner(par, ewi, ewc, out, top, *, tall, rows, rem):
    west, east = sided(par, ewi, ewc, HALO, tall, rem)
    for side, slot in enumerate((west, east)):
        for k in range(HALO):
            tiles = unpack(slot, k, HALO, tall, rem)
            for t in range(2):
                put_column(top, 0, side * HALO + k, t, tiles[t][rows - 8 : rows])
    pack(lambda k, t: top[7 - k, t], putter(out, 2 * HALO), 3, 2 * HALO, rem)


def k_corner2(par, ewi, ewc, out, *, rows, rem):
    west, east = sided(par, ewi, ewc, rows, HALO, rem)
    tiles = []
    for k in range(8):
        w = unpack(west, rows - 1 - k, rows, HALO, rem)
        e = unpack(east, rows - 1 - k, rows, HALO, rem)
        tiles.append([jnp.concatenate([w[t], e[t]], axis=0) for t in range(2)])
    pack(lambda k, t: tiles[k][t], putter(out, 2 * HALO), 8, 2 * HALO, rem)


def k_a(par, field, south, ewi, ewc, wh, wl, bias, st1, se, x0, *buffers):
    cols, rows, channels = field.shape
    rem = channels - LANES - HALF
    deep = south.shape[1]
    west, east = sided(par, ewi, ewc, HALO, rows + deep, rem)

    def put(col, tiles):
        for t in range(2):
            for h in range(0, rows, 8):
                put_column(x0, h, col, t, tiles[t][h : h + 8])
            put_column(se, 0, col, t, tiles[t][rows : rows + 8])

    for k in range(HALO):
        put(k, unpack(west, k, HALO, rows + deep, rem))
        put(HALO + cols + k, unpack(east, k, HALO, rows + deep, rem))
    for col in range(cols):
        for t in range(2):
            for h in range(0, rows, 8):
                put_column(x0, h, HALO + col, t, tile_at(field, col, h, h + 8, t))
            put_column(se, 0, HALO + col, t, tile_at(south, col, 0, 8, t))
    count = st1.shape[0]
    first = rows - 1 - count
    sources = run(x0, first - 1, count + 2, (1, 2, 3))
    conv(buffers, wh, wl, bias_of(bias, 0), 1, sources, count, 5, add_rows(st1, 0, x0, first, 2, 5))


def signed(tiles, sign):
    return tiles if sign is None else [tiles[t] * sign[t] for t in range(2)]


def north_rows(dst, dst_row, main, sign, count, width, left, rem):
    slot = turned(slots_of(main, count, width, rem)).__getitem__
    for k in range(count):
        put_row(dst, dst_row + k, left, signed(unpack(slot, k, count, width, rem), sign))


def north_corners(dst, dst_row, corner, sign, count, cols, left, rem):
    width = 2 * HALO
    slot = turned(slots_of(corner, count, width, rem)).__getitem__
    for k in range(count):
        t = signed(unpack(slot, k, count, width, rem), sign)
        put_row(dst, dst_row + k, left - HALO, [x[0:HALO] for x in t])
        put_row(dst, dst_row + k, left + cols, [x[HALO:] for x in t])


def k_b(edge, se, main, corner, st1, sign, wh0, wl0, wh1, wl1, bias, st2, out, low, x0, xr, x1, hi, lo, h1, l1, *buffers, cols, rem):
    rows = edge.shape[0]
    sign = lanes_of(sign, 0)
    north_rows(xr, 1, main, None, 3, cols, HALO, rem)
    north_corners(xr, 1, corner, None, 3, cols, HALO, rem)
    x0[0:2] = edge[rows - 2 :]
    for t in range(2):
        x0[2, t] = xr[1, t] * sign[t]
        xr[0, t] = edge[rows - 1, t] * sign[t]
    x1[0:5] = st1[st1.shape[0] - 5 :]
    offs = (1, 2, 3)
    fill(hi, lo, 0, x0, 0, 3, offs)
    fill(hi, lo, 3, xr, 0, 4, offs[::-1])
    total = None
    for a in range(3):
        both = [jnp.concatenate([x[a : a + 1], x[5 - a : 7 - a]]).reshape(3 * MW, x.shape[-1]) for x in (hi, lo)]
        for left, right in ((both[0], wh0), (both[1], wh0), (both[0], wl0)):
            term = jnp.dot(left, right[a], preferred_element_type=F32)
            total = term if total is None else total + term
    grown = jax.nn.gelu(total + bias_of(bias, 0))
    for q in range(3):
        for t in range(2):
            g = grown[q * MW : (q + 1) * MW, t * LANES : (t + 1) * LANES]
            if q == 0:
                x1[5, t, 0:MW, :] = x0[1, t, 2 : 2 + MW, :] + g
            else:
                x1[5 + q, t, 0:MW, :] = sign[t] * (xr[q, t, 2 : 2 + MW, :] + g)
    count = low.shape[0]
    sources = run(se, se.shape[0] - 1, 1, offs) + run(edge, 0, count + 1, offs)
    conv((h1, l1), wh0, wl0, bias_of(bias, 0), 1, sources, count, count, add_rows(low, 0, edge, 0, 2, count))
    conv(buffers, wh1, wl1, bias_of(bias, 1), 2, run(x1, 0, 8, (0, 2, 4)), 4, 4, add_rows(st2, 0, x1, 2, 2, 4))
    wide = cols + 8
    pack(lambda k, t: st2[3 - k, t, 0:wide, :], putter(out, wide), 4, wide, rem)


def k_c1(low, st1a, st2b, se, wh1, wl1, wh2, wl2, bias, st2, st3, st3l, out, st1, h0, l0, h1, l1, h2, l2, *, cols, rem):
    south = se.shape[0]
    done = low.shape[0]
    st1[0:done] = low[...]
    st1[done:] = st1a[...]
    bias1 = bias_of(bias, 1)
    conv((h1, l1), wh1, wl1, bias1, 2, run(st1, 2, 12, (0, 2, 4)), 8, 4, add_rows(st2, 4, st1, 4, 2, 4))
    sources = run(se, south - 2, 2, (2, 4, 6)) + run(st1, 0, 6, (0, 2, 4))
    conv((h0, l0), wh1, wl1, bias1, 2, sources, 4, 4, add_rows(st2, 0, st1, 0, 2, 4))
    st2[12:16] = st2b[...]
    bias2 = bias_of(bias, 2)
    sources = run(se, south - 4, 4, (4, 8, 12)) + run(st2, 0, 16, (0, 4, 8))
    for i in range(8, 20, 2):
        fill_pair(h2, l2, i, sources, i)
    for row in (8, 0, 4):
        for i in range(0, 8 if row == 0 else 0, 2):
            fill_pair(h2, l2, i, sources, i)
        total = narrow(h2, l2, wh2, wl2, (0, 1, 2), row, 4, 4)
        emit = add_rows(st3, -8, st2, 0, 4, 4, NW) if row == 8 else add_rows(st3l, 0, st2, 0, 4, 4, NW)
        emit(row, jax.nn.gelu(total + bias2))
        if row == 8:
            pack(lambda k, t: st3[3 - k, t, 0:cols, :], putter(out, cols), 4, cols, rem)


def row_of(parts, row):
    for part in parts:
        if row < part.shape[0]:
            return part, row
        row -= part.shape[0]


def k_d(par, st2, north, st3l, st3m, sign, wh, wl, bias, st3b, out, ewi, ewc, x2, hi, lo, *, cols, rem):
    wide = cols + 8
    north_rows(x2, 0, north, lanes_of(sign, 0), 4, wide, 0, rem)
    sources = run(st2, 8, 8, (0, 4, 8)) + run(x2, 0, 4, (0, 4, 8))
    for i in range(0, 12, 2):
        fill_pair(hi, lo, i, sources, i)
    total = narrow(hi, lo, wh, wl, (0, 1, 2), 0, 4, 4)
    add_rows(st3b, 0, st2, 12, 4, 4, NW)(0, jax.nn.gelu(total + bias_of(bias, 2)))
    pack(lambda k, t: st3b[3 - k, t, 0:cols, :], putter(out, cols), 4, cols, rem)
    even = par[0] == 0
    parts = (st3l, st3m, st3b)
    rows = sum(x.shape[0] for x in parts)

    def edge(flip):
        def get(k, t):
            ref, row = row_of(parts, k)
            west, east = ref[row, t, 0:HALO, :], ref[row, t, cols - HALO : cols, :]
            return jnp.where(even != flip, east, west)

        return get

    pack(edge(False), putter(ewi, HALO), rows, HALO, rem)
    pack(edge(True), putter(ewc, HALO), rows, HALO, rem)


def put_out(out, first, src, cols, channels):
    for col in range(cols):
        out[col, first : first + 8, 0:LANES] = get_column(src, 0, col, 0)
        out[col, first : first + 8, LANES:channels] = get_column(src, 0, col, 1)[:, 0 : channels - LANES]


def k_f(st3l, st3m, st3b, se, wh, wl, bias, acc, top, x3, hi, lo, *, cols):
    low, south = acc.shape[0], se.shape[0]
    rows = low + top.shape[0]
    zero = jnp.zeros((2, HALO, LANES), F32)
    for k in range(rows + south):
        ref, row = (se, k) if k < south else row_of((st3l, st3m, st3b), k - south)
        x3[k, :, 0:HALO, :] = zero
        at = HALO if k < south else 0
        x3[k, :, HALO : HALO + cols, :] = ref[row, :, at : at + cols, :]
        x3[k, :, HALO + cols : 2 * HALO + cols, :] = zero
    bias = bias_of(bias, 3)
    filled = 0
    for row in range(0, rows, 4):
        taps = (0, 1, 2) if row < low else (0, 1)
        while filled < row + 4 + 8 * taps[-1]:
            fill_pair(hi, lo, filled, run(x3, filled, 2, (0, 8, 16)), 0)
            filled += 2
        total = narrow(hi, lo, wh, wl, taps, row, 4, 8)
        ref, at = (acc, row) if row < low else (top, row - low)
        ref[at : at + 4] = (total + bias).reshape(4, NW, 2 * LANES)


def split_bf16(x):
    h = x.astype(BF16)
    return h, (x - h.astype(F32)).astype(BF16)


def edge_sums(tiles_of, wh, wl, taps):
    total = None
    for a in taps:
        h, l = split_bf16(tiles_of(a))
        for left, right in ((h, wh), (l, wh), (h, wl)):
            term = jnp.dot(left, right(a), preferred_element_type=F32)
            total = term if total is None else total + term
    return total


def side_weights(ref, b):
    at = b * 2 * LANES
    return lambda a: ref[a, at : at + 2 * LANES, :]


def k_g(par, acc1, acc, st3l, st3m, st3b, se, ewi, ewc, na, nb, sign, wh, wl, out, accn, xn, halo, end, hi, lo, *, cols, rem):
    rows = accn.shape[0]
    channels = out.shape[-1]
    south = se.shape[0]
    sign = lanes_of(sign, 0)
    zero = jnp.zeros((8, 2, HALO, LANES), F32)
    xn[:, :, 0:HALO, :] = zero
    xn[:, :, HALO + cols : 2 * HALO + cols, :] = zero
    north_rows(xn, 0, nb, sign, 4, cols, HALO, rem)
    north_rows(xn, 4, na, sign, 4, cols, HALO, rem)
    for i in range(0, 8, 2):
        fill_pair(hi, lo, i, run(xn, i, 2, (0, 8, 16)), 0)
    accn[0 : rows - 8] = acc1[...]
    for i in range(0, 8, 4):
        at = slice(i * NW, (i + 4) * NW)
        total = acc[i : i + 4].reshape(4 * NW, 2 * LANES)
        for left, right in ((hi[at], wh), (lo[at], wh), (hi[at], wl)):
            total = total + jnp.dot(left, right[2], preferred_element_type=F32)
        accn[rows - 8 + i : rows - 4 + i] = total.reshape(4, NW, 2 * LANES)
    for side, slot in enumerate(sided(par, ewi, ewc, rows, HALO, rem)):
        b, to = ((0, 0), (2, cols - HALO))[side]
        at = side * (HALO + cols)
        for k in range(south):
            for t in range(2):
                halo[side, k * HALO : (k + 1) * HALO, t * LANES : (t + 1) * LANES] = se[k, t, at : at + HALO, :]
        for k in range(rows):
            tiles = unpack(slot, k, rows, HALO, rem)
            for t in range(2):
                halo[side, (south + k) * HALO : (south + k + 1) * HALO, t * LANES : (t + 1) * LANES] = tiles[t]
        halo[side, (south + rows) * HALO :, :] = jnp.zeros((8 * HALO, 2 * LANES), F32)
        total = edge_sums(
            lambda a: halo[side, 8 * a * HALO : (8 * a + rows) * HALO, :],
            side_weights(wh, b), side_weights(wl, b), (0, 1, 2),
        )
        for k in range(rows):
            accn[k, to : to + HALO, :] += total[k * HALO : (k + 1) * HALO]
    for half in range(0, rows, 8):
        for k in range(8):
            grown = jax.nn.gelu(accn[half + k])
            ref, row = row_of((st3l, st3m, st3b), half + k)
            for t in range(2):
                end[half // 8, k, t] = ref[row, t] + grown[:, t * LANES : (t + 1) * LANES]
        put_out(out, half, end.at[half // 8], cols, channels)


def k_h(before, accn, st3m, st3b, nc, sign, wh, wl, out, xc, end, done, sems, *, cols, rem):
    rows = accn.shape[0]
    channels = out.shape[-1]
    slot = turned(slots_of(nc, 8, 2 * HALO, rem)).__getitem__
    sign = lanes_of(sign, 0)
    for k in range(8):
        tiles = signed(unpack(slot, k, 8, 2 * HALO, rem), sign)
        for t in range(2):
            for side in range(2):
                xc[side, k * HALO : (k + 1) * HALO, t * LANES : (t + 1) * LANES] = tiles[t][side * HALO : (side + 1) * HALO]
    copies = []
    for side in range(2):
        b, at = ((0, 0), (2, cols - HALO))[side]
        total = edge_sums(lambda a: xc[side], side_weights(wh, b), side_weights(wl, b), (2,))
        for k in range(8):
            ref, row = row_of((st3m, st3b), k)
            grown = jax.nn.gelu(accn[rows - 8 + k, at : at + HALO, :] + total[k * HALO : (k + 1) * HALO])
            for t in range(2):
                end[k, t] = ref[row, t, at : at + HALO, :] + grown[:, t * LANES : (t + 1) * LANES]
        put_out(done.at[side], 0, end, HALO, channels)
        copies.append(
            pltpu.make_async_copy(done.at[side], out.at[pl.ds(at, HALO), pl.ds(rows - 8, 8), :], sems.at[side])
        )
        copies[-1].start()
    for copy in copies:
        copy.wait()


VM = pl.BlockSpec(memory_space=pltpu.VMEM)
SM = pl.BlockSpec(memory_space=pltpu.SMEM)
HB = pl.BlockSpec(memory_space=pltpu.HBM)


def lhs(rows):
    return [pltpu.VMEM((rows, MW, 6 * LANES), BF16)] * 2


def flat(rows):
    return [pltpu.VMEM((rows * NW, 6 * LANES), BF16)] * 2


def call(kernel, outs, scratch, args, smem=0, flops=0, limit=16, hbm=(), alias=None):
    args = [pltpu.with_memory_space_constraint(a, pltpu.HBM) if i in hbm else a for i, a in enumerate(args)]
    moved = sum(a.size * a.dtype.itemsize for a in args[smem:])
    outs = [o if isinstance(o, jax.ShapeDtypeStruct) else jax.ShapeDtypeStruct(o, F32) for o in outs]
    return pl.pallas_call(
        kernel,
        out_shape=outs,
        in_specs=[SM if i < smem else HB if i in hbm else VM for i in range(len(args))],
        out_specs=[HB if alias else VM] * len(outs),
        input_output_aliases=alias or {},
        scratch_shapes=scratch,
        compiler_params=pltpu.CompilerParams(vmem_limit_bytes=limit * 2**20),
        cost_estimate=pl.CostEstimate(flops=flops, bytes_accessed=moved, transcendentals=0),
    )(*args)


def layers_of(field, south_rows, sign_mask, weights, biases):
    rows, cols, channels = field.shape
    south = south_rows.shape[0]
    layers = weights.shape[0]
    rem = channels - LANES - HALF
    devices = lax.axis_size("lon")
    mirror = [(i, devices - 1 - i) for i in range(devices)]
    intra = [(i, i ^ 1) for i in range(devices)]
    cross = [(i, (i + 1) % devices if i % 2 else (i - 1) % devices) for i in range(devices)]
    send = lambda x, route: lax.ppermute(x, "lon", route)
    par = (lax.axis_index("lon") % 2).astype(jnp.int32).reshape(1)
    sign = sign_mask.reshape(1, channels)
    field = jnp.swapaxes(field, 0, 1)
    south_rows = jnp.swapaxes(south_rows, 0, 1)
    row_flops = MW * 6 * LANES * 2 * LANES * 2 * 9
    tall = rows + south

    def state(n, width):
        return (n, 2, width, LANES)

    ew_rows = packed_rows(HALO, tall, rem)
    main, ewi, ewc = call(
        k_first,
        [(packed_rows(3, cols, rem), LANES), (ew_rows, LANES), (ew_rows, LANES)],
        [pltpu.VMEM(state(8, 56), F32), pltpu.VMEM((2, HALO, rows, channels), F32),
         pltpu.VMEM((2, HALO, south, channels), F32), pltpu.VMEM((cols, 8, channels), F32),
         pltpu.SemaphoreType.DMA((5,))],
        [par, field, south_rows], smem=1, hbm=(1, 2), limit=16,
    )
    ewc = send(ewc, cross)
    ewi = send(ewi, intra)
    main = send(main, mirror)
    split = call(
        k_weights,
        [jax.ShapeDtypeStruct((3, 6 * LANES, 2 * LANES), BF16)] * (2 * layers),
        [pltpu.VMEM(weights.shape, F32), pltpu.SemaphoreType.DMA((layers,))],
        [weights], limit=24, hbm=(0,),
    )
    (corner,) = call(
        functools.partial(k_corner, tall=tall, rows=rows, rem=rem),
        [(packed_rows(3, 2 * HALO, rem), LANES)], [pltpu.VMEM(state(8, 2 * HALO), F32)],
        [par, ewi, ewc], smem=1,
    )
    corner = send(corner, mirror)
    st1, se, x0 = call(
        k_a,
        [state(rows - 6, 72), state(south, 80), state(rows, 72)],
        lhs(rows - 4),
        [par, field, south_rows, ewi, ewc, *split[0:2], biases],
        smem=1, flops=10 * row_flops,
    )
    st2b, north, low = call(
        functools.partial(k_b, cols=cols, rem=rem),
        [state(4, 72), (packed_rows(4, cols + 8, rem), LANES), state(5, 72)],
        [pltpu.VMEM(state(3, 72), F32), pltpu.VMEM(state(4, 72), F32), pltpu.VMEM(state(8, 72), F32)] + lhs(7) + lhs(7) + lhs(8),
        [x0, se, main, corner, st1, sign, *split[0:4], biases],
        flops=12 * row_flops,
    )
    north = send(north, mirror)
    st2m, st3m, st3l, na = call(
        functools.partial(k_c1, cols=cols, rem=rem),
        [state(rows, 72), state(4, NW), state(8, NW), (packed_rows(4, cols, rem), LANES)],
        [pltpu.VMEM(state(rows - 1, 72), F32)] + lhs(8) + lhs(12) + flat(rows + 4),
        [low, st1, st2b, se, *split[2:6], biases],
        flops=24 * row_flops,
    )
    na = send(na, mirror)
    ew_rows = packed_rows(rows, HALO, rem)
    st3b, nb, ewi, ewc = call(
        functools.partial(k_d, cols=cols, rem=rem),
        [state(4, NW), (packed_rows(4, cols, rem), LANES), (ew_rows, LANES), (ew_rows, LANES)],
        [pltpu.VMEM(state(4, 72), F32)] + flat(12),
        [par, st2m, north, st3l, st3m, sign, *split[4:6], biases],
        smem=1, flops=4 * row_flops,
    )
    ewi, ewc = send(ewi, intra), send(ewc, cross)
    nb = send(nb, mirror)
    acc, acc2 = call(
        functools.partial(k_f, cols=cols),
        [(rows - 8, NW, 2 * LANES), (8, NW, 2 * LANES)],
        [pltpu.VMEM(state(rows + south, 80), F32)] + flat(rows + south),
        [st3l, st3m, st3b, se, *split[6:8], biases],
        flops=(rows - 3) * row_flops,
    )
    ewi, ewc, acc, acc2 = lax.optimization_barrier((ewi, ewc, acc, acc2))
    (nc,) = call(
        functools.partial(k_corner2, rows=rows, rem=rem),
        [(packed_rows(8, 2 * HALO, rem), LANES)], [], [par, ewi, ewc], smem=1,
    )
    nc = send(nc, mirror)
    out, acc = call(
        functools.partial(k_g, cols=cols, rem=rem),
        [(cols, rows, channels), (rows, NW, 2 * LANES)],
        [pltpu.VMEM(state(8, 80), F32), pltpu.VMEM((2, (rows + south + 8) * HALO, 2 * LANES), F32),
         pltpu.VMEM((2,) + state(8, NW), F32)] + flat(8),
        [par, acc, acc2, st3l, st3m, st3b, se, ewi, ewc, na, nb, sign, *split[6:8]],
        smem=1, flops=4 * row_flops,
    )
    (out,) = call(
        functools.partial(k_h, cols=cols, rem=rem),
        [(cols, rows, channels)],
        [pltpu.VMEM((2, 8 * HALO, 2 * LANES), F32), pltpu.VMEM(state(8, HALO), F32),
         pltpu.VMEM((2, HALO, 8, channels), F32), pltpu.SemaphoreType.DMA((2,))],
        [out, acc, st3m, st3b, nc, sign, *split[6:8]],
        hbm=(0,), alias={0: 0}, flops=row_flops,
    )
    return jnp.swapaxes(out, 0, 1)


def solution(mesh):
    in_specs = (P(None, "lon", None), P(None, "lon", None), P(), P(), P())
    out_specs = P(None, "lon", None)
    return jax.shard_map(layers_of, mesh=mesh, in_specs=in_specs, out_specs=out_specs, check_vma=False)
```
